32 devices in a mesh: vis: 8 (over y, x, core), wav: 4 (over z).
Axes of the slice: x: 2, y: 2, z: 4, core: 2. Of those that a mesh axis runs over, the one named last changes fastest.
Arguments:
- image: float32 [4096, 4096], P('vis', 'wav'), may hold values from -6 to 6
- kernel_v: bfloat16 [1024, 64, 256], P(('vis', 'wav')), may hold values from -0.5 to 0.5
- kernel_u: bfloat16 [1024, 64, 256], P(('vis', 'wav')), may hold values from -0.5 to 0.5
- measured: bfloat16 [1024, 2, 256], P(('vis', 'wav')), may hold values from -4 to 4
- dest_owner: int32 [1024, 1], P(('vis', 'wav')), may hold values from 0 to 7; in each aligned block of 32 rows (0 to 31, 32 to 63, ...) at most 8 rows name the same one
- patch_slot: int32 [1024], P(('vis', 'wav')), may hold values from 0 to 127
- thresholds: float32 [4], replicated, may hold values from 0.1 to 1
Outputs:
- restored: float32 [4096, 4096], P('vis', 'wav')
- residual: float32 [1024, 2, 256], P(('vis', 'wav'))
The draws below stay inside these ranges and needn't reach their ends.
Inputs may be any that keep to these rules, and one draw needn't show every extreme that they name: `dest_owner`: the vis index of the owner of the block's uv cells; the 32 blocks of one device name one owner at most 8 times, a bound that some block reaches. `patch_slot`: the block's kernel block among the 128 of its owner's tile in the band of the block's wav index.
All inputs are finite; a program needn't handle non-finite values.
Results may differ from the reference program's by a relative error of at most 0.0017.
Values may be sent and summed in bfloat16 or wider, within the bound.
No kernel may reach another device: no remote copies, remote signals or barrier semaphores. Data moves between devices by JAX's collectives and lax.ppermute only.
A program may use at most 128 MiB of HBM per device.

```python
import math
import jax
import jax.numpy as jnp
import numpy as np
from jax import lax

IMG = 4096
PATCH = 64
VB = 256
B_DEV = 32
ITERS = 1
BLOCKS = 1024
CAP = 8
NBASIS = 4
KV = 512
KU = 1024
PATCH_DEV = 128
N_VIS = 8
N_WAV = 4


def set_ends(values, rng, smallest, top_value):
    longest = values.shape.index(max(values.shape))
    spots = []
    for shift in (0, 1):
        where = [jax.random.randint(jax.random.fold_in(rng, axis), (), 0, length) for axis, length in enumerate(values.shape)]
        where[longest] = (where[longest] + shift) % values.shape[longest]
        spots.append(tuple(where))
    return values.at[spots[0]].set(smallest).at[spots[1]].set(top_value)


def steps_of(stream_key, dims, cuts, low, top_value):
    level = 1.0
    for axis_at, parts in cuts:
        heights = jax.random.uniform(jax.random.fold_in(jax.random.fold_in(stream_key, 6), axis_at), (parts,), jnp.float32, low / len(cuts), top_value / len(cuts))
        level = level * jnp.repeat(jnp.exp(heights), dims[axis_at] // parts).reshape((-1,) + (1,) * (len(dims) - 1 - axis_at))
    return level


def shared_out(own_key, own, number, rows, number_of, top, reach, lean):
    ranking = jax.random.permutation(own_key, number_of)
    heavy_load, usual = shares(number_of, rows * top, reach, lean, True), shares(number_of, rows * top, reach, lean, False)
    places = jnp.arange(number_of)

    def named(sizes, offset_by):
        used = int((sizes > 0).sum())
        fixed = max(1, used // 4)
        passed = fixed + (places - fixed + offset_by * (used - fixed)) % max(1, number_of - fixed)
        return jnp.zeros((number_of,), jnp.int32).at[ranking[jnp.where(places < fixed, places, passed)]].set(jnp.asarray(sizes, jnp.int32))

    sizes = jnp.where(number % 4 == 0, named(heavy_load, number // 4), named(usual, number - number // 4 - 1))
    mixed = jax.random.permutation(jax.random.fold_in(own, 3), number_of)
    source_of, taker = mixed[0:number_of // 2 * 2:2], mixed[1:number_of // 2 * 2:2]
    slack = jnp.minimum(sizes[source_of] - 1, reach - sizes[taker]) // 2
    slack = jnp.where((source_of == ranking[0]) | (taker == ranking[0]) | (sizes[taker] == 0), 0, jnp.maximum(slack, 0))
    passed = jax.random.randint(jax.random.fold_in(own, 4), (number_of // 2,), 0, 1 << 20) % (slack + 1)
    sizes = sizes.at[source_of].add(-passed).at[taker].add(passed)
    members = jnp.searchsorted(jnp.cumsum(sizes), jnp.arange(rows * top), side="right").astype(jnp.int32)
    table = members.reshape(top, rows).T
    table = table[jax.random.permutation(jax.random.fold_in(own, 1), rows)]
    offset_by = jax.random.randint(jax.random.fold_in(own, 2), (rows, 1), 0, top)
    return jnp.take_along_axis(table, (jnp.arange(top)[None, :] + offset_by) % top, axis=1)


def shares(count, total, reach, skew, full):
    weights = [(1 << 20) // math.isqrt(grade ** skew) + 1 for grade in range(1, count + 1)]
    largest = reach if full else min(reach, max(-(-total // count), total * weights[0] // sum(weights)))
    least = 1 if total - largest >= count - 1 else 0
    given, rest = [largest] + [least] * (count - 1), total - largest - least * (count - 1)
    while rest > 0:
        movable = [i for i in range(1, count) if given[i] < largest] or [i for i in range(1, count) if given[i] < reach]
        mass, remaining = sum([weights[i] for i in movable]), rest
        for i in movable:
            more = min(reach - given[i], max(1, remaining * weights[i] // mass), rest)
            given[i] = given[i] + more
            rest = rest - more
    return np.array(given)


def bell_draw(stream_key, shape, scale, most, pieces=(), held_as=jnp.bfloat16):
    values = jax.random.normal(stream_key, shape, jnp.float32) * scale
    if len(pieces) > 0:
        values = steps_of(stream_key, shape, pieces, -0.22, 0.18) * values
    return jnp.clip(values, min=-most, max=most).astype(held_as)


def setup_inputs(seed: int = 0) -> dict:
    arg_keys = jax.random.split(jax.random.key(seed), 8)
    image = bell_draw(arg_keys[0], (IMG, IMG), 1.0, 6.0, ((0, 8), (1, 4)), jnp.float32)
    kernel_v = bell_draw(arg_keys[1], (BLOCKS, PATCH, VB), (2 * PATCH) ** -0.5, 0.5, ((0, 32),))
    kernel_u = bell_draw(arg_keys[2], (BLOCKS, PATCH, VB), (2 * PATCH) ** -0.5, 0.5, ((0, 32),))
    measured = bell_draw(arg_keys[3], (BLOCKS, 2, VB), 0.5, 4.0, ((0, 32),))
    dest_owner_keys = jax.random.split(jax.random.fold_in(arg_keys[4], 1), BLOCKS // B_DEV)
    dest_owner_turns = jax.random.permutation(jax.random.fold_in(arg_keys[4], 3), BLOCKS // B_DEV)
    dest_owner = jax.vmap(lambda own, number: shared_out(jax.random.fold_in(arg_keys[4], 2), own, number, B_DEV, N_VIS, 1, CAP, 2))(dest_owner_keys, dest_owner_turns).reshape((BLOCKS, 1))
    patch_slot = set_ends(jax.random.randint(arg_keys[5], (BLOCKS,), 0, PATCH_DEV), jax.random.fold_in(arg_keys[5], 1), 0, PATCH_DEV - 1).astype(jnp.int32)
    thresholds = jnp.clip(jnp.exp(jax.random.uniform(arg_keys[6], (NBASIS,), jnp.float32, math.log(0.1), math.log(1.0))), 0.1, 1.0)
    return {"image": image, "kernel_v": kernel_v, "kernel_u": kernel_u, "measured": measured, "dest_owner": dest_owner, "patch_slot": patch_slot, "thresholds": thresholds}


def haar_table():
    rows = np.zeros((8, 8))
    root = 1.0 / np.sqrt(8.0)
    rows[0, :] = root
    rows[1, :4] = root
    rows[1, 4:] = -root
    rows[2, 0:2] = 0.5
    rows[2, 2:4] = -0.5
    rows[3, 4:6] = 0.5
    rows[3, 6:8] = -0.5
    for index in range(4):
        rows[4 + index, 2 * index] = np.sqrt(0.5)
        rows[4 + index, 2 * index + 1] = -np.sqrt(0.5)
    return np.kron(np.eye(16), rows)

def basis_prox(field, shift, limit, table):
    height, width = field.shape
    moved = jnp.roll(field, -shift, axis=1).reshape(height, width // 128, 128)
    coeff = jnp.einsum('rgj,kj->rgk', moved, table, precision=lax.Precision.HIGHEST)
    coeff = coeff.reshape(height // 2, 2, width // 128, 128)
    factor = math.sqrt(0.5)
    upper = (coeff[:, 0] + coeff[:, 1]) * factor
    lower = (coeff[:, 0] - coeff[:, 1]) * factor
    upper = upper - jnp.clip(upper, -limit, limit)
    lower = lower - jnp.clip(lower, -limit, limit)
    coeff = jnp.stack([(upper + lower) * factor, (upper - lower) * factor], 1)
    coeff = coeff.reshape(height, width // 128, 128)
    back = jnp.einsum('rgk,kj->rgj', coeff, table, precision=lax.Precision.HIGHEST)
    return jnp.roll(back.reshape(height, width), shift, axis=1)

def corners(target_device, slot_number, device_number):
    wav_index = device_number % N_WAV
    across = KU // PATCH
    start_v = target_device * KV + slot_number // across * PATCH
    start_u = wav_index * KU + slot_number % across * PATCH
    offsets = jnp.arange(PATCH, dtype=jnp.int32)
    row_index = (start_v[:, None] + offsets[None, :])[:, :, None]
    col_index = (start_u[:, None] + offsets[None, :])[:, None, :]
    return (row_index, col_index)

def degrid_reference(v_side_length, u_side_length, grid_patch, measurements):
    product = jnp.einsum('nac,nat->nct', grid_patch.astype(jnp.float32), v_side_length.astype(jnp.float32), precision=lax.Precision.HIGHEST)
    side_f = u_side_length.astype(jnp.float32)
    sky_model_real = lax.optimization_barrier(jnp.sum(product[:, :PATCH] * side_f, 1))
    sky_model_imag = lax.optimization_barrier(jnp.sum(product[:, PATCH:] * side_f, 1))
    return jnp.stack([sky_model_real, sky_model_imag], 1) - measurements.astype(jnp.float32)

def grid_terms_ref(v_side_length, u_side_length, misfit):
    side_f = u_side_length.astype(jnp.float32)
    weighted = jnp.concatenate([misfit[:, 0, None, :] * side_f, misfit[:, 1, None, :] * side_f], 1).astype(jnp.bfloat16)
    return jnp.einsum('nat,nct->nac', v_side_length.astype(jnp.float32), weighted.astype(jnp.float32), precision=lax.Precision.HIGHEST)

def residual_of(estimate, grouped):
    spectrum = jnp.fft.fft2(estimate, norm='ortho').T
    grid_real = jnp.real(spectrum).astype(jnp.bfloat16)
    grid_imag = jnp.imag(spectrum).astype(jnp.bfloat16)

    def per_device(packed_items):
        v_side_length, u_side_length, measurements, target_device, slot_number, device_number = packed_items
        row_index, col_index = corners(target_device, slot_number, device_number)
        grid_patch = jnp.concatenate([grid_real[row_index, col_index], grid_imag[row_index, col_index]], -1)
        return degrid_reference(v_side_length, u_side_length, grid_patch, measurements)
    return lax.map(per_device, grouped)

def gradient_of(misfit, grouped):

    def add_device(carry, packed_items):
        real_acc, imag_acc = carry
        v_side_length, u_side_length, measurements, target_device, slot_number, device_number, residual_values = packed_items
        row_index, col_index = corners(target_device, slot_number, device_number)
        terms = grid_terms_ref(v_side_length, u_side_length, residual_values)
        real_acc = real_acc.at[row_index, col_index].add(terms[..., :PATCH])
        imag_acc = imag_acc.at[row_index, col_index].add(terms[..., PATCH:])
        return ((real_acc, imag_acc), None)
    zeros = jnp.zeros((IMG, IMG), jnp.float32)
    (real_acc, imag_acc), unused = lax.scan(add_device, (zeros, zeros), grouped + (misfit,))
    spectrum = lax.complex(real_acc, imag_acc).T
    return jnp.real(jnp.fft.ifft2(spectrum, norm='ortho'))

def reference(image, kernel_v, kernel_u, measured, dest_owner, patch_slot, thresholds):
    table = jnp.asarray(haar_table(), jnp.float32)
    devices = N_VIS * N_WAV
    grouped = (kernel_v.reshape(devices, B_DEV, PATCH, VB), kernel_u.reshape(devices, B_DEV, PATCH, VB), measured.reshape(devices, B_DEV, 2, VB), dest_owner[:, 0].reshape(devices, B_DEV), patch_slot.reshape(devices, B_DEV), jnp.arange(devices, dtype=jnp.int32))
    estimate = image
    misfit = None
    for turn in range(ITERS):
        misfit = residual_of(estimate, grouped)
        shifted = estimate - gradient_of(misfit, grouped)
        total = jnp.zeros_like(shifted)
        for basis in range(NBASIS):
            total = total + basis_prox(shifted, basis, thresholds[basis], table)
        estimate = total / NBASIS
    return (estimate, misfit.reshape(BLOCKS, 2, VB))
```

```python
import math

import jax
import jax.numpy as jnp
import numpy as np
from jax import lax
from jax.sharding import PartitionSpec as P

PATCH = 64
HIGH = lax.Precision.HIGH
F32 = jnp.float32
BF16 = jnp.bfloat16
F16 = jnp.float16


def turns(rows, cols, period):
    angle = (rows * cols % period).astype(F32) * (2.0 * math.pi / period)
    return jnp.cos(angle), jnp.sin(angle)


def iota(size):
    return jnp.arange(size, dtype=jnp.int32)


def spread_matrix(groups, size):
    width = groups * size
    c = iota(width)
    return (c[:, None] == (c % size * groups + c // size)[None, :]).astype(F32)


def rows_forward(x, groups):
    rows = x.shape[1]
    count = groups * rows
    cos_g, sin_g = (np.cos(2 * np.pi * np.outer(np.arange(groups), np.arange(groups)) / groups), np.sin(2 * np.pi * np.outer(np.arange(groups), np.arange(groups)) / groups))
    mixed_re = jnp.einsum("kv,vnm->knm", jnp.asarray(cos_g, F32), x, precision=HIGH)
    mixed_im = -jnp.einsum("kv,vnm->knm", jnp.asarray(sin_g, F32), x, precision=HIGH)
    cos_t, sin_t = turns(iota(groups)[:, None], iota(rows)[None, :], count)
    cos_t, sin_t = cos_t[:, :, None], sin_t[:, :, None]
    both = jnp.concatenate([mixed_re * cos_t + mixed_im * sin_t, mixed_im * cos_t - mixed_re * sin_t], -1)
    cos_r, sin_r = turns(iota(rows)[:, None], iota(rows)[None, :], rows)
    p = jnp.einsum("kn,vnm->vkm", cos_r, both, precision=HIGH)
    q = jnp.einsum("kn,vnm->vkm", sin_r, both, precision=HIGH)
    m = x.shape[2]
    return jnp.concatenate([p[..., :m] + q[..., m:], p[..., m:] - q[..., :m]], -1)


def rows_inverse(y, groups):
    rows = y.shape[1]
    m = y.shape[2] // 2
    count = groups * rows
    cos_r, sin_r = turns(iota(rows)[:, None], iota(rows)[None, :], rows)
    p = jnp.einsum("kn,vnm->vkm", cos_r, y, precision=HIGH)
    q = jnp.einsum("kn,vnm->vkm", sin_r, y, precision=HIGH)
    re, im = p[..., :m] - q[..., m:], p[..., m:] + q[..., :m]
    cos_t, sin_t = turns(iota(groups)[:, None], iota(rows)[None, :], count)
    cos_t, sin_t = cos_t[:, :, None], sin_t[:, :, None]
    re, im = re * cos_t - im * sin_t, im * cos_t + re * sin_t
    cos_g, sin_g = (np.cos(2 * np.pi * np.outer(np.arange(groups), np.arange(groups)) / groups), np.sin(2 * np.pi * np.outer(np.arange(groups), np.arange(groups)) / groups))
    out = jnp.einsum("vk,knm->vnm", jnp.asarray(cos_g, F32), re, precision=HIGH)
    return out - jnp.einsum("vk,knm->vnm", jnp.asarray(sin_g, F32), im, precision=HIGH)


def column_matrix(wavs, m, down, scale):
    size = wavs * m
    cos_c, sin_c = turns(iota(size)[:, None], iota(size)[None, :], size)
    cos_c = (cos_c * scale).reshape(wavs, 1, m, down, 1, PATCH)
    sin_c = (sin_c * scale).reshape(wavs, 1, m, down, 1, PATCH)
    from_re = jnp.concatenate([cos_c, -sin_c], 4)
    from_im = jnp.concatenate([sin_c, cos_c], 4)
    return jnp.concatenate([from_re, from_im], 1).reshape(2 * size, 2 * size)


def soft(x, limit):
    return x - jnp.clip(x, -limit, limit)


def haar_mean(field, halo_left, halo_right, thresholds):
    bases = thresholds.shape[0]
    rows, width = field.shape
    pad = halo_left.shape[1]
    ext = jnp.concatenate([field, halo_right, halo_left], 1)
    span = ext.shape[1]
    place = iota(span)
    place = jnp.where(place < width + pad, place, place - span)
    root = math.sqrt(0.5)
    pairs = ext.reshape(rows // 2, 2, span)
    u = jnp.stack([(pairs[:, 0] + pairs[:, 1]) * root, (pairs[:, 0] - pairs[:, 1]) * root], 0)

    def limited(x, period):
        total = None
        for start in range(0, bases, period):
            index = place % period + start
            limit = jnp.zeros((span,), F32)
            inside = jnp.zeros((span,), jnp.bool_)
            for s in range(start, min(start + period, bases)):
                limit = jnp.where(index == s, thresholds[s], limit)
                inside = inside | (index == s)
            part = jnp.where(inside, soft(x, limit), 0.0)
            total = part if total is None else total + part
        return total

    def ahead(x, by):
        return jnp.roll(x, -by, axis=-1)

    def behind(x, by):
        return jnp.roll(x, by, axis=-1)

    s1 = (u + ahead(u, 1)) * root
    d1 = (u - ahead(u, 1)) * root
    s2 = (s1 + ahead(s1, 2)) * root
    d2 = (s1 - ahead(s1, 2)) * root
    s3 = (s2 + ahead(s2, 4)) * root
    d3 = (s2 - ahead(s2, 4)) * root
    s3, d3, d2, d1 = limited(s3, 8), limited(d3, 8), limited(d2, 4), limited(d1, 2)
    a2 = ((s3 + d3) + behind(s3 - d3, 4)) * root
    a1 = ((a2 + d2) + behind(a2 - d2, 2)) * root
    a0 = ((a1 + d1) + behind(a1 - d1, 1)) * root
    a0 = a0[..., :width] * (root / bases)
    return jnp.stack([a0[0] + a0[1], a0[0] - a0[1]], 1).reshape(rows, width)


def shards(image, kernel_v, kernel_u, measured, dest_owner, patch_slot, thresholds):
    vis = lax.axis_size("vis")
    wavs = lax.axis_size("wav")
    v = lax.axis_index("vis")
    rows, cols = image.shape
    img = rows * vis
    m = cols // vis
    down = rows // PATCH
    across = cols // PATCH
    blocks = kernel_v.shape[0]
    low = PATCH // vis
    spread = spread_matrix(vis, m)

    ids = jnp.concatenate([dest_owner, patch_slot[:, None]], 1)
    ids = lax.all_gather(ids, "vis", axis=0, tiled=True)
    owner, slot = ids[:, 0], ids[:, 1]
    a_block, b_block = slot // across, slot % across

    x = jnp.dot(image, spread, precision=HIGH).astype(F16)
    x = x.reshape(rows, vis, m).transpose(1, 0, 2)
    x = lax.all_to_all(x, "vis", split_axis=0, concat_axis=0, tiled=True).astype(F32)
    y = rows_forward(x, vis).astype(F16)
    y = y.reshape(vis, wavs, rows // wavs, 2 * m).transpose(1, 0, 2, 3)
    y = lax.all_to_all(y, "wav", split_axis=0, concat_axis=0, tiled=True).astype(F32)
    y = y.transpose(1, 2, 0, 3).reshape(cols, 2 * wavs * m)
    table = column_matrix(wavs, m, down, 1.0 / img)
    z = jnp.dot(y, table, precision=HIGH)
    z = z.reshape(vis, across, low, down, 2 * PATCH)
    tiles = z[:, b_block, :, a_block, :].reshape(vis * blocks, PATCH, 2 * PATCH)
    cos_k, sin_k = turns(v, owner[:, None] * rows + a_block[:, None] * PATCH + iota(PATCH)[None, :], img)
    cos_k = jnp.concatenate([cos_k, cos_k], 1)[:, None, :]
    sin_k = jnp.concatenate([sin_k, -sin_k], 1)[:, None, :]
    tiles = tiles * cos_k + jnp.roll(tiles, PATCH, axis=2) * sin_k
    tiles = lax.all_to_all(tiles.astype(F16), "vis", split_axis=0, concat_axis=0, tiled=True)
    patch = jnp.sum(tiles.reshape(vis, blocks, PATCH, 2 * PATCH).astype(F32), 0).astype(BF16)

    side_u = kernel_u.reshape(blocks, low, vis, -1).transpose(0, 2, 1, 3).reshape(kernel_u.shape)
    part_re = jnp.einsum("nba,nat->nbt", patch[..., :PATCH], kernel_v, preferred_element_type=F32)
    part_im = jnp.einsum("nba,nat->nbt", patch[..., PATCH:], kernel_v, preferred_element_type=F32)
    side = side_u.astype(F32)
    misfit = jnp.stack([jnp.sum(part_re * side, 1), jnp.sum(part_im * side, 1)], 1) - measured.astype(F32)
    w_re = (misfit[:, 0, None, :] * side).astype(BF16)
    w_im = (misfit[:, 1, None, :] * side).astype(BF16)
    term_re = jnp.einsum("nbt,nat->nba", w_re, kernel_v, preferred_element_type=F32)
    term_im = jnp.einsum("nbt,nat->nba", w_im, kernel_v, preferred_element_type=F32)
    terms = jnp.concatenate([term_re, term_im], -1).astype(BF16)

    terms = lax.all_gather(terms, "vis", axis=0, tiled=True).astype(F32)
    terms = terms * cos_k - jnp.roll(terms, PATCH, axis=2) * sin_k
    terms = terms.reshape(vis * blocks, vis, low, 2 * PATCH)
    flat = jnp.zeros((across * down, vis, low, 2 * PATCH), F32).at[b_block * down + a_block].add(terms)
    grad = flat.reshape(across, down, vis, low, 2 * PATCH).transpose(2, 0, 3, 1, 4).reshape(cols, 2 * rows)
    grad = lax.dot_general(grad, table, (((1,), (1,)), ((), ())), precision=HIGH).astype(BF16)
    grad = grad.reshape(cols, wavs, 2 * m).transpose(1, 0, 2)
    grad = lax.all_to_all(grad, "wav", split_axis=0, concat_axis=0, tiled=True).astype(F32)
    grad = grad.reshape(wavs, vis, rows // wavs, 2 * m).transpose(1, 0, 2, 3).reshape(vis, rows, 2 * m)
    grad = rows_inverse(grad, vis).astype(BF16)
    grad = lax.all_to_all(grad, "vis", split_axis=0, concat_axis=0, tiled=True)
    grad = grad.transpose(1, 0, 2).reshape(rows, cols)
    grad = lax.dot_general(grad, spread.astype(BF16), (((1,), (1,)), ((), ())), preferred_element_type=F32)
    shifted = image - grad
    halo = 8
    right = lax.ppermute(shifted[:, :halo], "wav", [(i, (i - 1) % wavs) for i in range(wavs)])
    left = lax.ppermute(shifted[:, -halo:], "wav", [(i, (i + 1) % wavs) for i in range(wavs)])
    return haar_mean(shifted, left, right, thresholds), misfit


def solution(mesh):
    both = ("vis", "wav")
    in_specs = (
        P("vis", "wav"),
        P(both, None, None),
        P(both, None, None),
        P(both, None, None),
        P(both, None),
        P(both),
        P(),
    )
    out_specs = (P("vis", "wav"), P(both, None, None))
    return jax.shard_map(shards, mesh=mesh, in_specs=in_specs, out_specs=out_specs, check_vma=False)
```

```python
import math

import jax
import jax.numpy as jnp
import numpy as np
from jax import lax
from jax.experimental import pallas as pl
from jax.experimental.pallas import tpu as pltpu
from jax.sharding import PartitionSpec as P

PATCH = 64
HIGH = lax.Precision.HIGH
F32 = jnp.float32
BF16 = jnp.bfloat16
F16 = jnp.float16


def turns(rows, cols, period):
    angle = (rows * cols % period).astype(F32) * (2.0 * math.pi / period)
    return jnp.cos(angle), jnp.sin(angle)


def iota(size):
    return jnp.arange(size, dtype=jnp.int32)


def spread_matrix(groups, size):
    width = groups * size
    c = iota(width)
    return (c[:, None] == (c % size * groups + c // size)[None, :]).astype(F32)


def rows_forward(x, groups):
    rows = x.shape[1]
    count = groups * rows
    cos_g, sin_g = (np.cos(2 * np.pi * np.outer(np.arange(groups), np.arange(groups)) / groups), np.sin(2 * np.pi * np.outer(np.arange(groups), np.arange(groups)) / groups))
    mixed_re = jnp.einsum("kv,vnm->knm", jnp.asarray(cos_g, F32), x, precision=HIGH)
    mixed_im = -jnp.einsum("kv,vnm->knm", jnp.asarray(sin_g, F32), x, precision=HIGH)
    cos_t, sin_t = turns(iota(groups)[:, None], iota(rows)[None, :], count)
    cos_t, sin_t = cos_t[:, :, None], sin_t[:, :, None]
    both = jnp.concatenate([mixed_re * cos_t + mixed_im * sin_t, mixed_im * cos_t - mixed_re * sin_t], -1)
    cos_r, sin_r = turns(iota(rows)[:, None], iota(rows)[None, :], rows)
    p = jnp.einsum("kn,vnm->vkm", cos_r, both, precision=HIGH)
    q = jnp.einsum("kn,vnm->vkm", sin_r, both, precision=HIGH)
    m = x.shape[2]
    return jnp.concatenate([p[..., :m] + q[..., m:], p[..., m:] - q[..., :m]], -1)


def rows_inverse(y, groups):
    rows = y.shape[1]
    m = y.shape[2] // 2
    count = groups * rows
    cos_r, sin_r = turns(iota(rows)[:, None], iota(rows)[None, :], rows)
    p = jnp.einsum("kn,vnm->vkm", cos_r, y, precision=HIGH)
    q = jnp.einsum("kn,vnm->vkm", sin_r, y, precision=HIGH)
    re, im = p[..., :m] - q[..., m:], p[..., m:] + q[..., :m]
    cos_t, sin_t = turns(iota(groups)[:, None], iota(rows)[None, :], count)
    cos_t, sin_t = cos_t[:, :, None], sin_t[:, :, None]
    re, im = re * cos_t - im * sin_t, im * cos_t + re * sin_t
    cos_g, sin_g = (np.cos(2 * np.pi * np.outer(np.arange(groups), np.arange(groups)) / groups), np.sin(2 * np.pi * np.outer(np.arange(groups), np.arange(groups)) / groups))
    out = jnp.einsum("vk,knm->vnm", jnp.asarray(cos_g, F32), re, precision=HIGH)
    return out - jnp.einsum("vk,knm->vnm", jnp.asarray(sin_g, F32), im, precision=HIGH)


def column_matrix(wavs, m, down, scale):
    size = wavs * m
    cos_c, sin_c = turns(iota(size)[:, None], iota(size)[None, :], size)
    cos_c = (cos_c * scale).reshape(wavs, 1, m, down, 1, PATCH)
    sin_c = (sin_c * scale).reshape(wavs, 1, m, down, 1, PATCH)
    from_re = jnp.concatenate([cos_c, -sin_c], 4)
    from_im = jnp.concatenate([sin_c, cos_c], 4)
    return jnp.concatenate([from_re, from_im], 1).reshape(2 * size, 2 * size)


def split(x):
    high = lax.reduce_precision(x, 8, 7)
    return high.astype(BF16), (x - high).astype(BF16)


def cosine(count, period):
    part = (count % period).astype(F32) * (1.0 / period)
    part = 0.25 - jnp.abs(part - jnp.round(part))
    square = part * part
    terms = [(-1) ** i * (2 * math.pi) ** (2 * i + 1) / math.factorial(2 * i + 1) for i in range(7)]
    value = jnp.full_like(part, terms[-1])
    for term in terms[-2::-1]:
        value = value * square + term
    return value * part


def row_table(size):
    k, n = lax.broadcasted_iota(jnp.int32, (2 * size, size), 0), lax.broadcasted_iota(jnp.int32, (2 * size, size), 1)
    return split(cosine(k % size * n - k // size * (size // 4), size))


def column_table(wavs, m, turned):
    size = wavs * m
    shape = (2 * size, 2 * size)
    row, col = lax.broadcasted_iota(jnp.int32, shape, int(turned)), lax.broadcasted_iota(jnp.int32, shape, 1 - int(turned))
    n = row // (2 * m) * m + row % m
    k = col // (2 * PATCH) * PATCH + col % PATCH
    quarter = col // PATCH % 2 - row // m % 2
    return split(cosine(n * k + quarter * (size // 4), size))


def twist_table(groups, rows):
    n, k = lax.broadcasted_iota(jnp.int32, (rows, 2 * groups), 0), lax.broadcasted_iota(jnp.int32, (rows, 2 * groups), 1)
    count = groups * rows
    return cosine(n * (k % groups) - k // groups * (count // 4), count)


def in_vmem(count):
    return [pl.BlockSpec(memory_space=pltpu.VMEM)] * count


VMEM_LIMIT = 56 * 1024 * 1024
ROOT = math.sqrt(0.5)


def rows_forward_kernel(x_ref, high_ref, low_ref, twist_ref, y_ref):
    rows, m = x_ref.shape[1:]
    wavs = y_ref.shape[0]
    part = rows // wavs
    x = [x_ref[i] for i in range(8)]
    e0, e1, f0, f1 = x[0] + x[4], x[0] - x[4], x[2] + x[6], x[2] - x[6]
    g0, g1, h0, h1 = x[1] + x[5], x[1] - x[5], x[3] + x[7], x[3] - x[7]
    gm, gp = (g1 - h1) * ROOT, (g1 + h1) * ROOT
    zero = jnp.zeros_like(e0)
    mixed = (
        (e0 + f0 + g0 + h0, zero),
        (e1 + gm, -f1 - gp),
        (e0 - f0, h0 - g0),
        (e1 - gm, f1 - gp),
        (e0 + f0 - g0 - h0, zero),
    )
    for k, (re, im) in enumerate(mixed):
        if k:
            cos_t, sin_t = twist_ref[:, k : k + 1], twist_ref[:, 8 + k : 9 + k]
            re, im = re * cos_t + im * sin_t, im * cos_t - re * sin_t
        both = jnp.concatenate([re, im], 1)
        high = both.astype(BF16)
        low = (both - high.astype(F32)).astype(BF16)
        out = jnp.dot(high_ref[...], high, preferred_element_type=F32)
        out += jnp.dot(high_ref[...], low, preferred_element_type=F32)
        out += jnp.dot(low_ref[...], high, preferred_element_type=F32)
        p_re, p_im, q_re, q_im = out[:rows, :m], out[:rows, m:], out[rows:, :m], out[rows:, m:]
        here = jnp.concatenate([p_re + q_im, p_im - q_re], 1)
        for w in range(wavs):
            y_ref[w, k] = here[w * part : (w + 1) * part]
        if k in (1, 2, 3):
            there = jnp.concatenate([p_re - q_im, -p_im - q_re], 1)
            there = pltpu.roll(there, rows - 1, 0)
            for w in range(wavs):
                y_ref[w, 8 - k] = there[w * part : (w + 1) * part]


def rows_forward_fast(x, wavs, table, twist):
    groups, rows, m = x.shape
    return pl.pallas_call(
        rows_forward_kernel,
        in_specs=in_vmem(4),
        out_specs=in_vmem(1)[0],
        out_shape=jax.ShapeDtypeStruct((wavs, groups, rows // wavs, 2 * m), F32),
        compiler_params=pltpu.CompilerParams(vmem_limit_bytes=VMEM_LIMIT),
        name="rows_forward",
    )(x, *table, twist)


AT_ONCE = 8


def shares_kernel(a_ref, b_ref, y_ref, high_ref, low_ref, cos_ref, sin_ref, tile_ref, z_ref, head_ref, rest_ref):
    wavs, groups, part, double = y_ref.shape
    down = z_ref.shape[0]
    count, low = tile_ref.shape[0], PATCH // groups
    wide = 2 * PATCH
    scale = 1.0 / (groups * down * PATCH)
    for k in range(groups):
        for w in range(wavs):
            y = y_ref[w, k]
            high = y.astype(BF16)
            spot = (pl.ds(k * part, part), pl.ds(w * double, double))
            head_ref[spot] = high
            rest_ref[spot] = (y - high.astype(F32)).astype(BF16)
    for a in range(0, down, 2):
        spot = (slice(None), pl.ds(a * wide, 2 * wide))
        z = jnp.dot(head_ref[...], high_ref[spot], preferred_element_type=F32)
        z += jnp.dot(rest_ref[...], high_ref[spot], preferred_element_type=F32)
        z += jnp.dot(head_ref[...], low_ref[spot], preferred_element_type=F32)
        z = z * scale
        z_ref[a] = z[:, :wide].reshape(groups, part, wide)
        z_ref[a + 1] = z[:, wide:].reshape(groups, part, wide)

    @pl.loop(0, count // AT_ONCE)
    def _(step):
        for i in range(AT_ONCE):
            n = step * AT_ONCE + i
            start = pl.multiple_of(b_ref[n] * low, low)
            tile = z_ref[a_ref[n], :, pl.ds(start, low), :].reshape(PATCH, wide)
            tile_ref[n] = tile * cos_ref[pl.ds(n, 1), :] + pltpu.roll(tile, PATCH, 1) * sin_ref[pl.ds(n, 1), :]


def shares_fast(a_block, b_block, y, table, cos_k, sin_k):
    wavs, groups, part, double = y.shape
    down = wavs * double // 2 // PATCH
    return pl.pallas_call(
        shares_kernel,
        in_specs=[pl.BlockSpec(memory_space=pltpu.SMEM)] * 2 + in_vmem(5),
        out_specs=in_vmem(1)[0],
        out_shape=jax.ShapeDtypeStruct((a_block.shape[0], PATCH, 2 * PATCH), F32),
        scratch_shapes=[pltpu.VMEM((down, groups, part, 2 * PATCH), F32)] + [pltpu.VMEM((groups * part, wavs * double), BF16)] * 2,
        compiler_params=pltpu.CompilerParams(vmem_limit_bytes=VMEM_LIMIT),
        name="shares",
    )(a_block, b_block, y, *table, cos_k, sin_k)


def gather_kernel(a_ref, b_ref, term_ref, high_ref, low_ref, cos_ref, sin_ref, y_ref, g_ref, head_ref):
    wavs, groups, part, double = y_ref.shape
    down = g_ref.shape[0]
    count, low = term_ref.shape[0], PATCH // groups
    wide = 2 * PATCH
    g_ref[...] = jnp.zeros_like(g_ref)

    @pl.loop(0, count // AT_ONCE)
    def _(step):
        tiles = []
        for i in range(AT_ONCE):
            n = step * AT_ONCE + i
            tile = term_ref[n].astype(F32)
            tiles.append(tile * cos_ref[pl.ds(n, 1), :] - pltpu.roll(tile, PATCH, 1) * sin_ref[pl.ds(n, 1), :])
        for i in range(AT_ONCE):
            n = step * AT_ONCE + i
            start = pl.multiple_of(b_ref[n] * low, low)
            g_ref[a_ref[n], :, pl.ds(start, low), :] += tiles[i].reshape(groups, low, wide)

    for a in range(down):
        head_ref[:, a * wide : (a + 1) * wide] = g_ref[a].reshape(groups * part, wide).astype(BF16)
    scale = 1.0 / (groups * down * PATCH)
    for w in range(wavs):
        spot = (slice(None), pl.ds(w * double, double))
        y = jnp.dot(head_ref[...], high_ref[spot], preferred_element_type=F32)
        y += jnp.dot(head_ref[...], low_ref[spot], preferred_element_type=F32)
        y_ref[w] = (y * scale).astype(BF16).reshape(groups, part, double)


def gather_fast(a_block, b_block, terms, table, cos_k, sin_k, wavs, groups, part, m):
    down = wavs * m // PATCH
    return pl.pallas_call(
        gather_kernel,
        in_specs=[pl.BlockSpec(memory_space=pltpu.SMEM)] * 2 + in_vmem(5),
        out_specs=in_vmem(1)[0],
        out_shape=jax.ShapeDtypeStruct((wavs, groups, part, 2 * m), BF16),
        scratch_shapes=[pltpu.VMEM((down, groups, part, 2 * PATCH), F32), pltpu.VMEM((groups * part, 2 * PATCH * down), BF16)],
        compiler_params=pltpu.CompilerParams(vmem_limit_bytes=VMEM_LIMIT),
        name="gather",
    )(a_block, b_block, terms, *table, cos_k, sin_k)


def rows_inverse_kernel(y_ref, high_ref, low_ref, twist_ref, x_ref, re_ref, im_ref):
    rows, m = x_ref.shape[1:]
    wavs = y_ref.shape[0]
    for k in range(8):
        y = jnp.concatenate([y_ref[w, k] for w in range(wavs)], 0)
        out = jnp.dot(high_ref[...], y, preferred_element_type=F32)
        out += jnp.dot(low_ref[...], y, preferred_element_type=F32)
        re, im = out[:rows, :m] - out[rows:, m:], out[:rows, m:] + out[rows:, :m]
        if k:
            cos_t, sin_t = twist_ref[:, k : k + 1], twist_ref[:, 8 + k : 9 + k]
            re, im = re * cos_t - im * sin_t, im * cos_t + re * sin_t
        re_ref[k] = re
        im_ref[k] = im
    even, odd = re_ref[0] + re_ref[4], re_ref[0] - re_ref[4]
    r1, r2, r3 = re_ref[1] + re_ref[7], re_ref[2] + re_ref[6], re_ref[3] + re_ref[5]
    i1, i2, i3 = im_ref[1] - im_ref[7], im_ref[2] - im_ref[6], im_ref[3] - im_ref[5]
    rm, ip = (r1 - r3) * ROOT, (i1 + i3) * ROOT
    x_ref[0] = (even + r2 + (r1 + r3)).astype(BF16)
    x_ref[4] = (even + r2 - (r1 + r3)).astype(BF16)
    x_ref[2] = (even - r2 - (i1 - i3)).astype(BF16)
    x_ref[6] = (even - r2 + (i1 - i3)).astype(BF16)
    x_ref[1] = (odd + rm - ip - i2).astype(BF16)
    x_ref[7] = (odd + rm + ip + i2).astype(BF16)
    x_ref[3] = (odd - rm - ip + i2).astype(BF16)
    x_ref[5] = (odd - rm + ip - i2).astype(BF16)


def rows_inverse_fast(y, table, twist):
    wavs, groups, part, double = y.shape
    rows, m = wavs * part, double // 2
    return pl.pallas_call(
        rows_inverse_kernel,
        in_specs=in_vmem(4),
        out_specs=in_vmem(1)[0],
        out_shape=jax.ShapeDtypeStruct((groups, rows, m), BF16),
        scratch_shapes=[pltpu.VMEM((groups, rows, m), F32)] * 2,
        compiler_params=pltpu.CompilerParams(vmem_limit_bytes=VMEM_LIMIT),
        name="rows_inverse",
    )(y, *table, twist)


HALO = 8
LANES = 128


def haar_kernel(field_ref, edge_ref, limit_ref, out_ref, *, bases):
    rows, width = field_ref.shape
    span = width + LANES
    even = lax.broadcasted_iota(jnp.int32, (rows, span), 0) % 2 == 0

    def mix(x, even):
        other = jnp.where(even, pltpu.roll(x, rows - 1, 0), pltpu.roll(x, 1, 0))
        return jnp.where(even, x, -x) + other

    def ahead(x, by):
        return pltpu.roll(x, span - by, 1)

    def behind(x, by):
        return pltpu.roll(x, by, 1)

    def mean(u):
        spot = 0
        level = []
        for period in (2, 4, 8):
            forward = ahead(u, period // 2)
            parts = [u + forward, u - forward]
            limits = []
            for start in range(0, bases, period):
                limits.append(limit_ref[spot : spot + 1, :])
                spot += 1
            limited = []
            for x in parts if period == 8 else parts[1:]:
                total = None
                for limit in limits:
                    x_soft = x - jnp.minimum(jnp.maximum(x, -limit), limit)
                    total = x_soft if total is None else total + x_soft
                limited.append(total)
            level.append(limited)
            u = parts[0]
        s3, d3 = level[2]
        back = (s3 + d3) + behind(s3 - d3, 4)
        for by, (d,) in ((2, level[1]), (1, level[0])):
            back = back * 0.5
            back = (back + d) + behind(back - d, by)
        return back[:, :width] * (0.25 / bases)

    field = jnp.concatenate([field_ref[...], edge_ref[...]], 1)
    out_ref[...] = mix(mean(mix(field, even)), even[:, :width])


def haar_limits(width, thresholds):
    bases = thresholds.shape[0]
    span = width + LANES
    place = iota(span)
    place = jnp.where(place < width + LANES // 2, place, place - span) + 8
    out = []
    for period in (2, 4, 8):
        scale = math.sqrt(2.0 * period)
        for start in range(0, bases, period):
            index = place % period + start
            limit = jnp.full((span,), 3e38, F32)
            for s in range(start, min(start + period, bases)):
                limit = jnp.where(index == s, thresholds[s] * scale, limit)
            out.append(limit)
    return jnp.stack(out)


def haar_mean(field, halo_left, halo_right, thresholds):
    bases = thresholds.shape[0]
    rows, width = field.shape
    middle = jnp.zeros((rows, LANES - 2 * HALO), F32)
    edge = jnp.concatenate([halo_right, middle, halo_left], 1)
    limits = haar_limits(width, thresholds)
    step = min(rows, 64)
    return pl.pallas_call(
        lambda *refs: haar_kernel(*refs, bases=bases),
        grid=(rows // step,),
        in_specs=[
            pl.BlockSpec((step, width), lambda i: (i, 0)),
            pl.BlockSpec((step, LANES), lambda i: (i, 0)),
            pl.BlockSpec(limits.shape, lambda i: (0, 0)),
        ],
        out_specs=pl.BlockSpec((step, width), lambda i: (i, 0)),
        out_shape=jax.ShapeDtypeStruct((rows, width), F32),
        name="haar",
    )(field, edge, limits)


def shards(image, kernel_v, kernel_u, measured, dest_owner, patch_slot, thresholds):
    vis = lax.axis_size("vis")
    wavs = lax.axis_size("wav")
    v = lax.axis_index("vis")
    rows, cols = image.shape
    img = rows * vis
    m = cols // vis
    down = rows // PATCH
    across = cols // PATCH
    blocks = kernel_v.shape[0]
    low = PATCH // vis
    part = rows // wavs
    fast = vis == 8 and m == LANES and low == 8 and part % 8 == 0
    spread = spread_matrix(vis, m)

    ids = jnp.concatenate([dest_owner, patch_slot[:, None]], 1)
    ids = lax.all_gather(ids, "vis", axis=0, tiled=True)
    owner, slot = ids[:, 0], ids[:, 1]
    a_block, b_block = slot // across, slot % across

    x = jnp.dot(image, spread, precision=HIGH).astype(F16)
    x = x.reshape(rows, vis, m).transpose(1, 0, 2)
    x = lax.all_to_all(x, "vis", split_axis=0, concat_axis=0, tiled=True).astype(F32)
    if fast:
        rows_high_low, twist = row_table(rows), twist_table(vis, rows)
        y = rows_forward_fast(x, wavs, rows_high_low, twist).astype(F16)
    else:
        y = rows_forward(x, vis).astype(F16)
        y = y.reshape(vis, wavs, part, 2 * m).transpose(1, 0, 2, 3)
    y = lax.all_to_all(y, "wav", split_axis=0, concat_axis=0, tiled=True).astype(F32)
    cos_k, sin_k = turns(v, owner[:, None] * rows + a_block[:, None] * PATCH + iota(PATCH)[None, :], img)
    cos_k = jnp.concatenate([cos_k, cos_k], 1)
    sin_k = jnp.concatenate([sin_k, -sin_k], 1)
    if fast:
        tiles = shares_fast(a_block, b_block, y, column_table(wavs, m, False), cos_k, sin_k)
    else:
        y = y.transpose(1, 2, 0, 3).reshape(cols, 2 * wavs * m)
        table = column_matrix(wavs, m, down, 1.0 / img)
        z = jnp.dot(y, table, precision=HIGH)
        z = z.reshape(vis, across, low, down, 2 * PATCH)
        tiles = z[:, b_block, :, a_block, :].reshape(vis * blocks, PATCH, 2 * PATCH)
        tiles = tiles * cos_k[:, None] + jnp.roll(tiles, PATCH, axis=2) * sin_k[:, None]
    tiles = lax.all_to_all(tiles.astype(F16), "vis", split_axis=0, concat_axis=0, tiled=True)
    patch = jnp.sum(tiles.reshape(vis, blocks, PATCH, 2 * PATCH).astype(F32), 0).astype(BF16)

    side_u = kernel_u.reshape(blocks, low, vis, -1).transpose(0, 2, 1, 3).reshape(kernel_u.shape)
    part_re = jnp.einsum("nba,nat->nbt", patch[..., :PATCH], kernel_v, preferred_element_type=F32)
    part_im = jnp.einsum("nba,nat->nbt", patch[..., PATCH:], kernel_v, preferred_element_type=F32)
    side = side_u.astype(F32)
    misfit = jnp.stack([jnp.sum(part_re * side, 1), jnp.sum(part_im * side, 1)], 1) - measured.astype(F32)
    w_re = (misfit[:, 0, None, :] * side).astype(BF16)
    w_im = (misfit[:, 1, None, :] * side).astype(BF16)
    term_re = jnp.einsum("nbt,nat->nba", w_re, kernel_v, preferred_element_type=F32)
    term_im = jnp.einsum("nbt,nat->nba", w_im, kernel_v, preferred_element_type=F32)
    terms = jnp.concatenate([term_re, term_im], -1).astype(BF16)

    terms = lax.all_gather(terms, "vis", axis=0, tiled=True)
    if fast:
        grad = gather_fast(a_block, b_block, terms, column_table(wavs, m, True), cos_k, sin_k, wavs, vis, part, m)
    else:
        terms = terms.astype(F32)
        terms = terms * cos_k[:, None] - jnp.roll(terms, PATCH, axis=2) * sin_k[:, None]
        terms = terms.reshape(vis * blocks, vis, low, 2 * PATCH)
        flat = jnp.zeros((across * down, vis, low, 2 * PATCH), F32).at[b_block * down + a_block].add(terms)
        grad = flat.reshape(across, down, vis, low, 2 * PATCH).transpose(2, 0, 3, 1, 4).reshape(cols, 2 * rows)
        grad = lax.dot_general(grad, table, (((1,), (1,)), ((), ())), precision=HIGH).astype(BF16)
        grad = grad.reshape(vis, part, wavs, 2 * m).transpose(2, 0, 1, 3)
    grad = lax.all_to_all(grad, "wav", split_axis=0, concat_axis=0, tiled=True)
    if fast:
        grad = rows_inverse_fast(grad, rows_high_low, twist)
    else:
        grad = grad.astype(F32).transpose(1, 0, 2, 3).reshape(vis, rows, 2 * m)
        grad = rows_inverse(grad, vis).astype(BF16)
    grad = lax.all_to_all(grad, "vis", split_axis=0, concat_axis=0, tiled=True)
    grad = grad.transpose(1, 0, 2).reshape(rows, cols)
    grad = lax.dot_general(grad, spread.astype(BF16), (((1,), (1,)), ((), ())), preferred_element_type=F32)
    shifted = image - grad
    right = lax.ppermute(shifted[:, :HALO], "wav", [(i, (i - 1) % wavs) for i in range(wavs)])
    left = lax.ppermute(shifted[:, -HALO:], "wav", [(i, (i + 1) % wavs) for i in range(wavs)])
    return haar_mean(shifted, left, right, thresholds), misfit


def solution(mesh):
    both = ("vis", "wav")
    in_specs = (
        P("vis", "wav"),
        P(both, None, None),
        P(both, None, None),
        P(both, None, None),
        P(both, None),
        P(both),
        P(),
    )
    out_specs = (P("vis", "wav"), P(both, None, None))
    return jax.shard_map(shards, mesh=mesh, in_specs=in_specs, out_specs=out_specs, check_vma=False)
```

```python
import math

import jax
import jax.numpy as jnp
import numpy as np
from jax import lax
from jax.experimental import pallas as pl
from jax.experimental.pallas import tpu as pltpu
from jax.sharding import PartitionSpec as P


PATCH = 64
HIGH = lax.Precision.HIGH
F32 = jnp.float32
BF16 = jnp.bfloat16
F16 = jnp.float16


def turns(rows, cols, period):
    angle = (rows * cols % period).astype(F32) * (2.0 * math.pi / period)
    return jnp.cos(angle), jnp.sin(angle)


def iota(size):
    return jnp.arange(size, dtype=jnp.int32)


def spread_matrix(groups, size):
    width = groups * size
    c = iota(width)
    return (c[:, None] == (c % size * groups + c // size)[None, :]).astype(F32)


def rows_forward(x, groups):
    rows = x.shape[1]
    count = groups * rows
    cos_g, sin_g = (np.cos(2 * np.pi * np.outer(np.arange(groups), np.arange(groups)) / groups), np.sin(2 * np.pi * np.outer(np.arange(groups), np.arange(groups)) / groups))
    mixed_re = jnp.einsum("kv,vnm->knm", jnp.asarray(cos_g, F32), x, precision=HIGH)
    mixed_im = -jnp.einsum("kv,vnm->knm", jnp.asarray(sin_g, F32), x, precision=HIGH)
    cos_t, sin_t = turns(iota(groups)[:, None], iota(rows)[None, :], count)
    cos_t, sin_t = cos_t[:, :, None], sin_t[:, :, None]
    both = jnp.concatenate([mixed_re * cos_t + mixed_im * sin_t, mixed_im * cos_t - mixed_re * sin_t], -1)
    cos_r, sin_r = turns(iota(rows)[:, None], iota(rows)[None, :], rows)
    p = jnp.einsum("kn,vnm->vkm", cos_r, both, precision=HIGH)
    q = jnp.einsum("kn,vnm->vkm", sin_r, both, precision=HIGH)
    m = x.shape[2]
    return jnp.concatenate([p[..., :m] + q[..., m:], p[..., m:] - q[..., :m]], -1)


def rows_inverse(y, groups):
    rows = y.shape[1]
    m = y.shape[2] // 2
    count = groups * rows
    cos_r, sin_r = turns(iota(rows)[:, None], iota(rows)[None, :], rows)
    p = jnp.einsum("kn,vnm->vkm", cos_r, y, precision=HIGH)
    q = jnp.einsum("kn,vnm->vkm", sin_r, y, precision=HIGH)
    re, im = p[..., :m] - q[..., m:], p[..., m:] + q[..., :m]
    cos_t, sin_t = turns(iota(groups)[:, None], iota(rows)[None, :], count)
    cos_t, sin_t = cos_t[:, :, None], sin_t[:, :, None]
    re, im = re * cos_t - im * sin_t, im * cos_t + re * sin_t
    cos_g, sin_g = (np.cos(2 * np.pi * np.outer(np.arange(groups), np.arange(groups)) / groups), np.sin(2 * np.pi * np.outer(np.arange(groups), np.arange(groups)) / groups))
    out = jnp.einsum("vk,knm->vnm", jnp.asarray(cos_g, F32), re, precision=HIGH)
    return out - jnp.einsum("vk,knm->vnm", jnp.asarray(sin_g, F32), im, precision=HIGH)


def column_matrix(wavs, m, down, scale):
    size = wavs * m
    cos_c, sin_c = turns(iota(size)[:, None], iota(size)[None, :], size)
    cos_c = (cos_c * scale).reshape(wavs, 1, m, down, 1, PATCH)
    sin_c = (sin_c * scale).reshape(wavs, 1, m, down, 1, PATCH)
    from_re = jnp.concatenate([cos_c, -sin_c], 4)
    from_im = jnp.concatenate([sin_c, cos_c], 4)
    return jnp.concatenate([from_re, from_im], 1).reshape(2 * size, 2 * size)


def split(x):
    high = lax.reduce_precision(x, 8, 7)
    return high.astype(BF16), (x - high).astype(BF16)


def bits(size):
    return size.bit_length() - 1


def cosine(count, period):
    part = (count & (period - 1)).astype(F32) * (1.0 / period)
    part = 0.25 - jnp.abs(part - jnp.where(part > 0.5, 1.0, 0.0))
    square = part * part
    terms = [(-1) ** i * (2 * math.pi) ** (2 * i + 1) / math.factorial(2 * i + 1) for i in range(7)]
    value = jnp.full_like(part, terms[-1])
    for term in terms[-2::-1]:
        value = value * square + term
    return value * part


def grid_of(shape):
    return [lax.broadcasted_iota(jnp.int32, shape, axis) for axis in (0, 1)]


def row_table(size, first):
    k, n = grid_of((2 * size, size))
    return split(cosine(((k + first) & (size - 1)) * n - (k >> bits(size)) * (size // 4), size))


def row_table_back(size, first):
    r, k = grid_of((2 * size, size))
    return split(cosine(((k + first) & (size - 1)) * (r & (size - 1)) - (r >> bits(size)) * (size // 4), size))


def column_table(wavs, m, first, turned):
    size = wavs * m
    row, col = grid_of((2 * size, 2 * size))[:: -1 if turned else 1]
    n = (row >> bits(2 * m)) * m + (row & (m - 1)) + first * m
    k = (col >> bits(2 * PATCH)) * PATCH + (col & (PATCH - 1))
    quarter = (col >> bits(PATCH) & 1) - (row >> bits(m) & 1)
    return split(cosine((n & (size - 1)) * k + quarter * (size // 4), size))


def twist_table(groups, rows):
    n, k = grid_of((rows, 2 * groups))
    count = groups * rows
    return cosine(n * (k & (groups - 1)) - (k >> bits(groups)) * (count // 4), count)


def in_vmem(count):
    return [pl.BlockSpec(memory_space=pltpu.VMEM)] * count


VMEM_LIMIT = 56 * 1024 * 1024
ROOT = math.sqrt(0.5)


AT_ONCE = 8
HALVES = ((0, 4, 1, 7), (2, 6, 3, 5))
ORDER = HALVES[0] + HALVES[1]


def call(kernel, out_shapes, scratch, *args, smem=0):
    return pl.pallas_call(
        kernel,
        in_specs=[pl.BlockSpec(memory_space=pltpu.SMEM)] * smem + in_vmem(len(args) - smem),
        out_specs=in_vmem(len(out_shapes)),
        out_shape=[jax.ShapeDtypeStruct(shape, kind) for shape, kind in out_shapes],
        scratch_shapes=[pltpu.VMEM(shape, kind) for shape, kind in scratch],
        compiler_params=pltpu.CompilerParams(vmem_limit_bytes=VMEM_LIMIT),
    )(*args)


def rows_forward_kernel(x_ref, high_ref, low_ref, twist_ref, *y_refs, half):
    rows, m = x_ref.shape[1:]
    wavs = len(y_refs)
    part = rows // wavs
    x = [x_ref[i].astype(F32) for i in range(8)]
    e0, e1, f0, f1 = x[0] + x[4], x[0] - x[4], x[2] + x[6], x[2] - x[6]
    g0, g1, h0, h1 = x[1] + x[5], x[1] - x[5], x[3] + x[7], x[3] - x[7]
    gm, gp = (g1 - h1) * ROOT, (g1 + h1) * ROOT
    zero = jnp.zeros_like(e0)
    mixed = {
        0: (e0 + f0 + g0 + h0, zero),
        1: (e1 + gm, -f1 - gp),
        2: (e0 - f0, h0 - g0),
        3: (e1 - gm, f1 - gp),
        4: (e0 + f0 - g0 - h0, zero),
    }
    for spot, k in enumerate(HALVES[half]):
        if k > 4:
            continue
        re, im = mixed[k]
        if k:
            cos_t, sin_t = twist_ref[:, k : k + 1], twist_ref[:, 8 + k : 9 + k]
            re, im = re * cos_t + im * sin_t, im * cos_t - re * sin_t
        both = jnp.concatenate([re, im], 1)
        high = both.astype(BF16)
        low = (both - high.astype(F32)).astype(BF16)
        out = jnp.dot(high_ref[...], high, preferred_element_type=F32)
        out += jnp.dot(high_ref[...], low, preferred_element_type=F32)
        out += jnp.dot(low_ref[...], high, preferred_element_type=F32)
        p_re, p_im, q_re, q_im = out[:rows, :m], out[:rows, m:], out[rows:, :m], out[rows:, m:]
        here = jnp.concatenate([p_re + q_im, p_im - q_re], 1)
        for w in range(wavs):
            y_refs[w][spot] = here[w * part : (w + 1) * part]
        if k in (1, 2, 3):
            there = jnp.concatenate([p_re - q_im, -p_im - q_re], 1)
            there = pltpu.roll(there, rows - 1, 0)
            for w in range(wavs):
                y_refs[w][spot + 1] = there[w * part : (w + 1) * part]


def rows_forward_fast(x, wavs, table, twist, half):
    groups, rows, m = x.shape
    kernel = lambda *refs: rows_forward_kernel(*refs, half=half)
    return call(kernel, [((groups // 2, rows // wavs, 2 * m), F32)] * wavs, [], x, *table, twist)


def shares_kernel(a_ref, b_ref, *refs, wavs):
    y_refs = refs[:wavs]
    high_ref, low_ref, cos_ref, sin_ref, far_ref, near_ref, z_ref, head_ref, rest_ref = refs[wavs:]
    groups, part, double = y_refs[0].shape
    down = z_ref.shape[0]
    wide = 2 * PATCH
    low = 8
    blocks = near_ref.shape[1]
    scale = 1.0 / (2 * groups * down * PATCH)
    for w in range(wavs):
        y = y_refs[w][...].astype(F32).reshape(groups * part, double)
        high = y.astype(BF16)
        head_ref[:, w * double : (w + 1) * double] = high
        rest_ref[:, w * double : (w + 1) * double] = (y - high.astype(F32)).astype(BF16)
    for a in range(0, down, 2):
        spot = (slice(None), pl.ds(a * wide, 2 * wide))
        z = jnp.dot(head_ref[...], high_ref[spot], preferred_element_type=F32)
        z += jnp.dot(rest_ref[...], high_ref[spot], preferred_element_type=F32)
        z += jnp.dot(head_ref[...], low_ref[spot], preferred_element_type=F32)
        z = z * scale
        z_ref[a] = z[:, :wide].reshape(groups, part, wide)
        z_ref[a + 1] = z[:, wide:].reshape(groups, part, wide)
    for mask in (1, 3, 5, 7, 0, 2, 4, 6):
        out_ref = far_ref if mask % 2 else near_ref

        @pl.loop(0, blocks // AT_ONCE)
        def _(step):
            for i in range(AT_ONCE):
                at = step * AT_ONCE + i
                n = mask * blocks + at
                start = pl.multiple_of(b_ref[n] * low, low)
                tile = z_ref[a_ref[n], :, pl.ds(start, low), :].reshape(groups * low, wide)
                out_ref[mask // 2, at] = tile * cos_ref[pl.ds(n, 1), :] + pltpu.roll(tile, PATCH, 1) * sin_ref[pl.ds(n, 1), :]


def shares_fast(a_block, b_block, ys, table, cos_k, sin_k):
    groups, part, double = ys[0].shape
    wavs = len(ys)
    width = wavs * double
    blocks = a_block.shape[0] // 8
    out = ((4, blocks, groups * 8, 2 * PATCH), F32)
    scratch = [((width // (2 * PATCH), groups, part, 2 * PATCH), F32)] + [((groups * part, width), BF16)] * 2
    kernel = lambda *refs: shares_kernel(*refs, wavs=wavs)
    return call(kernel, [out, out], scratch, a_block, b_block, *ys, *table, cos_k, sin_k, smem=2)


def gather_kernel(a_ref, b_ref, *refs):
    term_refs = [ref for chip in range(4) for ref in (refs[chip], refs[4].at[chip])]
    high_ref, low_ref, cos_ref, sin_ref = refs[5:9]
    y_refs, (g_ref, head_ref) = refs[9:-2], refs[-2:]
    groups, part, double = y_refs[0].shape
    down = g_ref.shape[0]
    wide = 2 * PATCH
    low = 8
    blocks = term_refs[0].shape[0]
    g_ref[...] = jnp.zeros_like(g_ref)
    for mask in range(8):

        @pl.loop(0, blocks // AT_ONCE)
        def _(step):
            tiles = []
            for i in range(AT_ONCE):
                at = step * AT_ONCE + i
                n = mask * blocks + at
                tile = term_refs[mask][at].astype(F32)
                tiles.append(tile * cos_ref[pl.ds(n, 1), :] - pltpu.roll(tile, PATCH, 1) * sin_ref[pl.ds(n, 1), :])
            for i in range(AT_ONCE):
                n = mask * blocks + step * AT_ONCE + i
                start = pl.multiple_of(b_ref[n] * low, low)
                g_ref[a_ref[n], :, pl.ds(start, low), :] += tiles[i].reshape(groups, low, wide)

    for a in range(down):
        head_ref[:, a * wide : (a + 1) * wide] = g_ref[a].reshape(groups * part, wide).astype(BF16)
    scale = 1.0 / (2 * groups * down * PATCH)
    for w, y_ref in enumerate(y_refs):
        spot = (slice(None), pl.ds(w * double, double))
        y = jnp.dot(head_ref[...], high_ref[spot], preferred_element_type=F32)
        y += jnp.dot(head_ref[...], low_ref[spot], preferred_element_type=F32)
        y_ref[...] = (y * scale).astype(BF16).reshape(groups, part, double)


def gather_fast(a_block, b_block, terms, table, cos_k, sin_k, wavs, part, m):
    width = 2 * wavs * m
    out = [((4, part, 2 * m), BF16)] * wavs
    scratch = [((width // (2 * PATCH), 4, part, 2 * PATCH), F32), ((4 * part, width), BF16)]
    return call(gather_kernel, out, scratch, a_block, b_block, *terms, *table, cos_k, sin_k, smem=2)


def untwist(y_refs, spot, k, high_ref, low_ref, twist_ref):
    y = jnp.concatenate([ref[spot] for ref in y_refs], 0)
    rows, m = y.shape[0], y.shape[1] // 2
    out = jnp.dot(high_ref[...], y, preferred_element_type=F32)
    out += jnp.dot(low_ref[...], y, preferred_element_type=F32)
    re, im = out[:rows, :m] - out[rows:, m:], out[:rows, m:] + out[rows:, :m]
    if k:
        cos_t, sin_t = twist_ref[:, k : k + 1], twist_ref[:, 8 + k : 9 + k]
        re, im = re * cos_t - im * sin_t, im * cos_t + re * sin_t
    return re, im


def rows_inverse_first(*refs):
    y_refs, (high_ref, low_ref, twist_ref, out_ref) = refs[:-4], refs[-4:]
    (re0, _), (re4, _), (re1, im1), (re7, im7) = [
        untwist(y_refs, spot, k, high_ref, low_ref, twist_ref) for spot, k in enumerate(HALVES[0])
    ]
    out_ref[0] = re0 + re4
    out_ref[1] = re0 - re4
    out_ref[2] = re1 + re7
    out_ref[3] = im1 - im7


def rows_inverse_last(*refs):
    y_refs, (first_ref, high_ref, low_ref, twist_ref, x_ref) = refs[:-5], refs[-5:]
    (re2, im2), (re6, im6), (re3, im3), (re5, im5) = [
        untwist(y_refs, spot, k, high_ref, low_ref, twist_ref) for spot, k in enumerate(HALVES[1])
    ]
    even, odd, r1, i1 = [first_ref[i] for i in range(4)]
    r2, r3, i2, i3 = re2 + re6, re3 + re5, im2 - im6, im3 - im5
    rm, ip = (r1 - r3) * ROOT, (i1 + i3) * ROOT
    x_ref[0] = (even + r2 + (r1 + r3)).astype(BF16)
    x_ref[4] = (even + r2 - (r1 + r3)).astype(BF16)
    x_ref[2] = (even - r2 - (i1 - i3)).astype(BF16)
    x_ref[6] = (even - r2 + (i1 - i3)).astype(BF16)
    x_ref[1] = (odd + rm - ip - i2).astype(BF16)
    x_ref[7] = (odd + rm + ip + i2).astype(BF16)
    x_ref[3] = (odd - rm - ip + i2).astype(BF16)
    x_ref[5] = (odd - rm + ip - i2).astype(BF16)


HALO = 8
LANES = 128


def step_kernel(image_ref, grad_ref, spread_ref, out_ref, first_ref, last_ref):
    _, width = image_ref.shape
    grad = jnp.concatenate([grad_ref[i] for i in range(grad_ref.shape[0])], 1)
    out_ref[...] = image_ref[...] - jnp.dot(grad, spread_ref[...], preferred_element_type=F32)
    first_ref[...] = out_ref[:, :LANES].T[:HALO]
    last_ref[...] = out_ref[:, width - LANES :].T[LANES - HALO :]


def haar_kernel(field_ref, left_ref, right_ref, limit_ref, out_ref, *, bases):
    rows, width = field_ref.shape
    span = width + LANES
    middle = jnp.zeros((LANES - 2 * HALO, rows), F32)
    edge = jnp.concatenate([right_ref[...], middle, left_ref[...]], 0).T
    even = lax.broadcasted_iota(jnp.int32, (rows, span), 0) % 2 == 0

    def mix(x, even):
        other = jnp.where(even, pltpu.roll(x, rows - 1, 0), pltpu.roll(x, 1, 0))
        return jnp.where(even, x, -x) + other

    def ahead(x, by):
        return pltpu.roll(x, span - by, 1)

    def behind(x, by):
        return pltpu.roll(x, by, 1)

    def mean(u):
        spot = 0
        level = []
        for period in (2, 4, 8):
            forward = ahead(u, period // 2)
            parts = [u + forward, u - forward]
            limits = []
            for _ in range(0, bases, period):
                limits.append(limit_ref[spot : spot + 1, :])
                spot += 1
            limited = []
            for x in parts if period == 8 else parts[1:]:
                total = None
                for limit in limits:
                    x_soft = x - jnp.minimum(jnp.maximum(x, -limit), limit)
                    total = x_soft if total is None else total + x_soft
                limited.append(total)
            level.append(limited)
            u = parts[0]
        s3, d3 = level[2]
        back = (s3 + d3) + behind(s3 - d3, 4)
        for by, (d,) in ((2, level[1]), (1, level[0])):
            back = back * 0.5
            back = (back + d) + behind(back - d, by)
        return back[:, :width] * (0.25 / bases)

    field = jnp.concatenate([field_ref[...], edge], 1)
    out_ref[...] = mix(mean(mix(field, even)), even[:, :width])


def haar_limits(width, thresholds):
    bases = thresholds.shape[0]
    span = width + LANES
    place = iota(span)
    place = jnp.where(place < width + LANES // 2, place, place - span) + 8
    out = []
    for period in (2, 4, 8):
        scale = math.sqrt(2.0 * period)
        for start in range(0, bases, period):
            index = place % period + start
            limit = jnp.full((span,), 3e38, F32)
            for s in range(start, min(start + period, bases)):
                limit = jnp.where(index == s, thresholds[s] * scale, limit)
            out.append(limit)
    return jnp.stack(out)


def haar_mean(field, halo_left, halo_right, thresholds):
    bases = thresholds.shape[0]
    rows, width = field.shape
    limits = haar_limits(width, thresholds)
    step = LANES
    return pl.pallas_call(
        lambda *refs: haar_kernel(*refs, bases=bases),
        grid=(rows // step,),
        in_specs=[
            pl.BlockSpec((step, width), lambda i: (i, 0)),
            pl.BlockSpec((HALO, step), lambda i: (0, i)),
            pl.BlockSpec((HALO, step), lambda i: (0, i)),
            pl.BlockSpec(limits.shape, lambda i: (0, 0)),
        ],
        out_specs=pl.BlockSpec((step, width), lambda i: (i, 0)),
        out_shape=jax.ShapeDtypeStruct((rows, width), F32),
        compiler_params=pltpu.CompilerParams(vmem_limit_bytes=VMEM_LIMIT),
        name="haar",
    )(field, halo_left, halo_right, limits)


def phases(owner, a_block, v, rows, img):
    cos_k, sin_k = turns(v, owner[:, None] * rows + a_block[:, None] * PATCH + iota(PATCH)[None, :], img)
    return jnp.concatenate([cos_k, cos_k], 1), jnp.concatenate([sin_k, -sin_k], 1)


def shards_fast(image, kernel_v, kernel_u, measured, dest_owner, patch_slot, thresholds):
    vis = lax.axis_size("vis")
    wavs = lax.axis_size("wav")
    v, w = lax.axis_index("vis"), lax.axis_index("wav")
    rows, cols = image.shape
    img = rows * vis
    m = cols // vis
    across = cols // PATCH
    blocks = kernel_v.shape[0]
    part = rows // wavs

    def flip(x, mask):
        return lax.ppermute(x, "vis", [(i, i ^ mask) for i in range(vis)])

    def ahead(x, by):
        return lax.ppermute(x, "wav", [(i, (i + by) % wavs) for i in range(wavs)])

    def exchange(parts):
        out = [parts[0]]
        for s in range(1, wavs):
            out.append(ahead(parts[wavs - s], wavs - s))
        return out

    def to_chips(parts):
        out = []
        for chip in (1, 2, 3):
            out.append(flip(parts[chip - 1], 2 * chip))
        return out

    x = jnp.dot(image, spread_matrix(vis, m), precision=HIGH).astype(F16)
    x = x.reshape(rows, vis, m).transpose(1, 0, 2)
    x = lax.all_to_all(x, "vis", split_axis=0, concat_axis=0, tiled=True).astype(F32)

    ids = jnp.stack([dest_owner[:, 0], patch_slot])
    for mask in (1, 2, 4):
        ids = jnp.concatenate([ids, flip(ids, mask)], 1)
    owner, slot = ids[0], ids[1]
    a_block, b_block = slot // across, slot % across
    cos_k, sin_k = phases(owner, a_block, v, rows, img)

    forward_table, twist = row_table(rows, w * part), twist_table(vis, rows)
    sent, spectra = [], []
    for half in (0, 1):
        y = rows_forward_fast(x, wavs, forward_table, twist, half)
        sent.append([part_y.astype(F16) for part_y in y])
        spectra.append(exchange(sent[half]))
    spectra[0], _ = lax.optimization_barrier((spectra[0], sent[1]))

    table = column_table(wavs, m, w, False)
    patches = []
    for half in (0, 1):
        y = [part_y.astype(F32) for part_y in spectra[half]]
        far, near = shares_fast(a_block, b_block, y, table, cos_k, sin_k)
        near = near + flip(far.astype(F16), 1).astype(F32)
        ready = [near[0]] + [near[chip].astype(F16) for chip in (1, 2, 3)]
        if half == 0:
            spectra[1], ready = lax.optimization_barrier((spectra[1], ready))
        total = ready[0]
        for came in to_chips(ready[1:]):
            total = total + came.astype(F32)
        patches.append(total.astype(BF16))

    order = jnp.asarray(ORDER)
    side = kernel_u.reshape(blocks, 8, vis, -1)[:, :, order].transpose(0, 2, 1, 3).reshape(kernel_u.shape).astype(F32)
    sides = [side[:, : PATCH // 2], side[:, PATCH // 2 :]]
    model = 0.0
    for patch, side in zip(patches, sides):
        part_re = jnp.einsum("nba,nat->nbt", patch[..., :PATCH], kernel_v, preferred_element_type=F32)
        part_im = jnp.einsum("nba,nat->nbt", patch[..., PATCH:], kernel_v, preferred_element_type=F32)
        model = model + jnp.stack([jnp.sum(part_re * side, 1), jnp.sum(part_im * side, 1)], 1)
    misfit = model - measured.astype(F32)

    table_back = column_table(wavs, m, w, True)
    grads = []
    for half, side in enumerate(sides):
        w_re = (misfit[:, 0, None, :] * side).astype(BF16)
        w_im = (misfit[:, 1, None, :] * side).astype(BF16)
        term_re = jnp.einsum("nbt,nat->nba", w_re, kernel_v, preferred_element_type=F32)
        term_im = jnp.einsum("nbt,nat->nba", w_im, kernel_v, preferred_element_type=F32)
        terms = jnp.concatenate([term_re, term_im], -1).astype(BF16)
        if half == 1:
            terms, chips = lax.optimization_barrier((terms, chips))
        chips = [terms] + to_chips([terms] * 3)
        other = flip(jnp.stack(chips), 1)
        grad = gather_fast(a_block, b_block, chips + [other], table_back, cos_k, sin_k, wavs, part, m)
        grads.append(exchange(grad))

    back_table = row_table_back(rows, w * part)
    shape = (4, rows, m)
    first = call(rows_inverse_first, [(shape, F32)], [], *grads[0], *back_table, twist)
    grad = call(rows_inverse_last, [((vis, rows, m), BF16)], [], *grads[1], *first, *back_table, twist)[0]
    grad = lax.all_to_all(grad, "vis", split_axis=0, concat_axis=0, tiled=True)
    edge = ((HALO, rows), F32)
    back = spread_matrix(vis, m).T.astype(BF16)
    shifted, first_cols, last_cols = call(step_kernel, [((rows, cols), F32), edge, edge], [], image, grad, back)
    right = ahead(first_cols, wavs - 1)
    left = ahead(last_cols, 1)
    return haar_mean(shifted, left, right, thresholds), misfit


def shards(image, kernel_v, kernel_u, measured, dest_owner, patch_slot, thresholds):
    vis = lax.axis_size("vis")
    wavs = lax.axis_size("wav")
    v = lax.axis_index("vis")
    rows, cols = image.shape
    img = rows * vis
    m = cols // vis
    down = rows // PATCH
    across = cols // PATCH
    blocks = kernel_v.shape[0]
    low = PATCH // vis
    part = rows // wavs
    if vis == 8 and m == LANES and low == 8 and part % 8 == 0 and rows & (rows - 1) == 0:
        return shards_fast(image, kernel_v, kernel_u, measured, dest_owner, patch_slot, thresholds)
    spread = spread_matrix(vis, m)

    ids = jnp.concatenate([dest_owner, patch_slot[:, None]], 1)
    ids = lax.all_gather(ids, "vis", axis=0, tiled=True)
    owner, slot = ids[:, 0], ids[:, 1]
    a_block, b_block = slot // across, slot % across

    x = jnp.dot(image, spread, precision=HIGH).astype(F16)
    x = x.reshape(rows, vis, m).transpose(1, 0, 2)
    x = lax.all_to_all(x, "vis", split_axis=0, concat_axis=0, tiled=True).astype(F32)
    y = rows_forward(x, vis).astype(F16)
    y = y.reshape(vis, wavs, part, 2 * m).transpose(1, 0, 2, 3)
    y = lax.all_to_all(y, "wav", split_axis=0, concat_axis=0, tiled=True).astype(F32)
    cos_k, sin_k = turns(v, owner[:, None] * rows + a_block[:, None] * PATCH + iota(PATCH)[None, :], img)
    cos_k = jnp.concatenate([cos_k, cos_k], 1)
    sin_k = jnp.concatenate([sin_k, -sin_k], 1)
    y = y.transpose(1, 2, 0, 3).reshape(cols, 2 * wavs * m)
    table = column_matrix(wavs, m, down, 1.0 / img)
    z = jnp.dot(y, table, precision=HIGH)
    z = z.reshape(vis, across, low, down, 2 * PATCH)
    tiles = z[:, b_block, :, a_block, :].reshape(vis * blocks, PATCH, 2 * PATCH)
    tiles = tiles * cos_k[:, None] + jnp.roll(tiles, PATCH, axis=2) * sin_k[:, None]
    tiles = lax.all_to_all(tiles.astype(F16), "vis", split_axis=0, concat_axis=0, tiled=True)
    patch = jnp.sum(tiles.reshape(vis, blocks, PATCH, 2 * PATCH).astype(F32), 0).astype(BF16)

    side_u = kernel_u.reshape(blocks, low, vis, -1).transpose(0, 2, 1, 3).reshape(kernel_u.shape)
    part_re = jnp.einsum("nba,nat->nbt", patch[..., :PATCH], kernel_v, preferred_element_type=F32)
    part_im = jnp.einsum("nba,nat->nbt", patch[..., PATCH:], kernel_v, preferred_element_type=F32)
    side = side_u.astype(F32)
    misfit = jnp.stack([jnp.sum(part_re * side, 1), jnp.sum(part_im * side, 1)], 1) - measured.astype(F32)
    w_re = (misfit[:, 0, None, :] * side).astype(BF16)
    w_im = (misfit[:, 1, None, :] * side).astype(BF16)
    term_re = jnp.einsum("nbt,nat->nba", w_re, kernel_v, preferred_element_type=F32)
    term_im = jnp.einsum("nbt,nat->nba", w_im, kernel_v, preferred_element_type=F32)
    terms = jnp.concatenate([term_re, term_im], -1).astype(BF16)

    terms = lax.all_gather(terms, "vis", axis=0, tiled=True)
    terms = terms.astype(F32)
    terms = terms * cos_k[:, None] - jnp.roll(terms, PATCH, axis=2) * sin_k[:, None]
    terms = terms.reshape(vis * blocks, vis, low, 2 * PATCH)
    flat = jnp.zeros((across * down, vis, low, 2 * PATCH), F32).at[b_block * down + a_block].add(terms)
    grad = flat.reshape(across, down, vis, low, 2 * PATCH).transpose(2, 0, 3, 1, 4).reshape(cols, 2 * rows)
    grad = lax.dot_general(grad, table, (((1,), (1,)), ((), ())), precision=HIGH).astype(BF16)
    grad = grad.reshape(vis, part, wavs, 2 * m).transpose(2, 0, 1, 3)
    grad = lax.all_to_all(grad, "wav", split_axis=0, concat_axis=0, tiled=True)
    grad = grad.astype(F32).transpose(1, 0, 2, 3).reshape(vis, rows, 2 * m)
    grad = rows_inverse(grad, vis).astype(BF16)
    grad = lax.all_to_all(grad, "vis", split_axis=0, concat_axis=0, tiled=True)
    grad = grad.transpose(1, 0, 2).reshape(rows, cols)
    grad = lax.dot_general(grad, spread.astype(BF16), (((1,), (1,)), ((), ())), preferred_element_type=F32)
    shifted = image - grad
    right = lax.ppermute(shifted[:, :HALO].T, "wav", [(i, (i - 1) % wavs) for i in range(wavs)])
    left = lax.ppermute(shifted[:, -HALO:].T, "wav", [(i, (i + 1) % wavs) for i in range(wavs)])
    return haar_mean(shifted, left, right, thresholds), misfit


def solution(mesh):
    both = ("vis", "wav")
    in_specs = (
        P("vis", "wav"),
        P(both, None, None),
        P(both, None, None),
        P(both, None, None),
        P(both, None),
        P(both),
        P(),
    )
    out_specs = (P("vis", "wav"), P(both, None, None))
    return jax.shard_map(shards, mesh=mesh, in_specs=in_specs, out_specs=out_specs, check_vma=False)
```

```python
import math

import jax
import jax.numpy as jnp
import numpy as np
from jax import lax
from jax.experimental import pallas as pl
from jax.experimental.pallas import tpu as pltpu
from jax.sharding import PartitionSpec as P


PATCH = 64
HIGH = lax.Precision.HIGH
F32 = jnp.float32
BF16 = jnp.bfloat16
F16 = jnp.float16


def turns(rows, cols, period):
    angle = (rows * cols % period).astype(F32) * (2.0 * math.pi / period)
    return jnp.cos(angle), jnp.sin(angle)


def iota(size):
    return jnp.arange(size, dtype=jnp.int32)


def spread_matrix(groups, size):
    width = groups * size
    c = iota(width)
    return (c[:, None] == (c % size * groups + c // size)[None, :]).astype(F32)


def rows_forward(x, groups):
    rows = x.shape[1]
    count = groups * rows
    cos_g, sin_g = (np.cos(2 * np.pi * np.outer(np.arange(groups), np.arange(groups)) / groups), np.sin(2 * np.pi * np.outer(np.arange(groups), np.arange(groups)) / groups))
    mixed_re = jnp.einsum("kv,vnm->knm", jnp.asarray(cos_g, F32), x, precision=HIGH)
    mixed_im = -jnp.einsum("kv,vnm->knm", jnp.asarray(sin_g, F32), x, precision=HIGH)
    cos_t, sin_t = turns(iota(groups)[:, None], iota(rows)[None, :], count)
    cos_t, sin_t = cos_t[:, :, None], sin_t[:, :, None]
    both = jnp.concatenate([mixed_re * cos_t + mixed_im * sin_t, mixed_im * cos_t - mixed_re * sin_t], -1)
    cos_r, sin_r = turns(iota(rows)[:, None], iota(rows)[None, :], rows)
    p = jnp.einsum("kn,vnm->vkm", cos_r, both, precision=HIGH)
    q = jnp.einsum("kn,vnm->vkm", sin_r, both, precision=HIGH)
    m = x.shape[2]
    return jnp.concatenate([p[..., :m] + q[..., m:], p[..., m:] - q[..., :m]], -1)


def rows_inverse(y, groups):
    rows = y.shape[1]
    m = y.shape[2] // 2
    count = groups * rows
    cos_r, sin_r = turns(iota(rows)[:, None], iota(rows)[None, :], rows)
    p = jnp.einsum("kn,vnm->vkm", cos_r, y, precision=HIGH)
    q = jnp.einsum("kn,vnm->vkm", sin_r, y, precision=HIGH)
    re, im = p[..., :m] - q[..., m:], p[..., m:] + q[..., :m]
    cos_t, sin_t = turns(iota(groups)[:, None], iota(rows)[None, :], count)
    cos_t, sin_t = cos_t[:, :, None], sin_t[:, :, None]
    re, im = re * cos_t - im * sin_t, im * cos_t + re * sin_t
    cos_g, sin_g = (np.cos(2 * np.pi * np.outer(np.arange(groups), np.arange(groups)) / groups), np.sin(2 * np.pi * np.outer(np.arange(groups), np.arange(groups)) / groups))
    out = jnp.einsum("vk,knm->vnm", jnp.asarray(cos_g, F32), re, precision=HIGH)
    return out - jnp.einsum("vk,knm->vnm", jnp.asarray(sin_g, F32), im, precision=HIGH)


def column_matrix(wavs, m, down, scale):
    size = wavs * m
    cos_c, sin_c = turns(iota(size)[:, None], iota(size)[None, :], size)
    cos_c = (cos_c * scale).reshape(wavs, 1, m, down, 1, PATCH)
    sin_c = (sin_c * scale).reshape(wavs, 1, m, down, 1, PATCH)
    from_re = jnp.concatenate([cos_c, -sin_c], 4)
    from_im = jnp.concatenate([sin_c, cos_c], 4)
    return jnp.concatenate([from_re, from_im], 1).reshape(2 * size, 2 * size)


def split(x):
    high = lax.reduce_precision(x, 8, 7)
    return high.astype(BF16), (x - high).astype(BF16)


def bits(size):
    return size.bit_length() - 1


def cosine(count, period):
    part = (count & (period - 1)).astype(F32) * (1.0 / period)
    part = 0.25 - jnp.abs(part - jnp.where(part > 0.5, 1.0, 0.0))
    square = part * part
    terms = [(-1) ** i * (2 * math.pi) ** (2 * i + 1) / math.factorial(2 * i + 1) for i in range(7)]
    value = jnp.full_like(part, terms[-1])
    for term in terms[-2::-1]:
        value = value * square + term
    return value * part


def grid_of(shape):
    return [lax.broadcasted_iota(jnp.int32, shape, axis) for axis in (0, 1)]


def row_table(size, first):
    k, n = grid_of((2 * size, size))
    return split(cosine(((k + first) & (size - 1)) * n - (k >> bits(size)) * (size // 4), size))


def row_table_back(size, first):
    r, k = grid_of((2 * size, size))
    return split(cosine(((k + first) & (size - 1)) * (r & (size - 1)) - (r >> bits(size)) * (size // 4), size))


def column_table(wavs, m, first, turned):
    size = wavs * m
    row, col = grid_of((2 * size, 2 * size))[:: -1 if turned else 1]
    n = (row >> bits(2 * m)) * m + (row & (m - 1)) + first * m
    k = (col >> bits(2 * PATCH)) * PATCH + (col & (PATCH - 1))
    quarter = (col >> bits(PATCH) & 1) - (row >> bits(m) & 1)
    return split(cosine((n & (size - 1)) * k + quarter * (size // 4), size))


def twist_table(groups, rows):
    n, k = grid_of((rows, 2 * groups))
    count = groups * rows
    return cosine(n * (k & (groups - 1)) - (k >> bits(groups)) * (count // 4), count)


def in_vmem(count):
    return [pl.BlockSpec(memory_space=pltpu.VMEM)] * count


VMEM_LIMIT = 24 * 1024 * 1024
ROOT = math.sqrt(0.5)


AT_ONCE = 8
HALVES = ((0, 1, 7, 2, 6), (4, 3, 5))
ORDER = HALVES[0] + HALVES[1]


def call(kernel, out_shapes, scratch, *args, smem=0):
    return pl.pallas_call(
        kernel,
        in_specs=[pl.BlockSpec(memory_space=pltpu.SMEM)] * smem + in_vmem(len(args) - smem),
        out_specs=in_vmem(len(out_shapes)),
        out_shape=[jax.ShapeDtypeStruct(shape, kind) for shape, kind in out_shapes],
        scratch_shapes=[pltpu.VMEM(shape, kind) for shape, kind in scratch],
        compiler_params=pltpu.CompilerParams(vmem_limit_bytes=VMEM_LIMIT),
    )(*args)


def rows_forward_kernel(x_ref, high_ref, low_ref, twist_ref, *y_refs, half):
    rows, m = x_ref.shape[1:]
    wavs = len(y_refs)
    part = rows // wavs
    x = [x_ref[i].astype(F32) for i in range(8)]
    e0, e1, f0, f1 = x[0] + x[4], x[0] - x[4], x[2] + x[6], x[2] - x[6]
    g0, g1, h0, h1 = x[1] + x[5], x[1] - x[5], x[3] + x[7], x[3] - x[7]
    gm, gp = (g1 - h1) * ROOT, (g1 + h1) * ROOT
    zero = jnp.zeros_like(e0)
    mixed = {
        0: (e0 + f0 + g0 + h0, zero),
        1: (e1 + gm, -f1 - gp),
        2: (e0 - f0, h0 - g0),
        3: (e1 - gm, f1 - gp),
        4: (e0 + f0 - g0 - h0, zero),
    }
    for spot, k in enumerate(HALVES[half]):
        if k > 4:
            continue
        re, im = mixed[k]
        if k:
            cos_t, sin_t = twist_ref[:, k : k + 1], twist_ref[:, 8 + k : 9 + k]
            re, im = re * cos_t + im * sin_t, im * cos_t - re * sin_t
        both = jnp.concatenate([re, im], 1)
        high = both.astype(BF16)
        low = (both - high.astype(F32)).astype(BF16)
        out = jnp.dot(high_ref[...], high, preferred_element_type=F32)
        out += jnp.dot(high_ref[...], low, preferred_element_type=F32)
        out += jnp.dot(low_ref[...], high, preferred_element_type=F32)
        p_re, p_im, q_re, q_im = out[:rows, :m], out[:rows, m:], out[rows:, :m], out[rows:, m:]
        here = jnp.concatenate([p_re + q_im, p_im - q_re], 1)
        for w in range(wavs):
            y_refs[w][spot] = here[w * part : (w + 1) * part]
        if k in (1, 2, 3):
            there = jnp.concatenate([p_re - q_im, -p_im - q_re], 1)
            there = pltpu.roll(there, rows - 1, 0)
            for w in range(wavs):
                y_refs[w][spot + 1] = there[w * part : (w + 1) * part]


def rows_forward_fast(x, wavs, table, twist, half):
    _, rows, m = x.shape
    kernel = lambda *refs: rows_forward_kernel(*refs, half=half)
    return call(kernel, [((len(HALVES[half]), rows // wavs, 2 * m), F32)] * wavs, [], x, *table, twist)


def shares_kernel(a_ref, b_ref, *refs, wavs):
    y_refs = refs[:wavs]
    high_ref, low_ref, cos_ref, sin_ref, far_ref, near_ref, z_ref, head_ref, rest_ref = refs[wavs:]
    groups, part, double = y_refs[0].shape
    down = z_ref.shape[0]
    wide = 2 * PATCH
    low = 8
    blocks = near_ref.shape[1]
    scale = 1.0 / (8 * down * PATCH)
    for w in range(wavs):
        y = y_refs[w][...].astype(F32).reshape(groups * part, double)
        high = y.astype(BF16)
        head_ref[:, w * double : (w + 1) * double] = high
        rest_ref[:, w * double : (w + 1) * double] = (y - high.astype(F32)).astype(BF16)
    for a in range(0, down, 2):
        spot = (slice(None), pl.ds(a * wide, 2 * wide))
        z = jnp.dot(head_ref[...], high_ref[spot], preferred_element_type=F32)
        z += jnp.dot(rest_ref[...], high_ref[spot], preferred_element_type=F32)
        z += jnp.dot(head_ref[...], low_ref[spot], preferred_element_type=F32)
        z = z * scale
        z_ref[a] = z[:, :wide].reshape(groups, part, wide)
        z_ref[a + 1] = z[:, wide:].reshape(groups, part, wide)
    for mask in (1, 3, 5, 7, 0, 2, 4, 6):
        out_ref = far_ref if mask % 2 else near_ref

        @pl.loop(0, blocks // AT_ONCE)
        def _(step):
            for i in range(AT_ONCE):
                at = step * AT_ONCE + i
                n = mask * blocks + at
                start = pl.multiple_of(b_ref[n] * low, low)
                tile = z_ref[a_ref[n], :, pl.ds(start, low), :].reshape(groups * low, wide)
                out_ref[mask // 2, at] = tile * cos_ref[pl.ds(n, 1), :] + pltpu.roll(tile, PATCH, 1) * sin_ref[pl.ds(n, 1), :]


def shares_fast(a_block, b_block, ys, table, cos_k, sin_k):
    groups, part, double = ys[0].shape
    wavs = len(ys)
    width = wavs * double
    blocks = a_block.shape[0] // 8
    out = ((4, blocks, groups * 8, 2 * PATCH), F32)
    scratch = [((width // (2 * PATCH), groups, part, 2 * PATCH), F32)] + [((groups * part, width), BF16)] * 2
    kernel = lambda *refs: shares_kernel(*refs, wavs=wavs)
    return call(kernel, [out, out], scratch, a_block, b_block, *ys, *table, cos_k, sin_k, smem=2)


def gather_kernel(a_ref, b_ref, *refs):
    term_refs = [ref for chip in range(4) for ref in (refs[chip], refs[4].at[chip])]
    high_ref, low_ref, cos_ref, sin_ref = refs[5:9]
    y_refs, (g_ref, head_ref) = refs[9:-2], refs[-2:]
    groups, part, double = y_refs[0].shape
    down = g_ref.shape[0]
    wide = 2 * PATCH
    low = 8
    blocks = term_refs[0].shape[0]
    g_ref[...] = jnp.zeros_like(g_ref)
    for mask in range(8):

        @pl.loop(0, blocks // AT_ONCE)
        def _(step):
            tiles = []
            for i in range(AT_ONCE):
                at = step * AT_ONCE + i
                n = mask * blocks + at
                tile = term_refs[mask][at].astype(F32)
                tiles.append(tile * cos_ref[pl.ds(n, 1), :] - pltpu.roll(tile, PATCH, 1) * sin_ref[pl.ds(n, 1), :])
            for i in range(AT_ONCE):
                n = mask * blocks + step * AT_ONCE + i
                start = pl.multiple_of(b_ref[n] * low, low)
                g_ref[a_ref[n], :, pl.ds(start, low), :] += tiles[i].reshape(groups, low, wide)

    for a in range(down):
        head_ref[:, a * wide : (a + 1) * wide] = g_ref[a].reshape(groups * part, wide).astype(BF16)
    scale = 1.0 / (8 * down * PATCH)
    for w, y_ref in enumerate(y_refs):
        spot = (slice(None), pl.ds(w * double, double))
        y = jnp.dot(head_ref[...], high_ref[spot], preferred_element_type=F32)
        y += jnp.dot(head_ref[...], low_ref[spot], preferred_element_type=F32)
        y_ref[...] = (y * scale).astype(BF16).reshape(groups, part, double)


def gather_fast(a_block, b_block, terms, table, cos_k, sin_k, wavs, part, m, half):
    width = 2 * wavs * m
    groups = len(HALVES[half])
    out = [((groups, part, 2 * m), BF16)] * wavs
    scratch = [((width // (2 * PATCH), groups, part, 2 * PATCH), F32), ((groups * part, width), BF16)]
    return call(gather_kernel, out, scratch, a_block, b_block, *terms, *table, cos_k, sin_k, smem=2)


def untwist(y_refs, spot, k, high_ref, low_ref, twist_ref):
    y = jnp.concatenate([ref[spot] for ref in y_refs], 0)
    rows, m = y.shape[0], y.shape[1] // 2
    out = jnp.dot(high_ref[...], y, preferred_element_type=F32)
    out += jnp.dot(low_ref[...], y, preferred_element_type=F32)
    re, im = out[:rows, :m] - out[rows:, m:], out[:rows, m:] + out[rows:, :m]
    if k:
        cos_t, sin_t = twist_ref[:, k : k + 1], twist_ref[:, 8 + k : 9 + k]
        re, im = re * cos_t - im * sin_t, im * cos_t + re * sin_t
    return re, im


def rows_inverse_first(*refs):
    y_refs, (high_ref, low_ref, twist_ref, out_ref) = refs[:-4], refs[-4:]
    (re4, _), (re3, im3), (re5, im5) = [
        untwist(y_refs, spot, k, high_ref, low_ref, twist_ref) for spot, k in enumerate(HALVES[1])
    ]
    out_ref[0] = re4
    out_ref[1] = re3 + re5
    out_ref[2] = im3 - im5


def rows_inverse_last(*refs):
    y_refs, (first_ref, high_ref, low_ref, twist_ref, x_ref) = refs[:-5], refs[-5:]
    (re0, _), (re1, im1), (re7, im7), (re2, im2), (re6, im6) = [
        untwist(y_refs, spot, k, high_ref, low_ref, twist_ref) for spot, k in enumerate(HALVES[0])
    ]
    re4, r3, i3 = [first_ref[i] for i in range(3)]
    even, odd = re0 + re4, re0 - re4
    r1, r2, i1, i2 = re1 + re7, re2 + re6, im1 - im7, im2 - im6
    rm, ip = (r1 - r3) * ROOT, (i1 + i3) * ROOT
    x_ref[0] = (even + r2 + (r1 + r3)).astype(BF16)
    x_ref[4] = (even + r2 - (r1 + r3)).astype(BF16)
    x_ref[2] = (even - r2 - (i1 - i3)).astype(BF16)
    x_ref[6] = (even - r2 + (i1 - i3)).astype(BF16)
    x_ref[1] = (odd + rm - ip - i2).astype(BF16)
    x_ref[7] = (odd + rm + ip + i2).astype(BF16)
    x_ref[3] = (odd - rm - ip + i2).astype(BF16)
    x_ref[5] = (odd - rm + ip - i2).astype(BF16)


HALO = 8
LANES = 128


def step_kernel(image_ref, grad_ref, spread_ref, out_ref, first_ref, last_ref):
    _, width = image_ref.shape
    grad = jnp.concatenate([grad_ref[i] for i in range(grad_ref.shape[0])], 1)
    out_ref[...] = image_ref[...] - jnp.dot(grad, spread_ref[...], preferred_element_type=F32)
    first_ref[...] = out_ref[:, :LANES].T[:HALO]
    last_ref[...] = out_ref[:, width - LANES :].T[LANES - HALO :]


def haar_kernel(field_ref, left_ref, right_ref, limit_ref, out_ref, *, bases):
    rows, width = field_ref.shape
    span = width + LANES
    middle = jnp.zeros((LANES - 2 * HALO, rows), F32)
    edge = jnp.concatenate([right_ref[...], middle, left_ref[...]], 0).T
    even = lax.broadcasted_iota(jnp.int32, (rows, span), 0) % 2 == 0

    def mix(x, even):
        other = jnp.where(even, pltpu.roll(x, rows - 1, 0), pltpu.roll(x, 1, 0))
        return jnp.where(even, x, -x) + other

    def ahead(x, by):
        return pltpu.roll(x, span - by, 1)

    def behind(x, by):
        return pltpu.roll(x, by, 1)

    def mean(u):
        spot = 0
        level = []
        for period in (2, 4, 8):
            forward = ahead(u, period // 2)
            parts = [u + forward, u - forward]
            limits = []
            for _ in range(0, bases, period):
                limits.append(limit_ref[spot : spot + 1, :])
                spot += 1
            limited = []
            for x in parts if period == 8 else parts[1:]:
                total = None
                for limit in limits:
                    x_soft = x - jnp.minimum(jnp.maximum(x, -limit), limit)
                    total = x_soft if total is None else total + x_soft
                limited.append(total)
            level.append(limited)
            u = parts[0]
        s3, d3 = level[2]
        back = (s3 + d3) + behind(s3 - d3, 4)
        for by, (d,) in ((2, level[1]), (1, level[0])):
            back = back * 0.5
            back = (back + d) + behind(back - d, by)
        return back[:, :width] * (0.25 / bases)

    field = jnp.concatenate([field_ref[...], edge], 1)
    out_ref[...] = mix(mean(mix(field, even)), even[:, :width])


def haar_limits(width, thresholds):
    bases = thresholds.shape[0]
    span = width + LANES
    place = iota(span)
    place = jnp.where(place < width + LANES // 2, place, place - span) + 8
    out = []
    for period in (2, 4, 8):
        scale = math.sqrt(2.0 * period)
        for start in range(0, bases, period):
            index = place % period + start
            limit = jnp.full((span,), 3e38, F32)
            for s in range(start, min(start + period, bases)):
                limit = jnp.where(index == s, thresholds[s] * scale, limit)
            out.append(limit)
    return jnp.stack(out)


def haar_mean(field, halo_left, halo_right, thresholds):
    bases = thresholds.shape[0]
    rows, width = field.shape
    limits = haar_limits(width, thresholds)
    step = LANES
    return pl.pallas_call(
        lambda *refs: haar_kernel(*refs, bases=bases),
        grid=(rows // step,),
        in_specs=[
            pl.BlockSpec((step, width), lambda i: (i, 0)),
            pl.BlockSpec((HALO, step), lambda i: (0, i)),
            pl.BlockSpec((HALO, step), lambda i: (0, i)),
            pl.BlockSpec(limits.shape, lambda i: (0, 0)),
        ],
        out_specs=pl.BlockSpec((step, width), lambda i: (i, 0)),
        out_shape=jax.ShapeDtypeStruct((rows, width), F32),
        compiler_params=pltpu.CompilerParams(vmem_limit_bytes=VMEM_LIMIT),
        name="haar",
    )(field, halo_left, halo_right, limits)


def phases(owner, a_block, v, rows, img):
    cos_k, sin_k = turns(v, owner[:, None] * rows + a_block[:, None] * PATCH + iota(PATCH)[None, :], img)
    return jnp.concatenate([cos_k, cos_k], 1), jnp.concatenate([sin_k, -sin_k], 1)


def shards_fast(image, kernel_v, kernel_u, measured, dest_owner, patch_slot, thresholds):
    vis = lax.axis_size("vis")
    wavs = lax.axis_size("wav")
    v, w = lax.axis_index("vis"), lax.axis_index("wav")
    rows, cols = image.shape
    img = rows * vis
    m = cols // vis
    across = cols // PATCH
    blocks = kernel_v.shape[0]
    part = rows // wavs

    def flip(x, mask):
        return lax.ppermute(x, "vis", [(i, i ^ mask) for i in range(vis)])

    def ahead(x, by):
        return lax.ppermute(x, "wav", [(i, (i + by) % wavs) for i in range(wavs)])

    def exchange(parts):
        out = [parts[0]]
        for s in range(1, wavs):
            out.append(ahead(parts[wavs - s], wavs - s))
        return out

    def to_chips(parts):
        out = []
        for chip in (1, 2, 3):
            out.append(flip(parts[chip - 1], 2 * chip))
        return out

    x = jnp.dot(image, spread_matrix(vis, m), precision=HIGH).astype(F16)
    x = x.reshape(rows, vis, m).transpose(1, 0, 2)
    x = lax.all_to_all(x, "vis", split_axis=0, concat_axis=0, tiled=True).astype(F32)

    forward_table, twist = row_table(rows, w * part), twist_table(vis, rows)
    sent, spectra = [], []
    for half in (0, 1):
        y = rows_forward_fast(x, wavs, forward_table, twist, half)
        sent.append([part_y.astype(F16) for part_y in y])
        spectra.append(exchange(sent[half]))
    spectra[0], _ = lax.optimization_barrier((spectra[0], sent[1]))

    ids = jnp.stack([dest_owner[:, 0], patch_slot])
    ids, _ = lax.optimization_barrier((ids, sent[1]))
    for mask in (1, 2, 4):
        ids = jnp.concatenate([ids, flip(ids, mask)], 1)
    owner, slot = ids[0], ids[1]
    a_block, b_block = slot // across, slot % across
    cos_k, sin_k = phases(owner, a_block, v, rows, img)

    table = column_table(wavs, m, w, False)
    patches = []
    for half in (0, 1):
        y = []
        for part_y in spectra[half]:
            y.append(part_y.astype(F32))
        far, near = shares_fast(a_block, b_block, y, table, cos_k, sin_k)
        near = near + flip(far.astype(F16), 1).astype(F32)
        ready = [near[0]] + [near[chip].astype(F16) for chip in (1, 2, 3)]
        if half == 0:
            spectra[1], ready = lax.optimization_barrier((spectra[1], ready))
        total = ready[0]
        for came in to_chips(ready[1:]):
            total = total + came.astype(F32)
        patches.append(total.astype(BF16))

    order = jnp.asarray(ORDER)
    side = kernel_u.reshape(blocks, 8, vis, -1)[:, :, order].transpose(0, 2, 1, 3).reshape(kernel_u.shape).astype(F32)
    cut = 8 * len(HALVES[0])
    sides = [side[:, :cut], side[:, cut:]]
    model = 0.0
    for patch, side in zip(patches, sides):
        part_re = jnp.einsum("nba,nat->nbt", patch[..., :PATCH], kernel_v, preferred_element_type=F32)
        part_im = jnp.einsum("nba,nat->nbt", patch[..., PATCH:], kernel_v, preferred_element_type=F32)
        model = model + jnp.stack([jnp.sum(part_re * side, 1), jnp.sum(part_im * side, 1)], 1)
    misfit = model - measured.astype(F32)

    table_back = column_table(wavs, m, w, True)
    grads = {}
    for half in (1, 0):
        side = sides[half]
        w_re = (misfit[:, 0, None, :] * side).astype(BF16)
        w_im = (misfit[:, 1, None, :] * side).astype(BF16)
        term_re = jnp.einsum("nbt,nat->nba", w_re, kernel_v, preferred_element_type=F32)
        term_im = jnp.einsum("nbt,nat->nba", w_im, kernel_v, preferred_element_type=F32)
        terms = jnp.concatenate([term_re, term_im], -1).astype(BF16)
        if half == 0:
            terms, chips = lax.optimization_barrier((terms, chips))
        chips = [terms] + to_chips([terms] * 3)
        other = flip(jnp.stack(chips), 1)
        grad = gather_fast(a_block, b_block, chips + [other], table_back, cos_k, sin_k, wavs, part, m, half)
        grads[half] = exchange(grad)

    back_table = row_table_back(rows, w * part)
    first = call(rows_inverse_first, [((3, rows, m), F32)], [], *grads[1], *back_table, twist)
    grad = call(rows_inverse_last, [((vis, rows, m), BF16)], [], *grads[0], *first, *back_table, twist)[0]
    grad = lax.all_to_all(grad, "vis", split_axis=0, concat_axis=0, tiled=True)
    edge = ((HALO, rows), F32)
    back = spread_matrix(vis, m).T.astype(BF16)
    shifted, first_cols, last_cols = call(step_kernel, [((rows, cols), F32), edge, edge], [], image, grad, back)
    right = ahead(first_cols, wavs - 1)
    left = ahead(last_cols, 1)
    return haar_mean(shifted, left, right, thresholds), misfit


def shards(image, kernel_v, kernel_u, measured, dest_owner, patch_slot, thresholds):
    vis = lax.axis_size("vis")
    wavs = lax.axis_size("wav")
    v = lax.axis_index("vis")
    rows, cols = image.shape
    img = rows * vis
    m = cols // vis
    down = rows // PATCH
    across = cols // PATCH
    blocks = kernel_v.shape[0]
    low = PATCH // vis
    part = rows // wavs
    if vis == 8 and m == LANES and low == 8 and part % 8 == 0 and rows & (rows - 1) == 0:
        return shards_fast(image, kernel_v, kernel_u, measured, dest_owner, patch_slot, thresholds)
    spread = spread_matrix(vis, m)

    ids = jnp.concatenate([dest_owner, patch_slot[:, None]], 1)
    ids = lax.all_gather(ids, "vis", axis=0, tiled=True)
    owner, slot = ids[:, 0], ids[:, 1]
    a_block, b_block = slot // across, slot % across

    x = jnp.dot(image, spread, precision=HIGH).astype(F16)
    x = x.reshape(rows, vis, m).transpose(1, 0, 2)
    x = lax.all_to_all(x, "vis", split_axis=0, concat_axis=0, tiled=True).astype(F32)
    y = rows_forward(x, vis).astype(F16)
    y = y.reshape(vis, wavs, part, 2 * m).transpose(1, 0, 2, 3)
    y = lax.all_to_all(y, "wav", split_axis=0, concat_axis=0, tiled=True).astype(F32)
    cos_k, sin_k = turns(v, owner[:, None] * rows + a_block[:, None] * PATCH + iota(PATCH)[None, :], img)
    cos_k = jnp.concatenate([cos_k, cos_k], 1)
    sin_k = jnp.concatenate([sin_k, -sin_k], 1)
    y = y.transpose(1, 2, 0, 3).reshape(cols, 2 * wavs * m)
    table = column_matrix(wavs, m, down, 1.0 / img)
    z = jnp.dot(y, table, precision=HIGH)
    z = z.reshape(vis, across, low, down, 2 * PATCH)
    tiles = z[:, b_block, :, a_block, :].reshape(vis * blocks, PATCH, 2 * PATCH)
    tiles = tiles * cos_k[:, None] + jnp.roll(tiles, PATCH, axis=2) * sin_k[:, None]
    tiles = lax.all_to_all(tiles.astype(F16), "vis", split_axis=0, concat_axis=0, tiled=True)
    patch = jnp.sum(tiles.reshape(vis, blocks, PATCH, 2 * PATCH).astype(F32), 0).astype(BF16)

    side_u = kernel_u.reshape(blocks, low, vis, -1).transpose(0, 2, 1, 3).reshape(kernel_u.shape)
    part_re = jnp.einsum("nba,nat->nbt", patch[..., :PATCH], kernel_v, preferred_element_type=F32)
    part_im = jnp.einsum("nba,nat->nbt", patch[..., PATCH:], kernel_v, preferred_element_type=F32)
    side = side_u.astype(F32)
    misfit = jnp.stack([jnp.sum(part_re * side, 1), jnp.sum(part_im * side, 1)], 1) - measured.astype(F32)
    w_re = (misfit[:, 0, None, :] * side).astype(BF16)
    w_im = (misfit[:, 1, None, :] * side).astype(BF16)
    term_re = jnp.einsum("nbt,nat->nba", w_re, kernel_v, preferred_element_type=F32)
    term_im = jnp.einsum("nbt,nat->nba", w_im, kernel_v, preferred_element_type=F32)
    terms = jnp.concatenate([term_re, term_im], -1).astype(BF16)

    terms = lax.all_gather(terms, "vis", axis=0, tiled=True)
    terms = terms.astype(F32)
    terms = terms * cos_k[:, None] - jnp.roll(terms, PATCH, axis=2) * sin_k[:, None]
    terms = terms.reshape(vis * blocks, vis, low, 2 * PATCH)
    flat = jnp.zeros((across * down, vis, low, 2 * PATCH), F32).at[b_block * down + a_block].add(terms)
    grad = flat.reshape(across, down, vis, low, 2 * PATCH).transpose(2, 0, 3, 1, 4).reshape(cols, 2 * rows)
    grad = lax.dot_general(grad, table, (((1,), (1,)), ((), ())), precision=HIGH).astype(BF16)
    grad = grad.reshape(vis, part, wavs, 2 * m).transpose(2, 0, 1, 3)
    grad = lax.all_to_all(grad, "wav", split_axis=0, concat_axis=0, tiled=True)
    grad = grad.astype(F32).transpose(1, 0, 2, 3).reshape(vis, rows, 2 * m)
    grad = rows_inverse(grad, vis).astype(BF16)
    grad = lax.all_to_all(grad, "vis", split_axis=0, concat_axis=0, tiled=True)
    grad = grad.transpose(1, 0, 2).reshape(rows, cols)
    grad = lax.dot_general(grad, spread.astype(BF16), (((1,), (1,)), ((), ())), preferred_element_type=F32)
    shifted = image - grad
    right = lax.ppermute(shifted[:, :HALO].T, "wav", [(i, (i - 1) % wavs) for i in range(wavs)])
    left = lax.ppermute(shifted[:, -HALO:].T, "wav", [(i, (i + 1) % wavs) for i in range(wavs)])
    return haar_mean(shifted, left, right, thresholds), misfit


def solution(mesh):
    both = ("vis", "wav")
    in_specs = (
        P("vis", "wav"),
        P(both, None, None),
        P(both, None, None),
        P(both, None, None),
        P(both, None),
        P(both),
        P(),
    )
    out_specs = (P("vis", "wav"), P(both, None, None))
    return jax.shard_map(shards, mesh=mesh, in_specs=in_specs, out_specs=out_specs, check_vma=False)
```

```python
import math

import jax
import jax.numpy as jnp
import numpy as np
from jax import lax
from jax.experimental import pallas as pl
from jax.experimental.pallas import tpu as pltpu
from jax.sharding import PartitionSpec as P


PATCH = 64
HIGH = lax.Precision.HIGH
F32 = jnp.float32
BF16 = jnp.bfloat16
F16 = jnp.float16


def turns(rows, cols, period):
    angle = (rows * cols % period).astype(F32) * (2.0 * math.pi / period)
    return jnp.cos(angle), jnp.sin(angle)


def iota(size):
    return jnp.arange(size, dtype=jnp.int32)


def spread_matrix(groups, size):
    width = groups * size
    c = iota(width)
    return (c[:, None] == (c % size * groups + c // size)[None, :]).astype(F32)


def rows_forward(x, groups):
    rows = x.shape[1]
    count = groups * rows
    cos_g, sin_g = (np.cos(2 * np.pi * np.outer(np.arange(groups), np.arange(groups)) / groups), np.sin(2 * np.pi * np.outer(np.arange(groups), np.arange(groups)) / groups))
    mixed_re = jnp.einsum("kv,vnm->knm", jnp.asarray(cos_g, F32), x, precision=HIGH)
    mixed_im = -jnp.einsum("kv,vnm->knm", jnp.asarray(sin_g, F32), x, precision=HIGH)
    cos_t, sin_t = turns(iota(groups)[:, None], iota(rows)[None, :], count)
    cos_t, sin_t = cos_t[:, :, None], sin_t[:, :, None]
    both = jnp.concatenate([mixed_re * cos_t + mixed_im * sin_t, mixed_im * cos_t - mixed_re * sin_t], -1)
    cos_r, sin_r = turns(iota(rows)[:, None], iota(rows)[None, :], rows)
    p = jnp.einsum("kn,vnm->vkm", cos_r, both, precision=HIGH)
    q = jnp.einsum("kn,vnm->vkm", sin_r, both, precision=HIGH)
    m = x.shape[2]
    return jnp.concatenate([p[..., :m] + q[..., m:], p[..., m:] - q[..., :m]], -1)


def rows_inverse(y, groups):
    rows = y.shape[1]
    m = y.shape[2] // 2
    count = groups * rows
    cos_r, sin_r = turns(iota(rows)[:, None], iota(rows)[None, :], rows)
    p = jnp.einsum("kn,vnm->vkm", cos_r, y, precision=HIGH)
    q = jnp.einsum("kn,vnm->vkm", sin_r, y, precision=HIGH)
    re, im = p[..., :m] - q[..., m:], p[..., m:] + q[..., :m]
    cos_t, sin_t = turns(iota(groups)[:, None], iota(rows)[None, :], count)
    cos_t, sin_t = cos_t[:, :, None], sin_t[:, :, None]
    re, im = re * cos_t - im * sin_t, im * cos_t + re * sin_t
    cos_g, sin_g = (np.cos(2 * np.pi * np.outer(np.arange(groups), np.arange(groups)) / groups), np.sin(2 * np.pi * np.outer(np.arange(groups), np.arange(groups)) / groups))
    out = jnp.einsum("vk,knm->vnm", jnp.asarray(cos_g, F32), re, precision=HIGH)
    return out - jnp.einsum("vk,knm->vnm", jnp.asarray(sin_g, F32), im, precision=HIGH)


def column_matrix(wavs, m, down, scale):
    size = wavs * m
    cos_c, sin_c = turns(iota(size)[:, None], iota(size)[None, :], size)
    cos_c = (cos_c * scale).reshape(wavs, 1, m, down, 1, PATCH)
    sin_c = (sin_c * scale).reshape(wavs, 1, m, down, 1, PATCH)
    from_re = jnp.concatenate([cos_c, -sin_c], 4)
    from_im = jnp.concatenate([sin_c, cos_c], 4)
    return jnp.concatenate([from_re, from_im], 1).reshape(2 * size, 2 * size)


def split(x):
    high = lax.reduce_precision(x, 8, 7)
    return high.astype(BF16), (x - high).astype(BF16)


def bits(size):
    return size.bit_length() - 1


def cosine(count, period):
    part = (count & (period - 1)).astype(F32) * (1.0 / period)
    part = 0.25 - jnp.abs(part - jnp.where(part > 0.5, 1.0, 0.0))
    square = part * part
    terms = [(-1) ** i * (2 * math.pi) ** (2 * i + 1) / math.factorial(2 * i + 1) for i in range(7)]
    value = jnp.full_like(part, terms[-1])
    for term in terms[-2::-1]:
        value = value * square + term
    return value * part


def grid_of(shape):
    return [lax.broadcasted_iota(jnp.int32, shape, axis) for axis in (0, 1)]


def row_table(size, first):
    k, n = grid_of((2 * size, size))
    return split(cosine(((k + first) & (size - 1)) * n - (k >> bits(size)) * (size // 4), size))


def row_table_back(size, first):
    r, k = grid_of((2 * size, size))
    return split(cosine(((k + first) & (size - 1)) * (r & (size - 1)) - (r >> bits(size)) * (size // 4), size))


def column_table(wavs, m, first, turned):
    size = wavs * m
    row, col = grid_of((2 * size, 2 * size))[:: -1 if turned else 1]
    n = (row >> bits(2 * m)) * m + (row & (m - 1)) + first * m
    k = (col >> bits(2 * PATCH)) * PATCH + (col & (PATCH - 1))
    quarter = (col >> bits(PATCH) & 1) - (row >> bits(m) & 1)
    return split(cosine((n & (size - 1)) * k + quarter * (size // 4), size))


def twist_table(groups, rows):
    n, k = grid_of((rows, 2 * groups))
    count = groups * rows
    return cosine(n * (k & (groups - 1)) - (k >> bits(groups)) * (count // 4), count)


def in_vmem(count):
    return [pl.BlockSpec(memory_space=pltpu.VMEM)] * count


VMEM_LIMIT = 12 * 1024 * 1024
ROOT = math.sqrt(0.5)


AT_ONCE = 8
HALVES = ((0, 1, 7, 2, 6), (4, 3, 5))
ORDER = HALVES[0] + HALVES[1]


def call(kernel, out_shapes, scratch, *args, smem=0):
    return pl.pallas_call(
        kernel,
        in_specs=[pl.BlockSpec(memory_space=pltpu.SMEM)] * smem + in_vmem(len(args) - smem),
        out_specs=in_vmem(len(out_shapes)),
        out_shape=[jax.ShapeDtypeStruct(shape, kind) for shape, kind in out_shapes],
        scratch_shapes=[pltpu.VMEM(shape, kind) for shape, kind in scratch],
        compiler_params=pltpu.CompilerParams(vmem_limit_bytes=VMEM_LIMIT),
    )(*args)


def spread_kernel(image_ref, out_ref):
    groups, _, m = out_ref.shape
    width = groups * m
    high = image_ref[...].astype(BF16)
    low = (image_ref[...] - high.astype(F32)).astype(BF16)
    c = lax.broadcasted_iota(jnp.int32, (width, 2 * m), 0)
    place = lax.broadcasted_iota(jnp.int32, (width, 2 * m), 1)
    for v in range(0, groups, 2):
        table = (c == (place & (m - 1)) * groups + (place >> bits(m)) + v).astype(F32).astype(BF16)
        out = jnp.dot(high, table, preferred_element_type=F32) + jnp.dot(low, table, preferred_element_type=F32)
        out_ref[v] = out[:, :m]
        out_ref[v + 1] = out[:, m:]


def rows_forward_kernel(x_ref, high_ref, low_ref, twist_ref, *y_refs, half):
    rows, m = x_ref.shape[1:]
    wavs = len(y_refs)
    part = rows // wavs
    x = [x_ref[i].astype(F32) for i in range(8)]
    e0, e1, f0, f1 = x[0] + x[4], x[0] - x[4], x[2] + x[6], x[2] - x[6]
    g0, g1, h0, h1 = x[1] + x[5], x[1] - x[5], x[3] + x[7], x[3] - x[7]
    gm, gp = (g1 - h1) * ROOT, (g1 + h1) * ROOT
    zero = jnp.zeros_like(e0)
    mixed = {
        0: (e0 + f0 + g0 + h0, zero),
        1: (e1 + gm, -f1 - gp),
        2: (e0 - f0, h0 - g0),
        3: (e1 - gm, f1 - gp),
        4: (e0 + f0 - g0 - h0, zero),
    }
    for spot, k in enumerate(HALVES[half]):
        if k > 4:
            continue
        re, im = mixed[k]
        if k:
            cos_t, sin_t = twist_ref[:, k : k + 1], twist_ref[:, 8 + k : 9 + k]
            re, im = re * cos_t + im * sin_t, im * cos_t - re * sin_t
        both = jnp.concatenate([re, im], 1)
        high = both.astype(BF16)
        low = (both - high.astype(F32)).astype(BF16)
        out = jnp.dot(high_ref[...], high, preferred_element_type=F32)
        out += jnp.dot(high_ref[...], low, preferred_element_type=F32)
        out += jnp.dot(low_ref[...], high, preferred_element_type=F32)
        p_re, p_im, q_re, q_im = out[:rows, :m], out[:rows, m:], out[rows:, :m], out[rows:, m:]
        here = jnp.concatenate([p_re + q_im, p_im - q_re], 1)
        for w in range(wavs):
            y_refs[w][spot] = here[w * part : (w + 1) * part]
        if k in (1, 2, 3):
            there = jnp.concatenate([p_re - q_im, -p_im - q_re], 1)
            there = pltpu.roll(there, rows - 1, 0)
            for w in range(wavs):
                y_refs[w][spot + 1] = there[w * part : (w + 1) * part]


def rows_forward_fast(x, wavs, table, twist, half):
    _, rows, m = x.shape
    kernel = lambda *refs: rows_forward_kernel(*refs, half=half)
    return call(kernel, [((len(HALVES[half]), rows // wavs, 2 * m), F32)] * wavs, [], x, *table, twist)


def shares_kernel(a_ref, b_ref, *refs, wavs):
    y_refs = refs[:wavs]
    high_ref, low_ref, cos_ref, sin_ref, far_ref, near_ref, z_ref, head_ref, rest_ref = refs[wavs:]
    groups, part, double = y_refs[0].shape
    down = z_ref.shape[0]
    wide = 2 * PATCH
    low = 8
    blocks = near_ref.shape[1]
    scale = 1.0 / (8 * down * PATCH)
    for w in range(wavs):
        y = y_refs[w][...].astype(F32).reshape(groups * part, double)
        high = y.astype(BF16)
        head_ref[:, w * double : (w + 1) * double] = high
        rest_ref[:, w * double : (w + 1) * double] = (y - high.astype(F32)).astype(BF16)
    for a in range(0, down, 2):
        spot = (slice(None), pl.ds(a * wide, 2 * wide))
        z = jnp.dot(head_ref[...], high_ref[spot], preferred_element_type=F32)
        z += jnp.dot(rest_ref[...], high_ref[spot], preferred_element_type=F32)
        z += jnp.dot(head_ref[...], low_ref[spot], preferred_element_type=F32)
        z = z * scale
        z_ref[a] = z[:, :wide].reshape(groups, part, wide)
        z_ref[a + 1] = z[:, wide:].reshape(groups, part, wide)
    for core, out_ref in ((1, far_ref), (0, near_ref)):

        @pl.loop(0, 4 * blocks // AT_ONCE)
        def _(step):
            chip, first = step // (blocks // AT_ONCE), step % (blocks // AT_ONCE) * AT_ONCE
            for i in range(AT_ONCE):
                at = first + i
                n = (2 * chip + core) * blocks + at
                start = pl.multiple_of(b_ref[n] * low, low)
                tile = z_ref[a_ref[n], :, pl.ds(start, low), :].reshape(groups * low, wide)
                out_ref[chip, at] = tile * cos_ref[pl.ds(n, 1), :] + pltpu.roll(tile, PATCH, 1) * sin_ref[pl.ds(n, 1), :]


def shares_fast(a_block, b_block, ys, table, cos_k, sin_k):
    groups, part, double = ys[0].shape
    wavs = len(ys)
    width = wavs * double
    blocks = a_block.shape[0] // 8
    out = ((4, blocks, groups * 8, 2 * PATCH), F32)
    scratch = [((width // (2 * PATCH), groups, part, 2 * PATCH), F32)] + [((groups * part, width), BF16)] * 2
    kernel = lambda *refs: shares_kernel(*refs, wavs=wavs)
    return call(kernel, [out, out], scratch, a_block, b_block, *ys, *table, cos_k, sin_k, smem=2)


def gather_kernel(a_ref, b_ref, *refs):
    high_ref, low_ref, cos_ref, sin_ref = refs[5:9]
    y_refs, (g_ref, head_ref) = refs[9:-2], refs[-2:]
    groups, part, double = y_refs[0].shape
    down = g_ref.shape[0]
    wide = 2 * PATCH
    low = 8
    blocks = refs[0].shape[0]
    g_ref[...] = jnp.zeros_like(g_ref)

    def add(term_ref, mask, first):
        tiles = []
        for i in range(AT_ONCE):
            n = mask * blocks + first + i
            tile = term_ref[first + i].astype(F32)
            tiles.append(tile * cos_ref[pl.ds(n, 1), :] - pltpu.roll(tile, PATCH, 1) * sin_ref[pl.ds(n, 1), :])
        for i in range(AT_ONCE):
            n = mask * blocks + first + i
            start = pl.multiple_of(b_ref[n] * low, low)
            g_ref[a_ref[n], :, pl.ds(start, low), :] += tiles[i].reshape(groups, low, wide)

    steps = blocks // AT_ONCE
    for chip in range(4):
        pl.loop(0, steps)(lambda step: add(refs[chip], 2 * chip, step * AT_ONCE))
    pl.loop(0, 4 * steps)(lambda step: add(refs[4].at[step // steps], 2 * (step // steps) + 1, step % steps * AT_ONCE))

    for a in range(down):
        head_ref[:, a * wide : (a + 1) * wide] = g_ref[a].reshape(groups * part, wide).astype(BF16)
    scale = 1.0 / (8 * down * PATCH)
    for w, y_ref in enumerate(y_refs):
        spot = (slice(None), pl.ds(w * double, double))
        y = jnp.dot(head_ref[...], high_ref[spot], preferred_element_type=F32)
        y += jnp.dot(head_ref[...], low_ref[spot], preferred_element_type=F32)
        y_ref[...] = (y * scale).astype(BF16).reshape(groups, part, double)


def gather_fast(a_block, b_block, terms, table, cos_k, sin_k, wavs, part, m, half):
    width = 2 * wavs * m
    groups = len(HALVES[half])
    out = [((groups, part, 2 * m), BF16)] * wavs
    scratch = [((width // (2 * PATCH), groups, part, 2 * PATCH), F32), ((groups * part, width), BF16)]
    return call(gather_kernel, out, scratch, a_block, b_block, *terms, *table, cos_k, sin_k, smem=2)


def untwist(y_refs, spot, k, high_ref, low_ref, twist_ref):
    y = jnp.concatenate([ref[spot] for ref in y_refs], 0)
    rows, m = y.shape[0], y.shape[1] // 2
    out = jnp.dot(high_ref[...], y, preferred_element_type=F32)
    out += jnp.dot(low_ref[...], y, preferred_element_type=F32)
    re, im = out[:rows, :m] - out[rows:, m:], out[:rows, m:] + out[rows:, :m]
    if k:
        cos_t, sin_t = twist_ref[:, k : k + 1], twist_ref[:, 8 + k : 9 + k]
        re, im = re * cos_t - im * sin_t, im * cos_t + re * sin_t
    return re, im


def rows_inverse_first(*refs):
    y_refs, (high_ref, low_ref, twist_ref, out_ref) = refs[:-4], refs[-4:]
    (re4, _), (re3, im3), (re5, im5) = [
        untwist(y_refs, spot, k, high_ref, low_ref, twist_ref) for spot, k in enumerate(HALVES[1])
    ]
    out_ref[0] = re4
    out_ref[1] = re3 + re5
    out_ref[2] = im3 - im5


def rows_inverse_last(*refs):
    y_refs, (first_ref, high_ref, low_ref, twist_ref, x_ref) = refs[:-5], refs[-5:]
    (re0, _), (re1, im1), (re7, im7), (re2, im2), (re6, im6) = [
        untwist(y_refs, spot, k, high_ref, low_ref, twist_ref) for spot, k in enumerate(HALVES[0])
    ]
    re4, r3, i3 = [first_ref[i] for i in range(3)]
    even, odd = re0 + re4, re0 - re4
    r1, r2, i1, i2 = re1 + re7, re2 + re6, im1 - im7, im2 - im6
    rm, ip = (r1 - r3) * ROOT, (i1 + i3) * ROOT
    x_ref[0] = (even + r2 + (r1 + r3)).astype(BF16)
    x_ref[4] = (even + r2 - (r1 + r3)).astype(BF16)
    x_ref[2] = (even - r2 - (i1 - i3)).astype(BF16)
    x_ref[6] = (even - r2 + (i1 - i3)).astype(BF16)
    x_ref[1] = (odd + rm - ip - i2).astype(BF16)
    x_ref[7] = (odd + rm + ip + i2).astype(BF16)
    x_ref[3] = (odd - rm - ip + i2).astype(BF16)
    x_ref[5] = (odd - rm + ip - i2).astype(BF16)


HALO = 8
LANES = 128


def step_kernel(image_ref, grad_ref, spread_ref, out_ref, first_ref, last_ref):
    _, width = image_ref.shape
    grad = jnp.concatenate([grad_ref[i] for i in range(grad_ref.shape[0])], 1)
    out_ref[...] = image_ref[...] - jnp.dot(grad, spread_ref[...], preferred_element_type=F32)
    first_ref[...] = out_ref[:, :LANES].T[:HALO]
    last_ref[...] = out_ref[:, width - LANES :].T[LANES - HALO :]


def haar_kernel(field_ref, left_ref, right_ref, limit_ref, out_ref, edge_ref, *, bases):
    every, width = field_ref.shape
    rows = 64
    span = width + LANES
    middle = jnp.zeros((LANES - 2 * HALO, every), F32)
    edge_ref[...] = jnp.concatenate([right_ref[...], middle, left_ref[...]], 0).T
    even = lax.broadcasted_iota(jnp.int32, (rows, span), 0) % 2 == 0

    def mix(x, even):
        other = jnp.where(even, pltpu.roll(x, rows - 1, 0), pltpu.roll(x, 1, 0))
        return jnp.where(even, x, -x) + other

    def ahead(x, by):
        return pltpu.roll(x, span - by, 1)

    def behind(x, by):
        return pltpu.roll(x, by, 1)

    def mean(u):
        spot = 0
        level = []
        for period in (2, 4, 8):
            forward = ahead(u, period // 2)
            parts = [u + forward, u - forward]
            limits = []
            for _ in range(0, bases, period):
                limits.append(limit_ref[spot : spot + 1, :])
                spot += 1
            limited = []
            for x in parts if period == 8 else parts[1:]:
                total = None
                for limit in limits:
                    x_soft = x - jnp.minimum(jnp.maximum(x, -limit), limit)
                    total = x_soft if total is None else total + x_soft
                limited.append(total)
            level.append(limited)
            u = parts[0]
        s3, d3 = level[2]
        back = (s3 + d3) + behind(s3 - d3, 4)
        for by, (d,) in ((2, level[1]), (1, level[0])):
            back = back * 0.5
            back = (back + d) + behind(back - d, by)
        return back[:, :width] * (0.25 / bases)

    @pl.loop(0, every // rows)
    def _(step):
        spot = (pl.ds(pl.multiple_of(step * rows, rows), rows), slice(None))
        field = jnp.concatenate([field_ref[spot], edge_ref[spot]], 1)
        out_ref[spot] = mix(mean(mix(field, even)), even[:, :width])


def haar_limits(width, thresholds):
    bases = thresholds.shape[0]
    span = width + LANES
    place = iota(span)
    place = jnp.where(place < width + LANES // 2, place, place - span) + 8
    out = []
    for period in (2, 4, 8):
        scale = math.sqrt(2.0 * period)
        for start in range(0, bases, period):
            index = place % period + start
            limit = jnp.full((span,), 3e38, F32)
            for s in range(start, min(start + period, bases)):
                limit = jnp.where(index == s, thresholds[s] * scale, limit)
            out.append(limit)
    return jnp.stack(out)


def haar_mean(field, halo_left, halo_right, thresholds):
    bases = thresholds.shape[0]
    rows, width = field.shape
    limits = haar_limits(width, thresholds)
    step = LANES
    return pl.pallas_call(
        lambda *refs: haar_kernel(*refs, bases=bases),
        grid=(rows // step,),
        in_specs=[
            pl.BlockSpec((step, width), lambda i: (i, 0)),
            pl.BlockSpec((HALO, step), lambda i: (0, i)),
            pl.BlockSpec((HALO, step), lambda i: (0, i)),
            pl.BlockSpec(limits.shape, lambda i: (0, 0)),
        ],
        out_specs=pl.BlockSpec((step, width), lambda i: (i, 0)),
        out_shape=jax.ShapeDtypeStruct((rows, width), F32),
        scratch_shapes=[pltpu.VMEM((step, LANES), F32)],
        compiler_params=pltpu.CompilerParams(vmem_limit_bytes=VMEM_LIMIT),
        name="haar",
    )(field, halo_left, halo_right, limits)


def phases(owner, a_block, v, rows, img):
    cos_k, sin_k = turns(v, owner[:, None] * rows + a_block[:, None] * PATCH + iota(PATCH)[None, :], img)
    return jnp.concatenate([cos_k, cos_k], 1), jnp.concatenate([sin_k, -sin_k], 1)


def shards_fast(image, kernel_v, kernel_u, measured, dest_owner, patch_slot, thresholds):
    vis = lax.axis_size("vis")
    wavs = lax.axis_size("wav")
    v, w = lax.axis_index("vis"), lax.axis_index("wav")
    rows, cols = image.shape
    img = rows * vis
    m = cols // vis
    across = cols // PATCH
    blocks = kernel_v.shape[0]
    part = rows // wavs

    def flip(x, mask):
        return lax.ppermute(x, "vis", [(i, i ^ mask) for i in range(vis)])

    def ahead(x, by):
        return lax.ppermute(x, "wav", [(i, (i + by) % wavs) for i in range(wavs)])

    def exchange(parts):
        out = [parts[0]]
        for s in range(1, wavs):
            out.append(ahead(parts[wavs - s], wavs - s))
        return out

    def to_chips(parts):
        out = []
        for chip in (1, 2, 3):
            out.append(flip(parts[chip - 1], 2 * chip))
        return out

    x = call(spread_kernel, [((vis, rows, m), F32)], [], image)[0].astype(F16)
    x = lax.all_to_all(x, "vis", split_axis=0, concat_axis=0, tiled=True).astype(F32)

    forward_table, twist = row_table(rows, w * part), twist_table(vis, rows)
    sent, spectra = [], []
    for half in (0, 1):
        y = rows_forward_fast(x, wavs, forward_table, twist, half)
        sent.append([part_y.astype(F16) for part_y in y])
        spectra.append(exchange(sent[half]))
    spectra[0], _ = lax.optimization_barrier((spectra[0], sent[1]))

    ids = jnp.stack([dest_owner[:, 0], patch_slot])
    ids, _ = lax.optimization_barrier((ids, sent[1]))
    for mask in (1, 2, 4):
        ids = jnp.concatenate([ids, flip(ids, mask)], 1)
    owner, slot = ids[0], ids[1]
    a_block, b_block = slot // across, slot % across
    cos_k, sin_k = phases(owner, a_block, v, rows, img)

    table = column_table(wavs, m, w, False)
    patches = []
    for half in (0, 1):
        y = []
        for part_y in spectra[half]:
            y.append(part_y.astype(F32))
        far, near = shares_fast(a_block, b_block, y, table, cos_k, sin_k)
        near = near + flip(far.astype(F16), 1).astype(F32)
        ready = [near[0]] + [near[chip].astype(F16) for chip in (1, 2, 3)]
        if half == 0:
            spectra[1], ready = lax.optimization_barrier((spectra[1], ready))
        total = ready[0]
        for came in to_chips(ready[1:]):
            total = total + came.astype(F32)
        patches.append(total.astype(BF16))

    order = jnp.asarray(ORDER)
    side = kernel_u.reshape(blocks, 8, vis, -1)[:, :, order].transpose(0, 2, 1, 3).reshape(kernel_u.shape).astype(F32)
    cut = 8 * len(HALVES[0])
    sides = [side[:, :cut], side[:, cut:]]
    model = 0.0
    for patch, side in zip(patches, sides):
        part_re = jnp.einsum("nba,nat->nbt", patch[..., :PATCH], kernel_v, preferred_element_type=F32)
        part_im = jnp.einsum("nba,nat->nbt", patch[..., PATCH:], kernel_v, preferred_element_type=F32)
        model = model + jnp.stack([jnp.sum(part_re * side, 1), jnp.sum(part_im * side, 1)], 1)
    misfit = model - measured.astype(F32)

    table_back = column_table(wavs, m, w, True)
    grads = {}
    for half in (1, 0):
        side = sides[half]
        w_re = (misfit[:, 0, None, :] * side).astype(BF16)
        w_im = (misfit[:, 1, None, :] * side).astype(BF16)
        term_re = jnp.einsum("nbt,nat->nba", w_re, kernel_v, preferred_element_type=F32)
        term_im = jnp.einsum("nbt,nat->nba", w_im, kernel_v, preferred_element_type=F32)
        terms = jnp.concatenate([term_re, term_im], -1).astype(BF16)
        if half == 0:
            terms, chips = lax.optimization_barrier((terms, chips))
        chips = [terms] + to_chips([terms] * 3)
        other = flip(jnp.stack(chips), 1)
        grad = gather_fast(a_block, b_block, chips + [other], table_back, cos_k, sin_k, wavs, part, m, half)
        grads[half] = exchange(grad)

    back_table = row_table_back(rows, w * part)
    first = call(rows_inverse_first, [((3, rows, m), F32)], [], *grads[1], *back_table, twist)
    grad = call(rows_inverse_last, [((vis, rows, m), BF16)], [], *grads[0], *first, *back_table, twist)[0]
    grad = lax.all_to_all(grad, "vis", split_axis=0, concat_axis=0, tiled=True)
    edge = ((HALO, rows), F32)
    back = spread_matrix(vis, m).T.astype(BF16)
    shifted, first_cols, last_cols = call(step_kernel, [((rows, cols), F32), edge, edge], [], image, grad, back)
    right = ahead(first_cols, wavs - 1)
    left = ahead(last_cols, 1)
    return haar_mean(shifted, left, right, thresholds), misfit


def shards(image, kernel_v, kernel_u, measured, dest_owner, patch_slot, thresholds):
    vis = lax.axis_size("vis")
    wavs = lax.axis_size("wav")
    v = lax.axis_index("vis")
    rows, cols = image.shape
    img = rows * vis
    m = cols // vis
    down = rows // PATCH
    across = cols // PATCH
    blocks = kernel_v.shape[0]
    low = PATCH // vis
    part = rows // wavs
    if vis == 8 and m == LANES and low == 8 and part % 8 == 0 and rows & (rows - 1) == 0:
        return shards_fast(image, kernel_v, kernel_u, measured, dest_owner, patch_slot, thresholds)
    spread = spread_matrix(vis, m)

    ids = jnp.concatenate([dest_owner, patch_slot[:, None]], 1)
    ids = lax.all_gather(ids, "vis", axis=0, tiled=True)
    owner, slot = ids[:, 0], ids[:, 1]
    a_block, b_block = slot // across, slot % across

    x = jnp.dot(image, spread, precision=HIGH).astype(F16)
    x = x.reshape(rows, vis, m).transpose(1, 0, 2)
    x = lax.all_to_all(x, "vis", split_axis=0, concat_axis=0, tiled=True).astype(F32)
    y = rows_forward(x, vis).astype(F16)
    y = y.reshape(vis, wavs, part, 2 * m).transpose(1, 0, 2, 3)
    y = lax.all_to_all(y, "wav", split_axis=0, concat_axis=0, tiled=True).astype(F32)
    cos_k, sin_k = turns(v, owner[:, None] * rows + a_block[:, None] * PATCH + iota(PATCH)[None, :], img)
    cos_k = jnp.concatenate([cos_k, cos_k], 1)
    sin_k = jnp.concatenate([sin_k, -sin_k], 1)
    y = y.transpose(1, 2, 0, 3).reshape(cols, 2 * wavs * m)
    table = column_matrix(wavs, m, down, 1.0 / img)
    z = jnp.dot(y, table, precision=HIGH)
    z = z.reshape(vis, across, low, down, 2 * PATCH)
    tiles = z[:, b_block, :, a_block, :].reshape(vis * blocks, PATCH, 2 * PATCH)
    tiles = tiles * cos_k[:, None] + jnp.roll(tiles, PATCH, axis=2) * sin_k[:, None]
    tiles = lax.all_to_all(tiles.astype(F16), "vis", split_axis=0, concat_axis=0, tiled=True)
    patch = jnp.sum(tiles.reshape(vis, blocks, PATCH, 2 * PATCH).astype(F32), 0).astype(BF16)

    side_u = kernel_u.reshape(blocks, low, vis, -1).transpose(0, 2, 1, 3).reshape(kernel_u.shape)
    part_re = jnp.einsum("nba,nat->nbt", patch[..., :PATCH], kernel_v, preferred_element_type=F32)
    part_im = jnp.einsum("nba,nat->nbt", patch[..., PATCH:], kernel_v, preferred_element_type=F32)
    side = side_u.astype(F32)
    misfit = jnp.stack([jnp.sum(part_re * side, 1), jnp.sum(part_im * side, 1)], 1) - measured.astype(F32)
    w_re = (misfit[:, 0, None, :] * side).astype(BF16)
    w_im = (misfit[:, 1, None, :] * side).astype(BF16)
    term_re = jnp.einsum("nbt,nat->nba", w_re, kernel_v, preferred_element_type=F32)
    term_im = jnp.einsum("nbt,nat->nba", w_im, kernel_v, preferred_element_type=F32)
    terms = jnp.concatenate([term_re, term_im], -1).astype(BF16)

    terms = lax.all_gather(terms, "vis", axis=0, tiled=True)
    terms = terms.astype(F32)
    terms = terms * cos_k[:, None] - jnp.roll(terms, PATCH, axis=2) * sin_k[:, None]
    terms = terms.reshape(vis * blocks, vis, low, 2 * PATCH)
    flat = jnp.zeros((across * down, vis, low, 2 * PATCH), F32).at[b_block * down + a_block].add(terms)
    grad = flat.reshape(across, down, vis, low, 2 * PATCH).transpose(2, 0, 3, 1, 4).reshape(cols, 2 * rows)
    grad = lax.dot_general(grad, table, (((1,), (1,)), ((), ())), precision=HIGH).astype(BF16)
    grad = grad.reshape(vis, part, wavs, 2 * m).transpose(2, 0, 1, 3)
    grad = lax.all_to_all(grad, "wav", split_axis=0, concat_axis=0, tiled=True)
    grad = grad.astype(F32).transpose(1, 0, 2, 3).reshape(vis, rows, 2 * m)
    grad = rows_inverse(grad, vis).astype(BF16)
    grad = lax.all_to_all(grad, "vis", split_axis=0, concat_axis=0, tiled=True)
    grad = grad.transpose(1, 0, 2).reshape(rows, cols)
    grad = lax.dot_general(grad, spread.astype(BF16), (((1,), (1,)), ((), ())), preferred_element_type=F32)
    shifted = image - grad
    right = lax.ppermute(shifted[:, :HALO].T, "wav", [(i, (i - 1) % wavs) for i in range(wavs)])
    left = lax.ppermute(shifted[:, -HALO:].T, "wav", [(i, (i + 1) % wavs) for i in range(wavs)])
    return haar_mean(shifted, left, right, thresholds), misfit


def solution(mesh):
    both = ("vis", "wav")
    in_specs = (
        P("vis", "wav"),
        P(both, None, None),
        P(both, None, None),
        P(both, None, None),
        P(both, None),
        P(both),
        P(),
    )
    out_specs = (P("vis", "wav"), P(both, None, None))
    return jax.shard_map(shards, mesh=mesh, in_specs=in_specs, out_specs=out_specs, check_vma=False)
```

```python
import math

import jax
import jax.numpy as jnp
import numpy as np
from jax import lax
from jax.experimental import pallas as pl
from jax.experimental.pallas import tpu as pltpu
from jax.sharding import PartitionSpec as P


PATCH = 64
HIGH = lax.Precision.HIGH
F32 = jnp.float32
BF16 = jnp.bfloat16
F16 = jnp.float16


def turns(rows, cols, period):
    angle = (rows * cols % period).astype(F32) * (2.0 * math.pi / period)
    return jnp.cos(angle), jnp.sin(angle)


def iota(size):
    return jnp.arange(size, dtype=jnp.int32)


def spread_matrix(groups, size):
    width = groups * size
    c = iota(width)
    return (c[:, None] == (c % size * groups + c // size)[None, :]).astype(F32)


def rows_forward(x, groups):
    rows = x.shape[1]
    count = groups * rows
    cos_g, sin_g = (np.cos(2 * np.pi * np.outer(np.arange(groups), np.arange(groups)) / groups), np.sin(2 * np.pi * np.outer(np.arange(groups), np.arange(groups)) / groups))
    mixed_re = jnp.einsum("kv,vnm->knm", jnp.asarray(cos_g, F32), x, precision=HIGH)
    mixed_im = -jnp.einsum("kv,vnm->knm", jnp.asarray(sin_g, F32), x, precision=HIGH)
    cos_t, sin_t = turns(iota(groups)[:, None], iota(rows)[None, :], count)
    cos_t, sin_t = cos_t[:, :, None], sin_t[:, :, None]
    both = jnp.concatenate([mixed_re * cos_t + mixed_im * sin_t, mixed_im * cos_t - mixed_re * sin_t], -1)
    cos_r, sin_r = turns(iota(rows)[:, None], iota(rows)[None, :], rows)
    p = jnp.einsum("kn,vnm->vkm", cos_r, both, precision=HIGH)
    q = jnp.einsum("kn,vnm->vkm", sin_r, both, precision=HIGH)
    m = x.shape[2]
    return jnp.concatenate([p[..., :m] + q[..., m:], p[..., m:] - q[..., :m]], -1)


def rows_inverse(y, groups):
    rows = y.shape[1]
    m = y.shape[2] // 2
    count = groups * rows
    cos_r, sin_r = turns(iota(rows)[:, None], iota(rows)[None, :], rows)
    p = jnp.einsum("kn,vnm->vkm", cos_r, y, precision=HIGH)
    q = jnp.einsum("kn,vnm->vkm", sin_r, y, precision=HIGH)
    re, im = p[..., :m] - q[..., m:], p[..., m:] + q[..., :m]
    cos_t, sin_t = turns(iota(groups)[:, None], iota(rows)[None, :], count)
    cos_t, sin_t = cos_t[:, :, None], sin_t[:, :, None]
    re, im = re * cos_t - im * sin_t, im * cos_t + re * sin_t
    cos_g, sin_g = (np.cos(2 * np.pi * np.outer(np.arange(groups), np.arange(groups)) / groups), np.sin(2 * np.pi * np.outer(np.arange(groups), np.arange(groups)) / groups))
    out = jnp.einsum("vk,knm->vnm", jnp.asarray(cos_g, F32), re, precision=HIGH)
    return out - jnp.einsum("vk,knm->vnm", jnp.asarray(sin_g, F32), im, precision=HIGH)


def column_matrix(wavs, m, down, scale):
    size = wavs * m
    cos_c, sin_c = turns(iota(size)[:, None], iota(size)[None, :], size)
    cos_c = (cos_c * scale).reshape(wavs, 1, m, down, 1, PATCH)
    sin_c = (sin_c * scale).reshape(wavs, 1, m, down, 1, PATCH)
    from_re = jnp.concatenate([cos_c, -sin_c], 4)
    from_im = jnp.concatenate([sin_c, cos_c], 4)
    return jnp.concatenate([from_re, from_im], 1).reshape(2 * size, 2 * size)


def split(x):
    high = lax.reduce_precision(x, 8, 7)
    return high.astype(BF16), (x - high).astype(BF16)


def bits(size):
    return size.bit_length() - 1


def cosine(count, period):
    part = (count & (period - 1)).astype(F32) * (1.0 / period)
    part = 0.25 - jnp.abs(part - jnp.where(part > 0.5, 1.0, 0.0))
    square = part * part
    terms = [(-1) ** i * (2 * math.pi) ** (2 * i + 1) / math.factorial(2 * i + 1) for i in range(7)]
    value = jnp.full_like(part, terms[-1])
    for term in terms[-2::-1]:
        value = value * square + term
    return value * part


def grid_of(shape):
    return [lax.broadcasted_iota(jnp.int32, shape, axis) for axis in (0, 1)]


def row_table(size, first):
    k, n = grid_of((2 * size, size))
    return split(cosine(((k + first) & (size - 1)) * n - (k >> bits(size)) * (size // 4), size))


def row_table_back(size, first):
    r, k = grid_of((2 * size, size))
    return split(cosine(((k + first) & (size - 1)) * (r & (size - 1)) - (r >> bits(size)) * (size // 4), size))


def column_table(wavs, m, first, turned):
    size = wavs * m
    row, col = grid_of((2 * size, 2 * size))[:: -1 if turned else 1]
    n = (row >> bits(2 * m)) * m + (row & (m - 1)) + first * m
    k = (col >> bits(2 * PATCH)) * PATCH + (col & (PATCH - 1))
    quarter = (col >> bits(PATCH) & 1) - (row >> bits(m) & 1)
    return split(cosine((n & (size - 1)) * k + quarter * (size // 4), size))


def twist_table(groups, rows):
    n, k = grid_of((rows, 2 * groups))
    count = groups * rows
    return cosine(n * (k & (groups - 1)) - (k >> bits(groups)) * (count // 4), count)


def in_vmem(count):
    return [pl.BlockSpec(memory_space=pltpu.VMEM)] * count


VMEM_LIMIT = 12 * 1024 * 1024
ROOT = math.sqrt(0.5)


AT_ONCE = 8
HALVES = ((0, 1, 7, 2, 6), (4, 3, 5))
ORDER = HALVES[0] + HALVES[1]


def call(kernel, out_shapes, scratch, *args, smem=0):
    return pl.pallas_call(
        kernel,
        in_specs=[pl.BlockSpec(memory_space=pltpu.SMEM)] * smem + in_vmem(len(args) - smem),
        out_specs=in_vmem(len(out_shapes)),
        out_shape=[jax.ShapeDtypeStruct(shape, kind) for shape, kind in out_shapes],
        scratch_shapes=[pltpu.VMEM(shape, kind) for shape, kind in scratch],
        compiler_params=pltpu.CompilerParams(vmem_limit_bytes=VMEM_LIMIT),
    )(*args)


def spread_kernel(image_ref, out_ref, first_ref, last_ref):
    first_ref[...] = image_ref[:, :LANES].T[:HALO]
    last_ref[...] = image_ref[:, image_ref.shape[1] - LANES :].T[LANES - HALO :]
    groups, _, m = out_ref.shape
    width = groups * m
    high = image_ref[...].astype(BF16)
    low = (image_ref[...] - high.astype(F32)).astype(BF16)
    c = lax.broadcasted_iota(jnp.int32, (width, 2 * m), 0)
    place = lax.broadcasted_iota(jnp.int32, (width, 2 * m), 1)
    for v in range(0, groups, 2):
        table = (c == (place & (m - 1)) * groups + (place >> bits(m)) + v).astype(F32).astype(BF16)
        out = jnp.dot(high, table, preferred_element_type=F32) + jnp.dot(low, table, preferred_element_type=F32)
        out_ref[v] = out[:, :m]
        out_ref[v + 1] = out[:, m:]


def rows_forward_kernel(x_ref, high_ref, low_ref, twist_ref, *y_refs, half):
    rows, m = x_ref.shape[1:]
    wavs = len(y_refs)
    part = rows // wavs
    x = [x_ref[i].astype(F32) for i in range(8)]
    e0, e1, f0, f1 = x[0] + x[4], x[0] - x[4], x[2] + x[6], x[2] - x[6]
    g0, g1, h0, h1 = x[1] + x[5], x[1] - x[5], x[3] + x[7], x[3] - x[7]
    gm, gp = (g1 - h1) * ROOT, (g1 + h1) * ROOT
    zero = jnp.zeros_like(e0)
    mixed = {
        0: (e0 + f0 + g0 + h0, zero),
        1: (e1 + gm, -f1 - gp),
        2: (e0 - f0, h0 - g0),
        3: (e1 - gm, f1 - gp),
        4: (e0 + f0 - g0 - h0, zero),
    }
    for spot, k in enumerate(HALVES[half]):
        if k > 4:
            continue
        re, im = mixed[k]
        if k:
            cos_t, sin_t = twist_ref[:, k : k + 1], twist_ref[:, 8 + k : 9 + k]
            re, im = re * cos_t + im * sin_t, im * cos_t - re * sin_t
        both = jnp.concatenate([re, im], 1)
        high = both.astype(BF16)
        low = (both - high.astype(F32)).astype(BF16)
        out = jnp.dot(high_ref[...], high, preferred_element_type=F32)
        out += jnp.dot(high_ref[...], low, preferred_element_type=F32)
        out += jnp.dot(low_ref[...], high, preferred_element_type=F32)
        p_re, p_im, q_re, q_im = out[:rows, :m], out[:rows, m:], out[rows:, :m], out[rows:, m:]
        here = jnp.concatenate([p_re + q_im, p_im - q_re], 1)
        for w in range(wavs):
            y_refs[w][spot] = here[w * part : (w + 1) * part]
        if k in (1, 2, 3):
            there = jnp.concatenate([p_re - q_im, -p_im - q_re], 1)
            there = pltpu.roll(there, rows - 1, 0)
            for w in range(wavs):
                y_refs[w][spot + 1] = there[w * part : (w + 1) * part]


def rows_forward_fast(x, wavs, table, twist, half):
    _, rows, m = x.shape
    kernel = lambda *refs: rows_forward_kernel(*refs, half=half)
    return call(kernel, [((len(HALVES[half]), rows // wavs, 2 * m), F32)] * wavs, [], x, *table, twist)


def shares_kernel(a_ref, b_ref, *refs, wavs):
    y_refs = refs[:wavs]
    high_ref, low_ref, cos_ref, sin_ref, far_ref, near_ref, z_ref, head_ref, rest_ref = refs[wavs:]
    groups, part, double = y_refs[0].shape
    down = z_ref.shape[0]
    wide = 2 * PATCH
    low = 8
    blocks = near_ref.shape[1]
    scale = 1.0 / (8 * down * PATCH)
    for w in range(wavs):
        y = y_refs[w][...].astype(F32).reshape(groups * part, double)
        high = y.astype(BF16)
        head_ref[:, w * double : (w + 1) * double] = high
        rest_ref[:, w * double : (w + 1) * double] = (y - high.astype(F32)).astype(BF16)
    for a in range(0, down, 2):
        spot = (slice(None), pl.ds(a * wide, 2 * wide))
        z = jnp.dot(head_ref[...], high_ref[spot], preferred_element_type=F32)
        z += jnp.dot(rest_ref[...], high_ref[spot], preferred_element_type=F32)
        z += jnp.dot(head_ref[...], low_ref[spot], preferred_element_type=F32)
        z = z * scale
        z_ref[a] = z[:, :wide].reshape(groups, part, wide)
        z_ref[a + 1] = z[:, wide:].reshape(groups, part, wide)
    for core, out_ref in ((1, far_ref), (0, near_ref)):

        @pl.loop(0, 4 * blocks // AT_ONCE)
        def _(step):
            chip, first = step // (blocks // AT_ONCE), step % (blocks // AT_ONCE) * AT_ONCE
            for i in range(AT_ONCE):
                at = first + i
                n = (2 * chip + core) * blocks + at
                start = pl.multiple_of(b_ref[n] * low, low)
                tile = z_ref[a_ref[n], :, pl.ds(start, low), :].reshape(groups * low, wide)
                out_ref[chip, at] = tile * cos_ref[pl.ds(n, 1), :] + pltpu.roll(tile, PATCH, 1) * sin_ref[pl.ds(n, 1), :]


def shares_fast(a_block, b_block, ys, table, cos_k, sin_k):
    groups, part, double = ys[0].shape
    wavs = len(ys)
    width = wavs * double
    blocks = a_block.shape[0] // 8
    out = ((4, blocks, groups * 8, 2 * PATCH), F32)
    scratch = [((width // (2 * PATCH), groups, part, 2 * PATCH), F32)] + [((groups * part, width), BF16)] * 2
    kernel = lambda *refs: shares_kernel(*refs, wavs=wavs)
    return call(kernel, [out, out], scratch, a_block, b_block, *ys, *table, cos_k, sin_k, smem=2)


def gather_kernel(a_ref, b_ref, *refs):
    high_ref, low_ref, cos_ref, sin_ref = refs[5:9]
    y_refs, (g_ref, head_ref) = refs[9:-2], refs[-2:]
    groups, part, double = y_refs[0].shape
    down = g_ref.shape[0]
    wide = 2 * PATCH
    low = 8
    blocks = refs[0].shape[0]
    g_ref[...] = jnp.zeros_like(g_ref)

    def add(term_ref, mask, first):
        tiles = []
        for i in range(AT_ONCE):
            n = mask * blocks + first + i
            tile = term_ref[first + i].astype(F32)
            tiles.append(tile * cos_ref[pl.ds(n, 1), :] - pltpu.roll(tile, PATCH, 1) * sin_ref[pl.ds(n, 1), :])
        for i in range(AT_ONCE):
            n = mask * blocks + first + i
            start = pl.multiple_of(b_ref[n] * low, low)
            g_ref[a_ref[n], :, pl.ds(start, low), :] += tiles[i].reshape(groups, low, wide)

    steps = blocks // AT_ONCE
    for chip in range(4):
        pl.loop(0, steps)(lambda step: add(refs[chip], 2 * chip, step * AT_ONCE))
    pl.loop(0, 4 * steps)(lambda step: add(refs[4].at[step // steps], 2 * (step // steps) + 1, step % steps * AT_ONCE))

    for a in range(down):
        head_ref[:, a * wide : (a + 1) * wide] = g_ref[a].reshape(groups * part, wide).astype(BF16)
    scale = 1.0 / (8 * down * PATCH)
    for w, y_ref in enumerate(y_refs):
        spot = (slice(None), pl.ds(w * double, double))
        y = jnp.dot(head_ref[...], high_ref[spot], preferred_element_type=F32)
        y += jnp.dot(head_ref[...], low_ref[spot], preferred_element_type=F32)
        y_ref[...] = (y * scale).astype(BF16).reshape(groups, part, double)


def gather_fast(a_block, b_block, terms, table, cos_k, sin_k, wavs, part, m, half):
    width = 2 * wavs * m
    groups = len(HALVES[half])
    out = [((groups, part, 2 * m), BF16)] * wavs
    scratch = [((width // (2 * PATCH), groups, part, 2 * PATCH), F32), ((groups * part, width), BF16)]
    return call(gather_kernel, out, scratch, a_block, b_block, *terms, *table, cos_k, sin_k, smem=2)


def untwist(y_refs, spot, k, high_ref, low_ref, twist_ref):
    y = jnp.concatenate([ref[spot] for ref in y_refs], 0)
    rows, m = y.shape[0], y.shape[1] // 2
    out = jnp.dot(high_ref[...], y, preferred_element_type=F32)
    out += jnp.dot(low_ref[...], y, preferred_element_type=F32)
    re, im = out[:rows, :m] - out[rows:, m:], out[:rows, m:] + out[rows:, :m]
    if k:
        cos_t, sin_t = twist_ref[:, k : k + 1], twist_ref[:, 8 + k : 9 + k]
        re, im = re * cos_t - im * sin_t, im * cos_t + re * sin_t
    return re, im


def rows_inverse_first(*refs):
    y_refs, (high_ref, low_ref, twist_ref, out_ref) = refs[:-4], refs[-4:]
    (re4, _), (re3, im3), (re5, im5) = [
        untwist(y_refs, spot, k, high_ref, low_ref, twist_ref) for spot, k in enumerate(HALVES[1])
    ]
    out_ref[0] = re4
    out_ref[1] = re3 + re5
    out_ref[2] = im3 - im5


def rows_inverse_last(*refs):
    y_refs, (first_ref, high_ref, low_ref, twist_ref, x_ref) = refs[:-5], refs[-5:]
    (re0, _), (re1, im1), (re7, im7), (re2, im2), (re6, im6) = [
        untwist(y_refs, spot, k, high_ref, low_ref, twist_ref) for spot, k in enumerate(HALVES[0])
    ]
    re4, r3, i3 = [first_ref[i] for i in range(3)]
    even, odd = re0 + re4, re0 - re4
    r1, r2, i1, i2 = re1 + re7, re2 + re6, im1 - im7, im2 - im6
    rm, ip = (r1 - r3) * ROOT, (i1 + i3) * ROOT
    x_ref[0] = (even + r2 + (r1 + r3)).astype(BF16)
    x_ref[4] = (even + r2 - (r1 + r3)).astype(BF16)
    x_ref[2] = (even - r2 - (i1 - i3)).astype(BF16)
    x_ref[6] = (even - r2 + (i1 - i3)).astype(BF16)
    x_ref[1] = (odd + rm - ip - i2).astype(BF16)
    x_ref[7] = (odd + rm + ip + i2).astype(BF16)
    x_ref[3] = (odd - rm - ip + i2).astype(BF16)
    x_ref[5] = (odd - rm + ip - i2).astype(BF16)


HALO = 8
LANES = 128


def step_kernel(image_ref, grad_ref, spread_ref, out_ref):
    grad = jnp.concatenate([grad_ref[i] for i in range(grad_ref.shape[0])], 1)
    out_ref[...] = image_ref[...] - jnp.dot(grad, spread_ref[...], preferred_element_type=F32)


def edge_kernel(grad_ref, first_ref, last_ref):
    groups, _, m = grad_ref.shape
    row = lax.broadcasted_iota(jnp.int32, (8, m), 0)
    lane = lax.broadcasted_iota(jnp.int32, (8, m), 1)
    pick = (lane == jnp.where(row == 0, 0, m - 1)).astype(F32).astype(BF16)
    for v in range(groups):
        both = lax.dot_general(pick, grad_ref[v], (((1,), (1,)), ((), ())), preferred_element_type=F32)
        first_ref[v : v + 1, :] = both[0:1]
        last_ref[v : v + 1, :] = both[1:2]


def haar_kernel(field_ref, left_ref, right_ref, limit_ref, out_ref, edge_ref, *, bases):
    every, width = field_ref.shape
    rows = 64
    span = width + LANES
    middle = jnp.zeros((LANES - 2 * HALO, every), F32)
    edge_ref[...] = jnp.concatenate([right_ref[...], middle, left_ref[...]], 0).T
    even = lax.broadcasted_iota(jnp.int32, (rows, span), 0) % 2 == 0

    def mix(x, even):
        other = jnp.where(even, pltpu.roll(x, rows - 1, 0), pltpu.roll(x, 1, 0))
        return jnp.where(even, x, -x) + other

    def ahead(x, by):
        return pltpu.roll(x, span - by, 1)

    def behind(x, by):
        return pltpu.roll(x, by, 1)

    def mean(u):
        spot = 0
        level = []
        for period in (2, 4, 8):
            forward = ahead(u, period // 2)
            parts = [u + forward, u - forward]
            limits = []
            for _ in range(0, bases, period):
                limits.append(limit_ref[spot : spot + 1, :])
                spot += 1
            limited = []
            for x in parts if period == 8 else parts[1:]:
                total = None
                for limit in limits:
                    x_soft = x - jnp.minimum(jnp.maximum(x, -limit), limit)
                    total = x_soft if total is None else total + x_soft
                limited.append(total)
            level.append(limited)
            u = parts[0]
        s3, d3 = level[2]
        back = (s3 + d3) + behind(s3 - d3, 4)
        for by, (d,) in ((2, level[1]), (1, level[0])):
            back = back * 0.5
            back = (back + d) + behind(back - d, by)
        return back[:, :width] * (0.25 / bases)

    @pl.loop(0, every // rows)
    def _(step):
        spot = (pl.ds(pl.multiple_of(step * rows, rows), rows), slice(None))
        field = jnp.concatenate([field_ref[spot], edge_ref[spot]], 1)
        out_ref[spot] = mix(mean(mix(field, even)), even[:, :width])


def haar_limits(width, thresholds):
    bases = thresholds.shape[0]
    span = width + LANES
    place = iota(span)
    place = jnp.where(place < width + LANES // 2, place, place - span) + 8
    out = []
    for period in (2, 4, 8):
        scale = math.sqrt(2.0 * period)
        for start in range(0, bases, period):
            index = place % period + start
            limit = jnp.full((span,), 3e38, F32)
            for s in range(start, min(start + period, bases)):
                limit = jnp.where(index == s, thresholds[s] * scale, limit)
            out.append(limit)
    return jnp.stack(out)


def haar_mean(field, halo_left, halo_right, thresholds):
    bases = thresholds.shape[0]
    rows, width = field.shape
    limits = haar_limits(width, thresholds)
    step = LANES
    return pl.pallas_call(
        lambda *refs: haar_kernel(*refs, bases=bases),
        grid=(rows // step,),
        in_specs=[
            pl.BlockSpec((step, width), lambda i: (i, 0)),
            pl.BlockSpec((HALO, step), lambda i: (0, i)),
            pl.BlockSpec((HALO, step), lambda i: (0, i)),
            pl.BlockSpec(limits.shape, lambda i: (0, 0)),
        ],
        out_specs=pl.BlockSpec((step, width), lambda i: (i, 0)),
        out_shape=jax.ShapeDtypeStruct((rows, width), F32),
        scratch_shapes=[pltpu.VMEM((step, LANES), F32)],
        compiler_params=pltpu.CompilerParams(vmem_limit_bytes=VMEM_LIMIT),
        name="haar",
    )(field, halo_left, halo_right, limits)


def phases(owner, a_block, v, rows, img):
    cos_k, sin_k = turns(v, owner[:, None] * rows + a_block[:, None] * PATCH + iota(PATCH)[None, :], img)
    return jnp.concatenate([cos_k, cos_k], 1), jnp.concatenate([sin_k, -sin_k], 1)


def shards_fast(image, kernel_v, kernel_u, measured, dest_owner, patch_slot, thresholds):
    vis = lax.axis_size("vis")
    wavs = lax.axis_size("wav")
    v, w = lax.axis_index("vis"), lax.axis_index("wav")
    rows, cols = image.shape
    img = rows * vis
    m = cols // vis
    across = cols // PATCH
    part = rows // wavs

    def flip(x, mask):
        return lax.ppermute(x, "vis", [(i, i ^ mask) for i in range(vis)])

    def ahead(x, by):
        return lax.ppermute(x, "wav", [(i, (i + by) % wavs) for i in range(wavs)])

    def exchange(parts):
        out = [parts[0]]
        for s in range(1, wavs):
            out.append(ahead(parts[wavs - s], wavs - s))
        return out

    def to_chips(parts):
        out = []
        for chip in (1, 2, 3):
            out.append(flip(parts[chip - 1], 2 * chip))
        return out

    edge = ((HALO, rows), F32)
    x, first_cols, last_cols = call(spread_kernel, [((vis, rows, m), F32), edge, edge], [], image)
    x = x.astype(F16)
    x = lax.all_to_all(x, "vis", split_axis=0, concat_axis=0, tiled=True)
    x = x.astype(F32)
    table, table_back = column_table(wavs, m, w, False), column_table(wavs, m, w, True)

    forward_table, twist = row_table(rows, w * part), twist_table(vis, rows)
    sent, spectra = [], []
    for half in (0, 1):
        y = rows_forward_fast(x, wavs, forward_table, twist, half)
        sent.append([part_y.astype(F16) for part_y in y])
        spectra.append(exchange(sent[half]))
    spectra[0], _ = lax.optimization_barrier((spectra[0], sent[1]))

    ids = jnp.stack([dest_owner[:, 0], patch_slot])
    ids, _ = lax.optimization_barrier((ids, sent[1]))
    for mask in (1, 2, 4):
        ids = jnp.concatenate([ids, flip(ids, mask)], 1)
    sky, _ = lax.optimization_barrier(((first_cols, last_cols), sent[1]))
    sky_right, sky_left = ahead(sky[0], wavs - 1), ahead(sky[1], 1)
    owner, slot = ids[0], ids[1]
    a_block, b_block = slot // across, slot % across
    cos_k, sin_k = phases(owner, a_block, v, rows, img)

    patches = []
    for half in (0, 1):
        y = []
        for part_y in spectra[half]:
            y.append(part_y.astype(F32))
        far, near = shares_fast(a_block, b_block, y, table, cos_k, sin_k)
        near = near + flip(far.astype(F16), 1).astype(F32)
        ready = [near[0]] + [near[chip].astype(F16) for chip in (1, 2, 3)]
        if half == 0:
            spectra[1], ready = lax.optimization_barrier((spectra[1], ready))
        total = ready[0]
        for came in to_chips(ready[1:]):
            total = total + came.astype(F32)
        patches.append(total.astype(BF16))

    place = np.arange(PATCH)
    chosen = (place % 8) * vis + np.asarray(ORDER)[place // 8]
    pick = jnp.asarray(chosen[:, None] == place[None, :], BF16)
    side = jnp.einsum("pb,nbt->npt", pick, kernel_u, preferred_element_type=F32)
    cut = 8 * len(HALVES[0])
    sides = [side[:, :cut], side[:, cut:]]
    model = 0.0
    for patch, side in zip(patches, sides):
        part_re = jnp.einsum("nba,nat->nbt", patch[..., :PATCH], kernel_v, preferred_element_type=F32)
        part_im = jnp.einsum("nba,nat->nbt", patch[..., PATCH:], kernel_v, preferred_element_type=F32)
        model = model + jnp.stack([jnp.sum(part_re * side, 1), jnp.sum(part_im * side, 1)], 1)
    misfit = model - measured.astype(F32)

    grads = {}
    for half in (1, 0):
        side = sides[half]
        w_re = (misfit[:, 0, None, :] * side).astype(BF16)
        w_im = (misfit[:, 1, None, :] * side).astype(BF16)
        term_re = jnp.einsum("nbt,nat->nba", w_re, kernel_v, preferred_element_type=F32)
        term_im = jnp.einsum("nbt,nat->nba", w_im, kernel_v, preferred_element_type=F32)
        terms = jnp.concatenate([term_re, term_im], -1).astype(BF16)
        if half == 0:
            terms, chips = lax.optimization_barrier((terms, chips))
        chips = [terms] + to_chips([terms] * 3)
        other = flip(jnp.stack(chips), 1)
        grad = gather_fast(a_block, b_block, chips + [other], table_back, cos_k, sin_k, wavs, part, m, half)
        grads[half] = exchange(grad)

    back_table = row_table_back(rows, w * part)
    first = call(rows_inverse_first, [((3, rows, m), F32)], [], *grads[1], *back_table, twist)
    grad = call(rows_inverse_last, [((vis, rows, m), BF16)], [], *grads[0], *first, *back_table, twist)[0]
    grad = lax.all_to_all(grad, "vis", split_axis=0, concat_axis=0, tiled=True)
    back = spread_matrix(vis, m).T.astype(BF16)
    grad_edges = call(edge_kernel, [edge, edge], [], grad)
    right = ahead(grad_edges[0], wavs - 1)
    left = ahead(grad_edges[1], 1)
    shifted = call(step_kernel, [((rows, cols), F32)], [], image, grad, back)[0]
    return haar_mean(shifted, sky_left - left, sky_right - right, thresholds), misfit


def shards(image, kernel_v, kernel_u, measured, dest_owner, patch_slot, thresholds):
    vis = lax.axis_size("vis")
    wavs = lax.axis_size("wav")
    v = lax.axis_index("vis")
    rows, cols = image.shape
    img = rows * vis
    m = cols // vis
    down = rows // PATCH
    across = cols // PATCH
    blocks = kernel_v.shape[0]
    low = PATCH // vis
    part = rows // wavs
    if vis == 8 and m == LANES and low == 8 and part % 8 == 0 and rows & (rows - 1) == 0:
        return shards_fast(image, kernel_v, kernel_u, measured, dest_owner, patch_slot, thresholds)
    spread = spread_matrix(vis, m)

    ids = jnp.concatenate([dest_owner, patch_slot[:, None]], 1)
    ids = lax.all_gather(ids, "vis", axis=0, tiled=True)
    owner, slot = ids[:, 0], ids[:, 1]
    a_block, b_block = slot // across, slot % across

    x = jnp.dot(image, spread, precision=HIGH).astype(F16)
    x = x.reshape(rows, vis, m).transpose(1, 0, 2)
    x = lax.all_to_all(x, "vis", split_axis=0, concat_axis=0, tiled=True).astype(F32)
    y = rows_forward(x, vis).astype(F16)
    y = y.reshape(vis, wavs, part, 2 * m).transpose(1, 0, 2, 3)
    y = lax.all_to_all(y, "wav", split_axis=0, concat_axis=0, tiled=True).astype(F32)
    cos_k, sin_k = turns(v, owner[:, None] * rows + a_block[:, None] * PATCH + iota(PATCH)[None, :], img)
    cos_k = jnp.concatenate([cos_k, cos_k], 1)
    sin_k = jnp.concatenate([sin_k, -sin_k], 1)
    y = y.transpose(1, 2, 0, 3).reshape(cols, 2 * wavs * m)
    table = column_matrix(wavs, m, down, 1.0 / img)
    z = jnp.dot(y, table, precision=HIGH)
    z = z.reshape(vis, across, low, down, 2 * PATCH)
    tiles = z[:, b_block, :, a_block, :].reshape(vis * blocks, PATCH, 2 * PATCH)
    tiles = tiles * cos_k[:, None] + jnp.roll(tiles, PATCH, axis=2) * sin_k[:, None]
    tiles = lax.all_to_all(tiles.astype(F16), "vis", split_axis=0, concat_axis=0, tiled=True)
    patch = jnp.sum(tiles.reshape(vis, blocks, PATCH, 2 * PATCH).astype(F32), 0).astype(BF16)

    side_u = kernel_u.reshape(blocks, low, vis, -1).transpose(0, 2, 1, 3).reshape(kernel_u.shape)
    part_re = jnp.einsum("nba,nat->nbt", patch[..., :PATCH], kernel_v, preferred_element_type=F32)
    part_im = jnp.einsum("nba,nat->nbt", patch[..., PATCH:], kernel_v, preferred_element_type=F32)
    side = side_u.astype(F32)
    misfit = jnp.stack([jnp.sum(part_re * side, 1), jnp.sum(part_im * side, 1)], 1) - measured.astype(F32)
    w_re = (misfit[:, 0, None, :] * side).astype(BF16)
    w_im = (misfit[:, 1, None, :] * side).astype(BF16)
    term_re = jnp.einsum("nbt,nat->nba", w_re, kernel_v, preferred_element_type=F32)
    term_im = jnp.einsum("nbt,nat->nba", w_im, kernel_v, preferred_element_type=F32)
    terms = jnp.concatenate([term_re, term_im], -1).astype(BF16)

    terms = lax.all_gather(terms, "vis", axis=0, tiled=True)
    terms = terms.astype(F32)
    terms = terms * cos_k[:, None] - jnp.roll(terms, PATCH, axis=2) * sin_k[:, None]
    terms = terms.reshape(vis * blocks, vis, low, 2 * PATCH)
    flat = jnp.zeros((across * down, vis, low, 2 * PATCH), F32).at[b_block * down + a_block].add(terms)
    grad = flat.reshape(across, down, vis, low, 2 * PATCH).transpose(2, 0, 3, 1, 4).reshape(cols, 2 * rows)
    grad = lax.dot_general(grad, table, (((1,), (1,)), ((), ())), precision=HIGH).astype(BF16)
    grad = grad.reshape(vis, part, wavs, 2 * m).transpose(2, 0, 1, 3)
    grad = lax.all_to_all(grad, "wav", split_axis=0, concat_axis=0, tiled=True)
    grad = grad.astype(F32).transpose(1, 0, 2, 3).reshape(vis, rows, 2 * m)
    grad = rows_inverse(grad, vis).astype(BF16)
    grad = lax.all_to_all(grad, "vis", split_axis=0, concat_axis=0, tiled=True)
    grad = grad.transpose(1, 0, 2).reshape(rows, cols)
    grad = lax.dot_general(grad, spread.astype(BF16), (((1,), (1,)), ((), ())), preferred_element_type=F32)
    shifted = image - grad
    right = lax.ppermute(shifted[:, :HALO].T, "wav", [(i, (i - 1) % wavs) for i in range(wavs)])
    left = lax.ppermute(shifted[:, -HALO:].T, "wav", [(i, (i + 1) % wavs) for i in range(wavs)])
    return haar_mean(shifted, left, right, thresholds), misfit


def solution(mesh):
    both = ("vis", "wav")
    in_specs = (
        P("vis", "wav"),
        P(both, None, None),
        P(both, None, None),
        P(both, None, None),
        P(both, None),
        P(both),
        P(),
    )
    out_specs = (P("vis", "wav"), P(both, None, None))
    return jax.shard_map(shards, mesh=mesh, in_specs=in_specs, out_specs=out_specs, check_vma=False)
```

```python
import math

import jax
import jax.numpy as jnp
import numpy as np
from jax import lax
from jax.experimental import pallas as pl
from jax.experimental.pallas import tpu as pltpu
from jax.sharding import PartitionSpec as P


PATCH = 64
HIGH = lax.Precision.HIGH
F32 = jnp.float32
BF16 = jnp.bfloat16
F16 = jnp.float16


def turns(rows, cols, period):
    angle = (rows * cols % period).astype(F32) * (2.0 * math.pi / period)
    return jnp.cos(angle), jnp.sin(angle)


def iota(size):
    return jnp.arange(size, dtype=jnp.int32)


def spread_matrix(groups, size):
    width = groups * size
    c = iota(width)
    return (c[:, None] == (c % size * groups + c // size)[None, :]).astype(F32)


def rows_forward(x, groups):
    rows = x.shape[1]
    count = groups * rows
    cos_g, sin_g = (np.cos(2 * np.pi * np.outer(np.arange(groups), np.arange(groups)) / groups), np.sin(2 * np.pi * np.outer(np.arange(groups), np.arange(groups)) / groups))
    mixed_re = jnp.einsum("kv,vnm->knm", jnp.asarray(cos_g, F32), x, precision=HIGH)
    mixed_im = -jnp.einsum("kv,vnm->knm", jnp.asarray(sin_g, F32), x, precision=HIGH)
    cos_t, sin_t = turns(iota(groups)[:, None], iota(rows)[None, :], count)
    cos_t, sin_t = cos_t[:, :, None], sin_t[:, :, None]
    both = jnp.concatenate([mixed_re * cos_t + mixed_im * sin_t, mixed_im * cos_t - mixed_re * sin_t], -1)
    cos_r, sin_r = turns(iota(rows)[:, None], iota(rows)[None, :], rows)
    p = jnp.einsum("kn,vnm->vkm", cos_r, both, precision=HIGH)
    q = jnp.einsum("kn,vnm->vkm", sin_r, both, precision=HIGH)
    m = x.shape[2]
    return jnp.concatenate([p[..., :m] + q[..., m:], p[..., m:] - q[..., :m]], -1)


def rows_inverse(y, groups):
    rows = y.shape[1]
    m = y.shape[2] // 2
    count = groups * rows
    cos_r, sin_r = turns(iota(rows)[:, None], iota(rows)[None, :], rows)
    p = jnp.einsum("kn,vnm->vkm", cos_r, y, precision=HIGH)
    q = jnp.einsum("kn,vnm->vkm", sin_r, y, precision=HIGH)
    re, im = p[..., :m] - q[..., m:], p[..., m:] + q[..., :m]
    cos_t, sin_t = turns(iota(groups)[:, None], iota(rows)[None, :], count)
    cos_t, sin_t = cos_t[:, :, None], sin_t[:, :, None]
    re, im = re * cos_t - im * sin_t, im * cos_t + re * sin_t
    cos_g, sin_g = (np.cos(2 * np.pi * np.outer(np.arange(groups), np.arange(groups)) / groups), np.sin(2 * np.pi * np.outer(np.arange(groups), np.arange(groups)) / groups))
    out = jnp.einsum("vk,knm->vnm", jnp.asarray(cos_g, F32), re, precision=HIGH)
    return out - jnp.einsum("vk,knm->vnm", jnp.asarray(sin_g, F32), im, precision=HIGH)


def column_matrix(wavs, m, down, scale):
    size = wavs * m
    cos_c, sin_c = turns(iota(size)[:, None], iota(size)[None, :], size)
    cos_c = (cos_c * scale).reshape(wavs, 1, m, down, 1, PATCH)
    sin_c = (sin_c * scale).reshape(wavs, 1, m, down, 1, PATCH)
    from_re = jnp.concatenate([cos_c, -sin_c], 4)
    from_im = jnp.concatenate([sin_c, cos_c], 4)
    return jnp.concatenate([from_re, from_im], 1).reshape(2 * size, 2 * size)


def split(x):
    high = lax.reduce_precision(x, 8, 7)
    return high.astype(BF16), (x - high).astype(BF16)


def bits(size):
    return size.bit_length() - 1


def cosine(count, period):
    part = (count & (period - 1)).astype(F32) * (1.0 / period)
    part = 0.25 - jnp.abs(part - jnp.where(part > 0.5, 1.0, 0.0))
    square = part * part
    terms = [(-1) ** i * (2 * math.pi) ** (2 * i + 1) / math.factorial(2 * i + 1) for i in range(7)]
    value = jnp.full_like(part, terms[-1])
    for term in terms[-2::-1]:
        value = value * square + term
    return value * part


def grid_of(shape):
    return [lax.broadcasted_iota(jnp.int32, shape, axis) for axis in (0, 1)]


def row_table(size, first):
    k, n = grid_of((2 * size, size))
    return split(cosine(((k + first) & (size - 1)) * n - (k >> bits(size)) * (size // 4), size))


def row_table_back(size, first):
    r, k = grid_of((2 * size, size))
    return split(cosine(((k + first) & (size - 1)) * (r & (size - 1)) - (r >> bits(size)) * (size // 4), size))


def column_table(wavs, m, first, turned):
    size = wavs * m
    row, col = grid_of((2 * size, 2 * size))[:: -1 if turned else 1]
    n = (row >> bits(2 * m)) * m + (row & (m - 1)) + first * m
    k = (col >> bits(2 * PATCH)) * PATCH + (col & (PATCH - 1))
    quarter = (col >> bits(PATCH) & 1) - (row >> bits(m) & 1)
    return split(cosine((n & (size - 1)) * k + quarter * (size // 4), size))


def twist_table(groups, rows):
    n, k = grid_of((rows, 2 * groups))
    count = groups * rows
    return cosine(n * (k & (groups - 1)) - (k >> bits(groups)) * (count // 4), count)


def in_vmem(count):
    return [pl.BlockSpec(memory_space=pltpu.VMEM)] * count


VMEM_LIMIT = 12 * 1024 * 1024
ROOT = math.sqrt(0.5)


AT_ONCE = 8
HALVES = ((0, 1, 7, 2, 6), (4, 3, 5))
ORDER = HALVES[0] + HALVES[1]


def call(kernel, out_shapes, scratch, *args, smem=0):
    return pl.pallas_call(
        kernel,
        in_specs=[pl.BlockSpec(memory_space=pltpu.SMEM)] * smem + in_vmem(len(args) - smem),
        out_specs=in_vmem(len(out_shapes)),
        out_shape=[jax.ShapeDtypeStruct(shape, kind) for shape, kind in out_shapes],
        scratch_shapes=[pltpu.VMEM(shape, kind) for shape, kind in scratch],
        compiler_params=pltpu.CompilerParams(vmem_limit_bytes=VMEM_LIMIT),
    )(*args)


def spread_kernel(image_ref, out_ref, first_ref, last_ref):
    first_ref[...] = image_ref[:, :LANES].T[:HALO]
    last_ref[...] = image_ref[:, image_ref.shape[1] - LANES :].T[LANES - HALO :]
    groups, _, m = out_ref.shape
    width = groups * m
    high = image_ref[...].astype(BF16)
    low = (image_ref[...] - high.astype(F32)).astype(BF16)
    c = lax.broadcasted_iota(jnp.int32, (width, 2 * m), 0)
    place = lax.broadcasted_iota(jnp.int32, (width, 2 * m), 1)
    for v in range(0, groups, 2):
        table = (c == (place & (m - 1)) * groups + (place >> bits(m)) + v).astype(F32).astype(BF16)
        out = jnp.dot(high, table, preferred_element_type=F32) + jnp.dot(low, table, preferred_element_type=F32)
        out_ref[v] = out[:, :m]
        out_ref[v + 1] = out[:, m:]


def rows_forward_kernel(x_ref, high_ref, low_ref, twist_ref, *y_refs, half):
    rows, m = x_ref.shape[1:]
    wavs = len(y_refs)
    part = rows // wavs
    x = [x_ref[i].astype(F32) for i in range(8)]
    e0, e1, f0, f1 = x[0] + x[4], x[0] - x[4], x[2] + x[6], x[2] - x[6]
    g0, g1, h0, h1 = x[1] + x[5], x[1] - x[5], x[3] + x[7], x[3] - x[7]
    gm, gp = (g1 - h1) * ROOT, (g1 + h1) * ROOT
    zero = jnp.zeros_like(e0)
    mixed = {
        0: (e0 + f0 + g0 + h0, zero),
        1: (e1 + gm, -f1 - gp),
        2: (e0 - f0, h0 - g0),
        3: (e1 - gm, f1 - gp),
        4: (e0 + f0 - g0 - h0, zero),
    }
    for spot, k in enumerate(HALVES[half]):
        if k > 4:
            continue
        re, im = mixed[k]
        if k:
            cos_t, sin_t = twist_ref[:, k : k + 1], twist_ref[:, 8 + k : 9 + k]
            re, im = re * cos_t + im * sin_t, im * cos_t - re * sin_t
        both = jnp.concatenate([re, im], 1)
        high = both.astype(BF16)
        low = (both - high.astype(F32)).astype(BF16)
        out = jnp.dot(high_ref[...], high, preferred_element_type=F32)
        out += jnp.dot(high_ref[...], low, preferred_element_type=F32)
        out += jnp.dot(low_ref[...], high, preferred_element_type=F32)
        p_re, p_im, q_re, q_im = out[:rows, :m], out[:rows, m:], out[rows:, :m], out[rows:, m:]
        here = jnp.concatenate([p_re + q_im, p_im - q_re], 1)
        for w in range(wavs):
            y_refs[w][spot] = here[w * part : (w + 1) * part]
        if k in (1, 2, 3):
            there = jnp.concatenate([p_re - q_im, -p_im - q_re], 1)
            there = pltpu.roll(there, rows - 1, 0)
            for w in range(wavs):
                y_refs[w][spot + 1] = there[w * part : (w + 1) * part]


def rows_forward_fast(x, wavs, table, twist, half):
    _, rows, m = x.shape
    kernel = lambda *refs: rows_forward_kernel(*refs, half=half)
    return call(kernel, [((len(HALVES[half]), rows // wavs, 2 * m), F32)] * wavs, [], x, *table, twist)


def shares_kernel(a_ref, b_ref, *refs, wavs):
    y_refs = refs[:wavs]
    high_ref, low_ref, cos_ref, sin_ref, far_ref, near_ref, z_ref, head_ref, rest_ref = refs[wavs:]
    groups, part, double = y_refs[0].shape
    down = z_ref.shape[0]
    wide = 2 * PATCH
    low = 8
    blocks = near_ref.shape[1]
    scale = 1.0 / (8 * down * PATCH)
    for w in range(wavs):
        y = y_refs[w][...].astype(F32).reshape(groups * part, double)
        high = y.astype(BF16)
        head_ref[:, w * double : (w + 1) * double] = high
        rest_ref[:, w * double : (w + 1) * double] = (y - high.astype(F32)).astype(BF16)
    for a in range(0, down, 2):
        spot = (slice(None), pl.ds(a * wide, 2 * wide))
        z = jnp.dot(head_ref[...], high_ref[spot], preferred_element_type=F32)
        z += jnp.dot(rest_ref[...], high_ref[spot], preferred_element_type=F32)
        z += jnp.dot(head_ref[...], low_ref[spot], preferred_element_type=F32)
        z = z * scale
        z_ref[a] = z[:, :wide].reshape(groups, part, wide)
        z_ref[a + 1] = z[:, wide:].reshape(groups, part, wide)
    for core, out_ref in ((1, far_ref), (0, near_ref)):

        @pl.loop(0, 4 * blocks // AT_ONCE)
        def _(step):
            chip, first = step // (blocks // AT_ONCE), step % (blocks // AT_ONCE) * AT_ONCE
            for i in range(AT_ONCE):
                at = first + i
                n = (2 * chip + core) * blocks + at
                start = pl.multiple_of(b_ref[n] * low, low)
                tile = z_ref[a_ref[n], :, pl.ds(start, low), :].reshape(groups * low, wide)
                out_ref[chip, at] = tile * cos_ref[pl.ds(n, 1), :] + pltpu.roll(tile, PATCH, 1) * sin_ref[pl.ds(n, 1), :]


def shares_fast(a_block, b_block, ys, table, cos_k, sin_k):
    groups, part, double = ys[0].shape
    wavs = len(ys)
    width = wavs * double
    blocks = a_block.shape[0] // 8
    out = ((4, blocks, groups * 8, 2 * PATCH), F32)
    scratch = [((width // (2 * PATCH), groups, part, 2 * PATCH), F32)] + [((groups * part, width), BF16)] * 2
    kernel = lambda *refs: shares_kernel(*refs, wavs=wavs)
    return call(kernel, [out, out], scratch, a_block, b_block, *ys, *table, cos_k, sin_k, smem=2)


def gather_kernel(a_ref, b_ref, *refs):
    high_ref, low_ref, cos_ref, sin_ref = refs[5:9]
    y_refs, (g_ref, head_ref) = refs[9:-2], refs[-2:]
    groups, part, double = y_refs[0].shape
    down = g_ref.shape[0]
    wide = 2 * PATCH
    low = 8
    blocks = refs[0].shape[0]
    g_ref[...] = jnp.zeros_like(g_ref)

    def add(term_ref, mask, first):
        tiles = []
        for i in range(AT_ONCE):
            n = mask * blocks + first + i
            tile = term_ref[first + i].astype(F32)
            tiles.append(tile * cos_ref[pl.ds(n, 1), :] - pltpu.roll(tile, PATCH, 1) * sin_ref[pl.ds(n, 1), :])
        for i in range(AT_ONCE):
            n = mask * blocks + first + i
            start = pl.multiple_of(b_ref[n] * low, low)
            g_ref[a_ref[n], :, pl.ds(start, low), :] += tiles[i].reshape(groups, low, wide)

    steps = blocks // AT_ONCE
    for chip in range(4):
        pl.loop(0, steps)(lambda step: add(refs[chip], 2 * chip, step * AT_ONCE))
    pl.loop(0, 4 * steps)(lambda step: add(refs[4].at[step // steps], 2 * (step // steps) + 1, step % steps * AT_ONCE))

    for a in range(down):
        head_ref[:, a * wide : (a + 1) * wide] = g_ref[a].reshape(groups * part, wide).astype(BF16)
    scale = 1.0 / (8 * down * PATCH)
    for w, y_ref in enumerate(y_refs):
        spot = (slice(None), pl.ds(w * double, double))
        y = jnp.dot(head_ref[...], high_ref[spot], preferred_element_type=F32)
        y += jnp.dot(head_ref[...], low_ref[spot], preferred_element_type=F32)
        y_ref[...] = (y * scale).astype(BF16).reshape(groups, part, double)


def gather_fast(a_block, b_block, terms, table, cos_k, sin_k, wavs, part, m, half):
    width = 2 * wavs * m
    groups = len(HALVES[half])
    out = [((groups, part, 2 * m), BF16)] * wavs
    scratch = [((width // (2 * PATCH), groups, part, 2 * PATCH), F32), ((groups * part, width), BF16)]
    return call(gather_kernel, out, scratch, a_block, b_block, *terms, *table, cos_k, sin_k, smem=2)


def untwist(y_refs, spot, k, high_ref, low_ref, twist_ref):
    y = jnp.concatenate([ref[spot] for ref in y_refs], 0)
    rows, m = y.shape[0], y.shape[1] // 2
    out = jnp.dot(high_ref[...], y, preferred_element_type=F32)
    out += jnp.dot(low_ref[...], y, preferred_element_type=F32)
    re, im = out[:rows, :m] - out[rows:, m:], out[:rows, m:] + out[rows:, :m]
    if k:
        cos_t, sin_t = twist_ref[:, k : k + 1], twist_ref[:, 8 + k : 9 + k]
        re, im = re * cos_t - im * sin_t, im * cos_t + re * sin_t
    return re, im


def rows_inverse_first(*refs):
    y_refs, (high_ref, low_ref, twist_ref, out_ref) = refs[:-4], refs[-4:]
    (re4, _), (re3, im3), (re5, im5) = [
        untwist(y_refs, spot, k, high_ref, low_ref, twist_ref) for spot, k in enumerate(HALVES[1])
    ]
    out_ref[0] = re4
    out_ref[1] = re3 + re5
    out_ref[2] = im3 - im5


def rows_inverse_last(*refs):
    y_refs, (first_ref, high_ref, low_ref, twist_ref, x_ref) = refs[:-5], refs[-5:]
    (re0, _), (re1, im1), (re7, im7), (re2, im2), (re6, im6) = [
        untwist(y_refs, spot, k, high_ref, low_ref, twist_ref) for spot, k in enumerate(HALVES[0])
    ]
    re4, r3, i3 = [first_ref[i] for i in range(3)]
    even, odd = re0 + re4, re0 - re4
    r1, r2, i1, i2 = re1 + re7, re2 + re6, im1 - im7, im2 - im6
    rm, ip = (r1 - r3) * ROOT, (i1 + i3) * ROOT
    x_ref[0] = (even + r2 + (r1 + r3)).astype(BF16)
    x_ref[4] = (even + r2 - (r1 + r3)).astype(BF16)
    x_ref[2] = (even - r2 - (i1 - i3)).astype(BF16)
    x_ref[6] = (even - r2 + (i1 - i3)).astype(BF16)
    x_ref[1] = (odd + rm - ip - i2).astype(BF16)
    x_ref[7] = (odd + rm + ip + i2).astype(BF16)
    x_ref[3] = (odd - rm - ip + i2).astype(BF16)
    x_ref[5] = (odd - rm + ip - i2).astype(BF16)


HALO = 8
LANES = 128


def step_kernel(image_ref, grad_ref, out_ref):
    groups, _, m = grad_ref.shape
    width = groups * m
    grad = jnp.concatenate([grad_ref[i] for i in range(groups)], 1)
    wide = 2 * LANES
    place = lax.broadcasted_iota(jnp.int32, (width, wide), 0)
    column = (place & (m - 1)) * groups + (place >> bits(m))
    lane = lax.broadcasted_iota(jnp.int32, (width, wide), 1)
    for start in range(0, width, wide):
        spot = (slice(None), slice(start, start + wide))
        table = (column == lane + start).astype(F32).astype(BF16)
        out_ref[spot] = image_ref[spot] - jnp.dot(grad, table, preferred_element_type=F32)


def edge_kernel(grad_ref, first_ref, last_ref):
    groups, _, m = grad_ref.shape
    row = lax.broadcasted_iota(jnp.int32, (8, m), 0)
    lane = lax.broadcasted_iota(jnp.int32, (8, m), 1)
    pick = (lane == jnp.where(row == 0, 0, m - 1)).astype(F32).astype(BF16)
    for v in range(groups):
        both = lax.dot_general(pick, grad_ref[v], (((1,), (1,)), ((), ())), preferred_element_type=F32)
        first_ref[v : v + 1, :] = both[0:1]
        last_ref[v : v + 1, :] = both[1:2]


def haar_kernel(field_ref, left_ref, right_ref, limit_ref, out_ref, edge_ref, *, bases):
    every, width = field_ref.shape
    rows = 64
    span = width + LANES
    middle = jnp.zeros((LANES - 2 * HALO, every), F32)
    edge_ref[...] = jnp.concatenate([right_ref[...], middle, left_ref[...]], 0).T
    even = lax.broadcasted_iota(jnp.int32, (rows, span), 0) % 2 == 0

    def mix(x, even):
        other = jnp.where(even, pltpu.roll(x, rows - 1, 0), pltpu.roll(x, 1, 0))
        return jnp.where(even, x, -x) + other

    def ahead(x, by):
        return pltpu.roll(x, span - by, 1)

    def behind(x, by):
        return pltpu.roll(x, by, 1)

    def mean(u):
        spot = 0
        level = []
        for period in (2, 4, 8):
            forward = ahead(u, period // 2)
            parts = [u + forward, u - forward]
            limits = []
            for _ in range(0, bases, period):
                limits.append(limit_ref[spot : spot + 1, :])
                spot += 1
            limited = []
            for x in parts if period == 8 else parts[1:]:
                total = None
                for limit in limits:
                    x_soft = x - jnp.minimum(jnp.maximum(x, -limit), limit)
                    total = x_soft if total is None else total + x_soft
                limited.append(total)
            level.append(limited)
            u = parts[0]
        s3, d3 = level[2]
        back = (s3 + d3) + behind(s3 - d3, 4)
        for by, (d,) in ((2, level[1]), (1, level[0])):
            back = back * 0.5
            back = (back + d) + behind(back - d, by)
        return back[:, :width] * (0.25 / bases)

    @pl.loop(0, every // rows)
    def _(step):
        spot = (pl.ds(pl.multiple_of(step * rows, rows), rows), slice(None))
        field = jnp.concatenate([field_ref[spot], edge_ref[spot]], 1)
        out_ref[spot] = mix(mean(mix(field, even)), even[:, :width])


def haar_limits(width, thresholds):
    bases = thresholds.shape[0]
    span = width + LANES
    place = iota(span)
    place = jnp.where(place < width + LANES // 2, place, place - span) + 8
    out = []
    for period in (2, 4, 8):
        scale = math.sqrt(2.0 * period)
        for start in range(0, bases, period):
            index = place % period + start
            limit = jnp.full((span,), 3e38, F32)
            for s in range(start, min(start + period, bases)):
                limit = jnp.where(index == s, thresholds[s] * scale, limit)
            out.append(limit)
    return jnp.stack(out)


def haar_mean(field, halo_left, halo_right, thresholds):
    bases = thresholds.shape[0]
    rows, width = field.shape
    limits = haar_limits(width, thresholds)
    step = LANES
    return pl.pallas_call(
        lambda *refs: haar_kernel(*refs, bases=bases),
        grid=(rows // step,),
        in_specs=[
            pl.BlockSpec((step, width), lambda i: (i, 0)),
            pl.BlockSpec((HALO, step), lambda i: (0, i)),
            pl.BlockSpec((HALO, step), lambda i: (0, i)),
            pl.BlockSpec(limits.shape, lambda i: (0, 0)),
        ],
        out_specs=pl.BlockSpec((step, width), lambda i: (i, 0)),
        out_shape=jax.ShapeDtypeStruct((rows, width), F32),
        scratch_shapes=[pltpu.VMEM((step, LANES), F32)],
        compiler_params=pltpu.CompilerParams(vmem_limit_bytes=VMEM_LIMIT),
        name="haar",
    )(field, halo_left, halo_right, limits)


def phases(owner, a_block, v, rows, img):
    cos_k, sin_k = turns(v, owner[:, None] * rows + a_block[:, None] * PATCH + iota(PATCH)[None, :], img)
    return jnp.concatenate([cos_k, cos_k], 1), jnp.concatenate([sin_k, -sin_k], 1)


def shards_fast(image, kernel_v, kernel_u, measured, dest_owner, patch_slot, thresholds):
    vis = lax.axis_size("vis")
    wavs = lax.axis_size("wav")
    v, w = lax.axis_index("vis"), lax.axis_index("wav")
    rows, cols = image.shape
    img = rows * vis
    m = cols // vis
    across = cols // PATCH
    part = rows // wavs

    def flip(x, mask):
        return lax.ppermute(x, "vis", [(i, i ^ mask) for i in range(vis)])

    def ahead(x, by):
        return lax.ppermute(x, "wav", [(i, (i + by) % wavs) for i in range(wavs)])

    def exchange(parts):
        out = [parts[0]]
        for s in range(1, wavs):
            out.append(ahead(parts[wavs - s], wavs - s))
        return out

    def to_chips(parts):
        out = []
        for chip in (1, 2, 3):
            out.append(flip(parts[chip - 1], 2 * chip))
        return out

    edge = ((HALO, rows), F32)
    x, first_cols, last_cols = call(spread_kernel, [((vis, rows, m), F32), edge, edge], [], image)
    x = x.astype(F16)
    x = lax.all_to_all(x, "vis", split_axis=0, concat_axis=0, tiled=True)
    x = x.astype(F32)
    table, table_back = column_table(wavs, m, w, False), column_table(wavs, m, w, True)

    forward_table, twist = row_table(rows, w * part), twist_table(vis, rows)
    sent, spectra = [], []
    for half in (0, 1):
        y = rows_forward_fast(x, wavs, forward_table, twist, half)
        sent.append([part_y.astype(F16) for part_y in y])
        spectra.append(exchange(sent[half]))

    ids = jnp.stack([dest_owner[:, 0], patch_slot])
    ids, _ = lax.optimization_barrier((ids, sent[1]))
    for mask in (1, 2, 4):
        ids = jnp.concatenate([ids, flip(ids, mask)], 1)
    sky, _ = lax.optimization_barrier(((first_cols, last_cols), sent[1]))
    sky_right, sky_left = ahead(sky[0], wavs - 1), ahead(sky[1], 1)
    owner, slot = ids[0], ids[1]
    a_block, b_block = slot // across, slot % across
    cos_k, sin_k = phases(owner, a_block, v, rows, img)

    patches = []
    for half in (0, 1):
        y = []
        for part_y in spectra[half]:
            y.append(part_y.astype(F32))
        far, near = shares_fast(a_block, b_block, y, table, cos_k, sin_k)
        near = near + flip(far.astype(F16), 1).astype(F32)
        ready = [near[0]] + [near[chip].astype(F16) for chip in (1, 2, 3)]
        came = to_chips(ready[1:])
        patches.append(sum([part_sum.astype(F32) for part_sum in came], ready[0]).astype(BF16))

    place = np.arange(PATCH)
    chosen = (place % 8) * vis + np.asarray(ORDER)[place // 8]
    pick = jnp.asarray(chosen[:, None] == place[None, :], BF16)
    side = jnp.einsum("pb,nbt->npt", pick, kernel_u, preferred_element_type=F32)
    cut = 8 * len(HALVES[0])
    sides = [side[:, :cut], side[:, cut:]]
    model = 0.0
    for patch, side in zip(patches, sides):
        part_re = jnp.einsum("nba,nat->nbt", patch[..., :PATCH], kernel_v, preferred_element_type=F32)
        part_im = jnp.einsum("nba,nat->nbt", patch[..., PATCH:], kernel_v, preferred_element_type=F32)
        model = model + jnp.stack([jnp.sum(part_re * side, 1), jnp.sum(part_im * side, 1)], 1)
    misfit = model - measured.astype(F32)

    grads = {}
    for half in (1, 0):
        side = sides[half]
        w_re = (misfit[:, 0, None, :] * side).astype(BF16)
        w_im = (misfit[:, 1, None, :] * side).astype(BF16)
        term_re = jnp.einsum("nbt,nat->nba", w_re, kernel_v, preferred_element_type=F32)
        term_im = jnp.einsum("nbt,nat->nba", w_im, kernel_v, preferred_element_type=F32)
        terms = jnp.concatenate([term_re, term_im], -1).astype(BF16)
        if half == 0:
            terms, chips = lax.optimization_barrier((terms, chips))
        chips = [terms] + to_chips([terms] * 3)
        other = flip(jnp.stack(chips), 1)
        grad = gather_fast(a_block, b_block, chips + [other], table_back, cos_k, sin_k, wavs, part, m, half)
        grads[half] = exchange(grad)

    back_table = row_table_back(rows, w * part)
    first = call(rows_inverse_first, [((3, rows, m), F32)], [], *grads[1], *back_table, twist)
    grad = call(rows_inverse_last, [((vis, rows, m), BF16)], [], *grads[0], *first, *back_table, twist)[0]
    grad = lax.all_to_all(grad, "vis", split_axis=0, concat_axis=0, tiled=True)
    grad_edges = call(edge_kernel, [edge, edge], [], grad)
    right = ahead(grad_edges[0], wavs - 1)
    left = ahead(grad_edges[1], 1)
    shifted = call(step_kernel, [((rows, cols), F32)], [], image, grad)[0]
    return haar_mean(shifted, sky_left - left, sky_right - right, thresholds), misfit


def shards(image, kernel_v, kernel_u, measured, dest_owner, patch_slot, thresholds):
    vis = lax.axis_size("vis")
    wavs = lax.axis_size("wav")
    v = lax.axis_index("vis")
    rows, cols = image.shape
    img = rows * vis
    m = cols // vis
    down = rows // PATCH
    across = cols // PATCH
    blocks = kernel_v.shape[0]
    low = PATCH // vis
    part = rows // wavs
    if vis == 8 and m == LANES and low == 8 and part % 8 == 0 and rows & (rows - 1) == 0:
        return shards_fast(image, kernel_v, kernel_u, measured, dest_owner, patch_slot, thresholds)
    spread = spread_matrix(vis, m)

    ids = jnp.concatenate([dest_owner, patch_slot[:, None]], 1)
    ids = lax.all_gather(ids, "vis", axis=0, tiled=True)
    owner, slot = ids[:, 0], ids[:, 1]
    a_block, b_block = slot // across, slot % across

    x = jnp.dot(image, spread, precision=HIGH).astype(F16)
    x = x.reshape(rows, vis, m).transpose(1, 0, 2)
    x = lax.all_to_all(x, "vis", split_axis=0, concat_axis=0, tiled=True).astype(F32)
    y = rows_forward(x, vis).astype(F16)
    y = y.reshape(vis, wavs, part, 2 * m).transpose(1, 0, 2, 3)
    y = lax.all_to_all(y, "wav", split_axis=0, concat_axis=0, tiled=True).astype(F32)
    cos_k, sin_k = turns(v, owner[:, None] * rows + a_block[:, None] * PATCH + iota(PATCH)[None, :], img)
    cos_k = jnp.concatenate([cos_k, cos_k], 1)
    sin_k = jnp.concatenate([sin_k, -sin_k], 1)
    y = y.transpose(1, 2, 0, 3).reshape(cols, 2 * wavs * m)
    table = column_matrix(wavs, m, down, 1.0 / img)
    z = jnp.dot(y, table, precision=HIGH)
    z = z.reshape(vis, across, low, down, 2 * PATCH)
    tiles = z[:, b_block, :, a_block, :].reshape(vis * blocks, PATCH, 2 * PATCH)
    tiles = tiles * cos_k[:, None] + jnp.roll(tiles, PATCH, axis=2) * sin_k[:, None]
    tiles = lax.all_to_all(tiles.astype(F16), "vis", split_axis=0, concat_axis=0, tiled=True)
    patch = jnp.sum(tiles.reshape(vis, blocks, PATCH, 2 * PATCH).astype(F32), 0).astype(BF16)

    side_u = kernel_u.reshape(blocks, low, vis, -1).transpose(0, 2, 1, 3).reshape(kernel_u.shape)
    part_re = jnp.einsum("nba,nat->nbt", patch[..., :PATCH], kernel_v, preferred_element_type=F32)
    part_im = jnp.einsum("nba,nat->nbt", patch[..., PATCH:], kernel_v, preferred_element_type=F32)
    side = side_u.astype(F32)
    misfit = jnp.stack([jnp.sum(part_re * side, 1), jnp.sum(part_im * side, 1)], 1) - measured.astype(F32)
    w_re = (misfit[:, 0, None, :] * side).astype(BF16)
    w_im = (misfit[:, 1, None, :] * side).astype(BF16)
    term_re = jnp.einsum("nbt,nat->nba", w_re, kernel_v, preferred_element_type=F32)
    term_im = jnp.einsum("nbt,nat->nba", w_im, kernel_v, preferred_element_type=F32)
    terms = jnp.concatenate([term_re, term_im], -1).astype(BF16)

    terms = lax.all_gather(terms, "vis", axis=0, tiled=True)
    terms = terms.astype(F32)
    terms = terms * cos_k[:, None] - jnp.roll(terms, PATCH, axis=2) * sin_k[:, None]
    terms = terms.reshape(vis * blocks, vis, low, 2 * PATCH)
    flat = jnp.zeros((across * down, vis, low, 2 * PATCH), F32).at[b_block * down + a_block].add(terms)
    grad = flat.reshape(across, down, vis, low, 2 * PATCH).transpose(2, 0, 3, 1, 4).reshape(cols, 2 * rows)
    grad = lax.dot_general(grad, table, (((1,), (1,)), ((), ())), precision=HIGH).astype(BF16)
    grad = grad.reshape(vis, part, wavs, 2 * m).transpose(2, 0, 1, 3)
    grad = lax.all_to_all(grad, "wav", split_axis=0, concat_axis=0, tiled=True)
    grad = grad.astype(F32).transpose(1, 0, 2, 3).reshape(vis, rows, 2 * m)
    grad = rows_inverse(grad, vis).astype(BF16)
    grad = lax.all_to_all(grad, "vis", split_axis=0, concat_axis=0, tiled=True)
    grad = grad.transpose(1, 0, 2).reshape(rows, cols)
    grad = lax.dot_general(grad, spread.astype(BF16), (((1,), (1,)), ((), ())), preferred_element_type=F32)
    shifted = image - grad
    right = lax.ppermute(shifted[:, :HALO].T, "wav", [(i, (i - 1) % wavs) for i in range(wavs)])
    left = lax.ppermute(shifted[:, -HALO:].T, "wav", [(i, (i + 1) % wavs) for i in range(wavs)])
    return haar_mean(shifted, left, right, thresholds), misfit


def solution(mesh):
    both = ("vis", "wav")
    in_specs = (
        P("vis", "wav"),
        P(both, None, None),
        P(both, None, None),
        P(both, None, None),
        P(both, None),
        P(both),
        P(),
    )
    out_specs = (P("vis", "wav"), P(both, None, None))
    return jax.shard_map(shards, mesh=mesh, in_specs=in_specs, out_specs=out_specs, check_vma=False)
```

```python
import math

import jax
import jax.numpy as jnp
import numpy as np
from jax import lax
from jax.experimental import pallas as pl
from jax.experimental.pallas import tpu as pltpu
from jax.sharding import PartitionSpec as P


PATCH = 64
HIGH = lax.Precision.HIGH
F32 = jnp.float32
BF16 = jnp.bfloat16
F16 = jnp.float16


def turns(rows, cols, period):
    angle = (rows * cols % period).astype(F32) * (2.0 * math.pi / period)
    return jnp.cos(angle), jnp.sin(angle)


def iota(size):
    return jnp.arange(size, dtype=jnp.int32)


def spread_matrix(groups, size):
    width = groups * size
    c = iota(width)
    return (c[:, None] == (c % size * groups + c // size)[None, :]).astype(F32)


def rows_forward(x, groups):
    rows = x.shape[1]
    count = groups * rows
    cos_g, sin_g = (np.cos(2 * np.pi * np.outer(np.arange(groups), np.arange(groups)) / groups), np.sin(2 * np.pi * np.outer(np.arange(groups), np.arange(groups)) / groups))
    mixed_re = jnp.einsum("kv,vnm->knm", jnp.asarray(cos_g, F32), x, precision=HIGH)
    mixed_im = -jnp.einsum("kv,vnm->knm", jnp.asarray(sin_g, F32), x, precision=HIGH)
    cos_t, sin_t = turns(iota(groups)[:, None], iota(rows)[None, :], count)
    cos_t, sin_t = cos_t[:, :, None], sin_t[:, :, None]
    both = jnp.concatenate([mixed_re * cos_t + mixed_im * sin_t, mixed_im * cos_t - mixed_re * sin_t], -1)
    cos_r, sin_r = turns(iota(rows)[:, None], iota(rows)[None, :], rows)
    p = jnp.einsum("kn,vnm->vkm", cos_r, both, precision=HIGH)
    q = jnp.einsum("kn,vnm->vkm", sin_r, both, precision=HIGH)
    m = x.shape[2]
    return jnp.concatenate([p[..., :m] + q[..., m:], p[..., m:] - q[..., :m]], -1)


def rows_inverse(y, groups):
    rows = y.shape[1]
    m = y.shape[2] // 2
    count = groups * rows
    cos_r, sin_r = turns(iota(rows)[:, None], iota(rows)[None, :], rows)
    p = jnp.einsum("kn,vnm->vkm", cos_r, y, precision=HIGH)
    q = jnp.einsum("kn,vnm->vkm", sin_r, y, precision=HIGH)
    re, im = p[..., :m] - q[..., m:], p[..., m:] + q[..., :m]
    cos_t, sin_t = turns(iota(groups)[:, None], iota(rows)[None, :], count)
    cos_t, sin_t = cos_t[:, :, None], sin_t[:, :, None]
    re, im = re * cos_t - im * sin_t, im * cos_t + re * sin_t
    cos_g, sin_g = (np.cos(2 * np.pi * np.outer(np.arange(groups), np.arange(groups)) / groups), np.sin(2 * np.pi * np.outer(np.arange(groups), np.arange(groups)) / groups))
    out = jnp.einsum("vk,knm->vnm", jnp.asarray(cos_g, F32), re, precision=HIGH)
    return out - jnp.einsum("vk,knm->vnm", jnp.asarray(sin_g, F32), im, precision=HIGH)


def column_matrix(wavs, m, down, scale):
    size = wavs * m
    cos_c, sin_c = turns(iota(size)[:, None], iota(size)[None, :], size)
    cos_c = (cos_c * scale).reshape(wavs, 1, m, down, 1, PATCH)
    sin_c = (sin_c * scale).reshape(wavs, 1, m, down, 1, PATCH)
    from_re = jnp.concatenate([cos_c, -sin_c], 4)
    from_im = jnp.concatenate([sin_c, cos_c], 4)
    return jnp.concatenate([from_re, from_im], 1).reshape(2 * size, 2 * size)


def split(x):
    high = lax.reduce_precision(x, 8, 7)
    return high.astype(BF16), (x - high).astype(BF16)


def bits(size):
    return size.bit_length() - 1


def cosine(count, period):
    part = (count & (period - 1)).astype(F32) * (1.0 / period)
    part = 0.25 - jnp.abs(part - jnp.where(part > 0.5, 1.0, 0.0))
    square = part * part
    terms = [(-1) ** i * (2 * math.pi) ** (2 * i + 1) / math.factorial(2 * i + 1) for i in range(7)]
    value = jnp.full_like(part, terms[-1])
    for term in terms[-2::-1]:
        value = value * square + term
    return value * part


def grid_of(shape):
    return [lax.broadcasted_iota(jnp.int32, shape, axis) for axis in (0, 1)]


def row_table(size, first):
    k, n = grid_of((2 * size, size))
    return split(cosine(((k + first) & (size - 1)) * n - (k >> bits(size)) * (size // 4), size))


def row_table_back(size, first):
    r, k = grid_of((2 * size, size))
    return split(cosine(((k + first) & (size - 1)) * (r & (size - 1)) - (r >> bits(size)) * (size // 4), size))


def column_table(wavs, m, first, turned):
    size = wavs * m
    row, col = grid_of((2 * size, 2 * size))[:: -1 if turned else 1]
    n = (row >> bits(2 * m)) * m + (row & (m - 1)) + first * m
    k = (col >> bits(2 * PATCH)) * PATCH + (col & (PATCH - 1))
    quarter = (col >> bits(PATCH) & 1) - (row >> bits(m) & 1)
    return split(cosine((n & (size - 1)) * k + quarter * (size // 4), size))


def twist_table(groups, rows):
    n, k = grid_of((rows, 2 * groups))
    count = groups * rows
    return cosine(n * (k & (groups - 1)) - (k >> bits(groups)) * (count // 4), count)


def in_vmem(count):
    return [pl.BlockSpec(memory_space=pltpu.VMEM)] * count


VMEM_LIMIT = 12 * 1024 * 1024
ROOT = math.sqrt(0.5)


AT_ONCE = 8
SHARES_AT_ONCE = 16
HALVES = ((0, 1, 7, 2, 6), (4, 3, 5))
ORDER = HALVES[0] + HALVES[1]


def call(kernel, out_shapes, scratch, *args, smem=0):
    return pl.pallas_call(
        kernel,
        in_specs=[pl.BlockSpec(memory_space=pltpu.SMEM)] * smem + in_vmem(len(args) - smem),
        out_specs=in_vmem(len(out_shapes)),
        out_shape=[jax.ShapeDtypeStruct(shape, kind) for shape, kind in out_shapes],
        scratch_shapes=[pltpu.VMEM(shape, kind) for shape, kind in scratch],
        compiler_params=pltpu.CompilerParams(vmem_limit_bytes=VMEM_LIMIT),
    )(*args)


def spread_kernel(image_ref, out_ref, first_ref, last_ref):
    first_ref[...] = image_ref[:, :LANES].T[:HALO]
    last_ref[...] = image_ref[:, image_ref.shape[1] - LANES :].T[LANES - HALO :]
    groups, _, m = out_ref.shape
    width = groups * m
    high = image_ref[...].astype(BF16)
    low = (image_ref[...] - high.astype(F32)).astype(BF16)
    c = lax.broadcasted_iota(jnp.int32, (width, 2 * m), 0)
    place = lax.broadcasted_iota(jnp.int32, (width, 2 * m), 1)
    for v in range(0, groups, 2):
        table = (c == (place & (m - 1)) * groups + (place >> bits(m)) + v).astype(F32).astype(BF16)
        out = jnp.dot(high, table, preferred_element_type=F32) + jnp.dot(low, table, preferred_element_type=F32)
        out_ref[v] = out[:, :m]
        out_ref[v + 1] = out[:, m:]


def rows_forward_kernel(x_ref, high_ref, low_ref, twist_ref, *y_refs, half):
    rows, m = x_ref.shape[1:]
    wavs = len(y_refs)
    part = rows // wavs
    x = [x_ref[i].astype(F32) for i in range(8)]
    e0, e1, f0, f1 = x[0] + x[4], x[0] - x[4], x[2] + x[6], x[2] - x[6]
    g0, g1, h0, h1 = x[1] + x[5], x[1] - x[5], x[3] + x[7], x[3] - x[7]
    gm, gp = (g1 - h1) * ROOT, (g1 + h1) * ROOT
    zero = jnp.zeros_like(e0)
    mixed = {
        0: (e0 + f0 + g0 + h0, zero),
        1: (e1 + gm, -f1 - gp),
        2: (e0 - f0, h0 - g0),
        3: (e1 - gm, f1 - gp),
        4: (e0 + f0 - g0 - h0, zero),
    }
    for spot, k in enumerate(HALVES[half]):
        if k > 4:
            continue
        re, im = mixed[k]
        if k:
            cos_t, sin_t = twist_ref[:, k : k + 1], twist_ref[:, 8 + k : 9 + k]
            re, im = re * cos_t + im * sin_t, im * cos_t - re * sin_t
        both = jnp.concatenate([re, im], 1)
        high = both.astype(BF16)
        low = (both - high.astype(F32)).astype(BF16)
        out = jnp.dot(high_ref[...], high, preferred_element_type=F32)
        out += jnp.dot(high_ref[...], low, preferred_element_type=F32)
        out += jnp.dot(low_ref[...], high, preferred_element_type=F32)
        p_re, p_im, q_re, q_im = out[:rows, :m], out[:rows, m:], out[rows:, :m], out[rows:, m:]
        here = jnp.concatenate([p_re + q_im, p_im - q_re], 1)
        for w in range(wavs):
            y_refs[w][spot] = here[w * part : (w + 1) * part]
        if k in (1, 2, 3):
            there = jnp.concatenate([p_re - q_im, -p_im - q_re], 1)
            there = pltpu.roll(there, rows - 1, 0)
            for w in range(wavs):
                y_refs[w][spot + 1] = there[w * part : (w + 1) * part]


def rows_forward_fast(x, wavs, table, twist, half):
    _, rows, m = x.shape
    kernel = lambda *refs: rows_forward_kernel(*refs, half=half)
    return call(kernel, [((len(HALVES[half]), rows // wavs, 2 * m), F32)] * wavs, [], x, *table, twist)


def shares_kernel(a_ref, b_ref, *refs, wavs):
    y_refs = refs[:wavs]
    high_ref, low_ref, cos_ref, sin_ref, far_ref, near_ref, z_ref, head_ref, rest_ref = refs[wavs:]
    groups, part, double = y_refs[0].shape
    down = z_ref.shape[0]
    wide = 2 * PATCH
    low = 8
    blocks = near_ref.shape[1]
    scale = 1.0 / (8 * down * PATCH)
    for w in range(wavs):
        y = y_refs[w][...].astype(F32).reshape(groups * part, double)
        high = y.astype(BF16)
        head_ref[:, w * double : (w + 1) * double] = high
        rest_ref[:, w * double : (w + 1) * double] = (y - high.astype(F32)).astype(BF16)
    for a in range(0, down, 2):
        spot = (slice(None), pl.ds(a * wide, 2 * wide))
        z = jnp.dot(head_ref[...], high_ref[spot], preferred_element_type=F32)
        z += jnp.dot(rest_ref[...], high_ref[spot], preferred_element_type=F32)
        z += jnp.dot(head_ref[...], low_ref[spot], preferred_element_type=F32)
        z = z * scale
        z_ref[a] = z[:, :wide].reshape(groups, part, wide)
        z_ref[a + 1] = z[:, wide:].reshape(groups, part, wide)
    for core, out_ref in ((1, far_ref), (0, near_ref)):

        @pl.loop(0, 4 * blocks // SHARES_AT_ONCE)
        def _(step):
            chip, first = step // (blocks // SHARES_AT_ONCE), step % (blocks // SHARES_AT_ONCE) * SHARES_AT_ONCE
            for i in range(SHARES_AT_ONCE):
                at = first + i
                n = (2 * chip + core) * blocks + at
                start = pl.multiple_of(b_ref[n] * low, low)
                tile = z_ref[a_ref[n], :, pl.ds(start, low), :].reshape(groups * low, wide)
                out_ref[chip, at] = tile * cos_ref[pl.ds(n, 1), :] + pltpu.roll(tile, PATCH, 1) * sin_ref[pl.ds(n, 1), :]


def shares_fast(a_block, b_block, ys, table, cos_k, sin_k):
    groups, part, double = ys[0].shape
    wavs = len(ys)
    width = wavs * double
    blocks = a_block.shape[0] // 8
    out = ((4, blocks, groups * 8, 2 * PATCH), F32)
    scratch = [((width // (2 * PATCH), groups, part, 2 * PATCH), F32)] + [((groups * part, width), BF16)] * 2
    kernel = lambda *refs: shares_kernel(*refs, wavs=wavs)
    return call(kernel, [out, out], scratch, a_block, b_block, *ys, *table, cos_k, sin_k, smem=2)


def gather_kernel(a_ref, b_ref, *refs):
    high_ref, low_ref, cos_ref, sin_ref = refs[5:9]
    y_refs, (g_ref, head_ref) = refs[9:-2], refs[-2:]
    groups, part, double = y_refs[0].shape
    down = g_ref.shape[0]
    wide = 2 * PATCH
    low = 8
    blocks = refs[0].shape[0]
    g_ref[...] = jnp.zeros_like(g_ref)

    def add(term_ref, mask, first):
        tiles = []
        for i in range(AT_ONCE):
            n = mask * blocks + first + i
            tile = term_ref[first + i].astype(F32)
            tiles.append(tile * cos_ref[pl.ds(n, 1), :] - pltpu.roll(tile, PATCH, 1) * sin_ref[pl.ds(n, 1), :])
        for i in range(AT_ONCE):
            n = mask * blocks + first + i
            start = pl.multiple_of(b_ref[n] * low, low)
            g_ref[a_ref[n], :, pl.ds(start, low), :] += tiles[i].reshape(groups, low, wide)

    steps = blocks // AT_ONCE
    for chip in range(4):
        pl.loop(0, steps)(lambda step: add(refs[chip], 2 * chip, step * AT_ONCE))
    pl.loop(0, 4 * steps)(lambda step: add(refs[4].at[step // steps], 2 * (step // steps) + 1, step % steps * AT_ONCE))

    for a in range(down):
        head_ref[:, a * wide : (a + 1) * wide] = g_ref[a].reshape(groups * part, wide).astype(BF16)
    scale = 1.0 / (8 * down * PATCH)
    for w, y_ref in enumerate(y_refs):
        spot = (slice(None), pl.ds(w * double, double))
        y = jnp.dot(head_ref[...], high_ref[spot], preferred_element_type=F32)
        y += jnp.dot(head_ref[...], low_ref[spot], preferred_element_type=F32)
        y_ref[...] = (y * scale).astype(BF16).reshape(groups, part, double)


def gather_fast(a_block, b_block, terms, table, cos_k, sin_k, wavs, part, m, half):
    width = 2 * wavs * m
    groups = len(HALVES[half])
    out = [((groups, part, 2 * m), BF16)] * wavs
    scratch = [((width // (2 * PATCH), groups, part, 2 * PATCH), F32), ((groups * part, width), BF16)]
    return call(gather_kernel, out, scratch, a_block, b_block, *terms, *table, cos_k, sin_k, smem=2)


def untwist(y_refs, spot, k, high_ref, low_ref, twist_ref):
    y = jnp.concatenate([ref[spot] for ref in y_refs], 0)
    rows, m = y.shape[0], y.shape[1] // 2
    out = jnp.dot(high_ref[...], y, preferred_element_type=F32)
    out += jnp.dot(low_ref[...], y, preferred_element_type=F32)
    re, im = out[:rows, :m] - out[rows:, m:], out[:rows, m:] + out[rows:, :m]
    if k:
        cos_t, sin_t = twist_ref[:, k : k + 1], twist_ref[:, 8 + k : 9 + k]
        re, im = re * cos_t - im * sin_t, im * cos_t + re * sin_t
    return re, im


def rows_inverse_first(*refs):
    y_refs, (high_ref, low_ref, twist_ref, out_ref) = refs[:-4], refs[-4:]
    (re4, _), (re3, im3), (re5, im5) = [
        untwist(y_refs, spot, k, high_ref, low_ref, twist_ref) for spot, k in enumerate(HALVES[1])
    ]
    out_ref[0] = re4
    out_ref[1] = re3 + re5
    out_ref[2] = im3 - im5


def rows_inverse_last(*refs):
    y_refs, (first_ref, high_ref, low_ref, twist_ref, x_ref) = refs[:-5], refs[-5:]
    (re0, _), (re1, im1), (re7, im7), (re2, im2), (re6, im6) = [
        untwist(y_refs, spot, k, high_ref, low_ref, twist_ref) for spot, k in enumerate(HALVES[0])
    ]
    re4, r3, i3 = [first_ref[i] for i in range(3)]
    even, odd = re0 + re4, re0 - re4
    r1, r2, i1, i2 = re1 + re7, re2 + re6, im1 - im7, im2 - im6
    rm, ip = (r1 - r3) * ROOT, (i1 + i3) * ROOT
    x_ref[0] = (even + r2 + (r1 + r3)).astype(BF16)
    x_ref[4] = (even + r2 - (r1 + r3)).astype(BF16)
    x_ref[2] = (even - r2 - (i1 - i3)).astype(BF16)
    x_ref[6] = (even - r2 + (i1 - i3)).astype(BF16)
    x_ref[1] = (odd + rm - ip - i2).astype(BF16)
    x_ref[7] = (odd + rm + ip + i2).astype(BF16)
    x_ref[3] = (odd - rm - ip + i2).astype(BF16)
    x_ref[5] = (odd - rm + ip - i2).astype(BF16)


HALO = 8
LANES = 128


def step_kernel(image_ref, grad_ref, out_ref):
    groups, _, m = grad_ref.shape
    width = groups * m
    grad = jnp.concatenate([grad_ref[i] for i in range(groups)], 1)
    wide = 2 * LANES
    place = lax.broadcasted_iota(jnp.int32, (width, wide), 0)
    column = (place & (m - 1)) * groups + (place >> bits(m))
    lane = lax.broadcasted_iota(jnp.int32, (width, wide), 1)
    for start in range(0, width, wide):
        spot = (slice(None), slice(start, start + wide))
        table = (column == lane + start).astype(F32).astype(BF16)
        out_ref[spot] = image_ref[spot] - jnp.dot(grad, table, preferred_element_type=F32)


def edge_kernel(grad_ref, first_ref, last_ref):
    groups, _, m = grad_ref.shape
    row = lax.broadcasted_iota(jnp.int32, (8, m), 0)
    lane = lax.broadcasted_iota(jnp.int32, (8, m), 1)
    pick = (lane == jnp.where(row == 0, 0, m - 1)).astype(F32).astype(BF16)
    for v in range(groups):
        both = lax.dot_general(pick, grad_ref[v], (((1,), (1,)), ((), ())), preferred_element_type=F32)
        first_ref[v : v + 1, :] = both[0:1]
        last_ref[v : v + 1, :] = both[1:2]


def haar_kernel(field_ref, left_ref, right_ref, limit_ref, out_ref, edge_ref, *, bases):
    every, width = field_ref.shape
    rows = 64
    span = width + LANES
    middle = jnp.zeros((LANES - 2 * HALO, every), F32)
    edge_ref[...] = jnp.concatenate([right_ref[...], middle, left_ref[...]], 0).T
    even = lax.broadcasted_iota(jnp.int32, (rows, span), 0) % 2 == 0

    def mix(x, even):
        other = jnp.where(even, pltpu.roll(x, rows - 1, 0), pltpu.roll(x, 1, 0))
        return jnp.where(even, x, -x) + other

    def ahead(x, by):
        return pltpu.roll(x, span - by, 1)

    def behind(x, by):
        return pltpu.roll(x, by, 1)

    def mean(u):
        spot = 0
        level = []
        for period in (2, 4, 8):
            forward = ahead(u, period // 2)
            parts = [u + forward, u - forward]
            limits = []
            for _ in range(0, bases, period):
                limits.append(limit_ref[spot : spot + 1, :])
                spot += 1
            limited = []
            for x in parts if period == 8 else parts[1:]:
                total = None
                for limit in limits:
                    x_soft = x - jnp.minimum(jnp.maximum(x, -limit), limit)
                    total = x_soft if total is None else total + x_soft
                limited.append(total)
            level.append(limited)
            u = parts[0]
        s3, d3 = level[2]
        back = (s3 + d3) + behind(s3 - d3, 4)
        for by, (d,) in ((2, level[1]), (1, level[0])):
            back = back * 0.5
            back = (back + d) + behind(back - d, by)
        return back[:, :width] * (0.25 / bases)

    @pl.loop(0, every // rows)
    def _(step):
        spot = (pl.ds(pl.multiple_of(step * rows, rows), rows), slice(None))
        field = jnp.concatenate([field_ref[spot], edge_ref[spot]], 1)
        out_ref[spot] = mix(mean(mix(field, even)), even[:, :width])


def haar_limits(width, thresholds):
    bases = thresholds.shape[0]
    span = width + LANES
    place = iota(span)
    place = jnp.where(place < width + LANES // 2, place, place - span) + 8
    out = []
    for period in (2, 4, 8):
        scale = math.sqrt(2.0 * period)
        for start in range(0, bases, period):
            index = place % period + start
            limit = jnp.full((span,), 3e38, F32)
            for s in range(start, min(start + period, bases)):
                limit = jnp.where(index == s, thresholds[s] * scale, limit)
            out.append(limit)
    return jnp.stack(out)


def haar_mean(field, halo_left, halo_right, thresholds):
    bases = thresholds.shape[0]
    rows, width = field.shape
    limits = haar_limits(width, thresholds)
    step = LANES
    return pl.pallas_call(
        lambda *refs: haar_kernel(*refs, bases=bases),
        grid=(rows // step,),
        in_specs=[
            pl.BlockSpec((step, width), lambda i: (i, 0)),
            pl.BlockSpec((HALO, step), lambda i: (0, i)),
            pl.BlockSpec((HALO, step), lambda i: (0, i)),
            pl.BlockSpec(limits.shape, lambda i: (0, 0)),
        ],
        out_specs=pl.BlockSpec((step, width), lambda i: (i, 0)),
        out_shape=jax.ShapeDtypeStruct((rows, width), F32),
        scratch_shapes=[pltpu.VMEM((step, LANES), F32)],
        compiler_params=pltpu.CompilerParams(vmem_limit_bytes=VMEM_LIMIT),
        name="haar",
    )(field, halo_left, halo_right, limits)


def phases(owner, a_block, v, rows, img):
    cos_k, sin_k = turns(v, owner[:, None] * rows + a_block[:, None] * PATCH + iota(PATCH)[None, :], img)
    return jnp.concatenate([cos_k, cos_k], 1), jnp.concatenate([sin_k, -sin_k], 1)


def shards_fast(image, kernel_v, kernel_u, measured, dest_owner, patch_slot, thresholds):
    vis = lax.axis_size("vis")
    wavs = lax.axis_size("wav")
    v, w = lax.axis_index("vis"), lax.axis_index("wav")
    rows, cols = image.shape
    img = rows * vis
    m = cols // vis
    across = cols // PATCH
    part = rows // wavs

    def flip(x, mask):
        return lax.ppermute(x, "vis", [(i, i ^ mask) for i in range(vis)])

    def ahead(x, by):
        return lax.ppermute(x, "wav", [(i, (i + by) % wavs) for i in range(wavs)])

    def exchange(parts):
        out = [parts[0]]
        for s in range(1, wavs):
            out.append(ahead(parts[wavs - s], wavs - s))
        return out

    def to_chips(parts):
        out = []
        for chip in (1, 2, 3):
            out.append(flip(parts[chip - 1], 2 * chip))
        return out

    edge = ((HALO, rows), F32)
    x, first_cols, last_cols = call(spread_kernel, [((vis, rows, m), F32), edge, edge], [], image)
    x = x.astype(F16)
    x = lax.all_to_all(x, "vis", split_axis=0, concat_axis=0, tiled=True)
    x = x.astype(F32)
    table, table_back = column_table(wavs, m, w, False), column_table(wavs, m, w, True)

    forward_table, twist = row_table(rows, w * part), twist_table(vis, rows)
    sent, spectra = [], []
    for half in (0, 1):
        y = rows_forward_fast(x, wavs, forward_table, twist, half)
        sent.append([part_y.astype(F16) for part_y in y])
        spectra.append(exchange(sent[half]))

    ids = jnp.stack([dest_owner[:, 0], patch_slot])
    ids, _ = lax.optimization_barrier((ids, sent[1]))
    for mask in (1, 2, 4):
        ids = jnp.concatenate([ids, flip(ids, mask)], 1)
    sky, _ = lax.optimization_barrier(((first_cols, last_cols), sent[1]))
    sky_right, sky_left = ahead(sky[0], wavs - 1), ahead(sky[1], 1)
    owner, slot = ids[0], ids[1]
    a_block, b_block = slot // across, slot % across
    cos_k, sin_k = phases(owner, a_block, v, rows, img)

    patches = []
    for half in (0, 1):
        y = []
        for part_y in spectra[half]:
            y.append(part_y.astype(F32))
        far, near = shares_fast(a_block, b_block, y, table, cos_k, sin_k)
        near = near + flip(far.astype(F16), 1).astype(F32)
        ready = [near[0]] + [near[chip].astype(F16) for chip in (1, 2, 3)]
        came = to_chips(ready[1:])
        patches.append(sum([part_sum.astype(F32) for part_sum in came], ready[0]).astype(BF16))

    place = np.arange(PATCH)
    chosen = (place % 8) * vis + np.asarray(ORDER)[place // 8]
    pick = jnp.asarray(chosen[:, None] == place[None, :], BF16)
    side = jnp.einsum("pb,nbt->npt", pick, kernel_u, preferred_element_type=F32)
    cut = 8 * len(HALVES[0])
    sides = [side[:, :cut], side[:, cut:]]
    model = 0.0
    for patch, side in zip(patches, sides):
        part_re = jnp.einsum("nba,nat->nbt", patch[..., :PATCH], kernel_v, preferred_element_type=F32)
        part_im = jnp.einsum("nba,nat->nbt", patch[..., PATCH:], kernel_v, preferred_element_type=F32)
        model = model + jnp.stack([jnp.sum(part_re * side, 1), jnp.sum(part_im * side, 1)], 1)
    misfit = model - measured.astype(F32)

    grads = {}
    for half in (1, 0):
        side = sides[half]
        w_re = (misfit[:, 0, None, :] * side).astype(BF16)
        w_im = (misfit[:, 1, None, :] * side).astype(BF16)
        term_re = jnp.einsum("nbt,nat->nba", w_re, kernel_v, preferred_element_type=F32)
        term_im = jnp.einsum("nbt,nat->nba", w_im, kernel_v, preferred_element_type=F32)
        terms = jnp.concatenate([term_re, term_im], -1).astype(BF16)
        if half == 0:
            terms, chips = lax.optimization_barrier((terms, chips))
        chips = [terms] + to_chips([terms] * 3)
        other = flip(jnp.stack(chips), 1)
        grad = gather_fast(a_block, b_block, chips + [other], table_back, cos_k, sin_k, wavs, part, m, half)
        grads[half] = exchange(grad)

    back_table = row_table_back(rows, w * part)
    first = call(rows_inverse_first, [((3, rows, m), F32)], [], *grads[1], *back_table, twist)
    grad = call(rows_inverse_last, [((vis, rows, m), BF16)], [], *grads[0], *first, *back_table, twist)[0]
    grad = lax.all_to_all(grad, "vis", split_axis=0, concat_axis=0, tiled=True)
    grad_edges = call(edge_kernel, [edge, edge], [], grad)
    right = ahead(grad_edges[0], wavs - 1)
    left = ahead(grad_edges[1], 1)
    shifted = call(step_kernel, [((rows, cols), F32)], [], image, grad)[0]
    return haar_mean(shifted, sky_left - left, sky_right - right, thresholds), misfit


def shards(image, kernel_v, kernel_u, measured, dest_owner, patch_slot, thresholds):
    vis = lax.axis_size("vis")
    wavs = lax.axis_size("wav")
    v = lax.axis_index("vis")
    rows, cols = image.shape
    img = rows * vis
    m = cols // vis
    down = rows // PATCH
    across = cols // PATCH
    blocks = kernel_v.shape[0]
    low = PATCH // vis
    part = rows // wavs
    if vis == 8 and m == LANES and low == 8 and part % 8 == 0 and rows & (rows - 1) == 0:
        return shards_fast(image, kernel_v, kernel_u, measured, dest_owner, patch_slot, thresholds)
    spread = spread_matrix(vis, m)

    ids = jnp.concatenate([dest_owner, patch_slot[:, None]], 1)
    ids = lax.all_gather(ids, "vis", axis=0, tiled=True)
    owner, slot = ids[:, 0], ids[:, 1]
    a_block, b_block = slot // across, slot % across

    x = jnp.dot(image, spread, precision=HIGH).astype(F16)
    x = x.reshape(rows, vis, m).transpose(1, 0, 2)
    x = lax.all_to_all(x, "vis", split_axis=0, concat_axis=0, tiled=True).astype(F32)
    y = rows_forward(x, vis).astype(F16)
    y = y.reshape(vis, wavs, part, 2 * m).transpose(1, 0, 2, 3)
    y = lax.all_to_all(y, "wav", split_axis=0, concat_axis=0, tiled=True).astype(F32)
    cos_k, sin_k = turns(v, owner[:, None] * rows + a_block[:, None] * PATCH + iota(PATCH)[None, :], img)
    cos_k = jnp.concatenate([cos_k, cos_k], 1)
    sin_k = jnp.concatenate([sin_k, -sin_k], 1)
    y = y.transpose(1, 2, 0, 3).reshape(cols, 2 * wavs * m)
    table = column_matrix(wavs, m, down, 1.0 / img)
    z = jnp.dot(y, table, precision=HIGH)
    z = z.reshape(vis, across, low, down, 2 * PATCH)
    tiles = z[:, b_block, :, a_block, :].reshape(vis * blocks, PATCH, 2 * PATCH)
    tiles = tiles * cos_k[:, None] + jnp.roll(tiles, PATCH, axis=2) * sin_k[:, None]
    tiles = lax.all_to_all(tiles.astype(F16), "vis", split_axis=0, concat_axis=0, tiled=True)
    patch = jnp.sum(tiles.reshape(vis, blocks, PATCH, 2 * PATCH).astype(F32), 0).astype(BF16)

    side_u = kernel_u.reshape(blocks, low, vis, -1).transpose(0, 2, 1, 3).reshape(kernel_u.shape)
    part_re = jnp.einsum("nba,nat->nbt", patch[..., :PATCH], kernel_v, preferred_element_type=F32)
    part_im = jnp.einsum("nba,nat->nbt", patch[..., PATCH:], kernel_v, preferred_element_type=F32)
    side = side_u.astype(F32)
    misfit = jnp.stack([jnp.sum(part_re * side, 1), jnp.sum(part_im * side, 1)], 1) - measured.astype(F32)
    w_re = (misfit[:, 0, None, :] * side).astype(BF16)
    w_im = (misfit[:, 1, None, :] * side).astype(BF16)
    term_re = jnp.einsum("nbt,nat->nba", w_re, kernel_v, preferred_element_type=F32)
    term_im = jnp.einsum("nbt,nat->nba", w_im, kernel_v, preferred_element_type=F32)
    terms = jnp.concatenate([term_re, term_im], -1).astype(BF16)

    terms = lax.all_gather(terms, "vis", axis=0, tiled=True)
    terms = terms.astype(F32)
    terms = terms * cos_k[:, None] - jnp.roll(terms, PATCH, axis=2) * sin_k[:, None]
    terms = terms.reshape(vis * blocks, vis, low, 2 * PATCH)
    flat = jnp.zeros((across * down, vis, low, 2 * PATCH), F32).at[b_block * down + a_block].add(terms)
    grad = flat.reshape(across, down, vis, low, 2 * PATCH).transpose(2, 0, 3, 1, 4).reshape(cols, 2 * rows)
    grad = lax.dot_general(grad, table, (((1,), (1,)), ((), ())), precision=HIGH).astype(BF16)
    grad = grad.reshape(vis, part, wavs, 2 * m).transpose(2, 0, 1, 3)
    grad = lax.all_to_all(grad, "wav", split_axis=0, concat_axis=0, tiled=True)
    grad = grad.astype(F32).transpose(1, 0, 2, 3).reshape(vis, rows, 2 * m)
    grad = rows_inverse(grad, vis).astype(BF16)
    grad = lax.all_to_all(grad, "vis", split_axis=0, concat_axis=0, tiled=True)
    grad = grad.transpose(1, 0, 2).reshape(rows, cols)
    grad = lax.dot_general(grad, spread.astype(BF16), (((1,), (1,)), ((), ())), preferred_element_type=F32)
    shifted = image - grad
    right = lax.ppermute(shifted[:, :HALO].T, "wav", [(i, (i - 1) % wavs) for i in range(wavs)])
    left = lax.ppermute(shifted[:, -HALO:].T, "wav", [(i, (i + 1) % wavs) for i in range(wavs)])
    return haar_mean(shifted, left, right, thresholds), misfit


def solution(mesh):
    both = ("vis", "wav")
    in_specs = (
        P("vis", "wav"),
        P(both, None, None),
        P(both, None, None),
        P(both, None, None),
        P(both, None),
        P(both),
        P(),
    )
    out_specs = (P("vis", "wav"), P(both, None, None))
    return jax.shard_map(shards, mesh=mesh, in_specs=in_specs, out_specs=out_specs, check_vma=False)
```
